32 devices in a mesh: lon: 4 (over y, x), lat: 4 (over z), comp: 2 (over core).
Axes of the slice: x: 2, y: 2, z: 4, core: 2. Of those that a mesh axis runs over, the one named last changes fastest.
Arguments:
- ocean_state: float32 [4, 80, 32, 1024], P(None, None, 'lon', ('lat', 'comp')), may hold values from -6 to 6
- level_count: int32 [32, 1024], P('lon', ('lat', 'comp')), may hold values from 0 to 80, as said below
- mix_rate: float32 [80, 32, 1024], P(None, 'lon', ('lat', 'comp')), may hold values from 0.05 to 5
- atmos_flux: bfloat16 [8, 16, 4, 256], P(('lat', 'comp'), 'lon'), may hold values from -6 to 6
- remap_weight: bfloat16 [8, 16, 256, 128], P(('lat', 'comp'), 'lon'), may hold values from -0.375 to 0.375
- remap_target: int32 [8, 16], P(('lat', 'comp'), 'lon'), may hold values from 0 to 3, as said below
- remap_slot: int32 [8, 16], P(('lat', 'comp'), 'lon'), may hold values from 0 to 7
Outputs:
- ocean_next: float32 [4, 80, 32, 1024], P(None, None, 'lon', ('lat', 'comp'))
The draws below stay inside these ranges and needn't reach their ends.
Inputs may be any that keep to these rules, and one draw needn't show every extreme that they name: `level_count`: 0 marks a land column. `remap_target`: among the blocks of one device each longitude tile index appears exactly 1 times.
All inputs are finite; a program needn't handle non-finite values.
Results may differ from the reference program's by a relative error of at most 0.0003.
Values sent between devices are 32-bit elements; how exact they have to be, the bound alone decides.
No kernel may reach another device: no remote copies, remote signals or barrier semaphores. Data moves between devices by JAX's collectives and lax.ppermute only.
A program may use at most 128 MiB of HBM per device.

```python
import math
import jax
import jax.numpy as jnp
from jax import lax

LON_DEV = 8
LAT_DEV = 128
LEVELS = 80
FLUXES = 4
BLOCK_CELLS = 256
SEND_BLOCKS = 1
SUBSTEPS = 2
BLOCKS_DEV = 4
LAT_TILES = 8
LON_CELLS = 32
LAT_CELLS = 1024
N_LON = 4


def draw_level_count(key, part):
    raw_levels = jax.random.randint(key, (LON_CELLS, LAT_CELLS), -(LEVELS // 3), LEVELS + 1)
    return jnp.maximum(raw_levels, 0).astype(jnp.int32)


def shuffled_blocks(device_key):
    return jax.random.permutation(device_key, BLOCKS_DEV)


def draw_remap_target(key, part):
    device_keys = jax.random.split(key, LAT_TILES * N_LON)
    orders = jax.vmap(shuffled_blocks)(device_keys)
    return (orders // SEND_BLOCKS).reshape(LAT_TILES, N_LON * BLOCKS_DEV).astype(jnp.int32)


def with_ends(values, key, smallest, high):
    shape = values.shape
    place = [jax.random.randint(jax.random.fold_in(key, axis), (), 0, shape[axis]) for axis in range(len(shape))]
    values = values.at[tuple(place)].set(smallest)
    longest = shape.index(max(shape))
    place[longest] = (place[longest] + 1) % shape[longest]
    return values.at[tuple(place)].set(high)


def shard_levels(key, shape, cuts, least, largest):
    def one(axis_at, blocks):
        steps = jax.random.uniform(jax.random.fold_in(jax.random.fold_in(key, 6), axis_at), (blocks,), jnp.float32, least / len(cuts), largest / len(cuts))
        return jnp.repeat(jnp.exp(steps), shape[axis_at] // blocks).reshape((-1,) + (1,) * (len(shape) - axis_at - 1))

    level = one(*cuts[0])
    for cut in cuts[1:]:
        level = level * one(*cut)
    return level


def centred(key, extent, scale, most, cuts=(), held_as=jnp.bfloat16):
    gain = shard_levels(key, extent, cuts, -0.22, 0.18) if cuts else 1.0
    values = jax.random.normal(key, extent, jnp.float32) * scale * gain
    return jnp.minimum(jnp.maximum(values, -most), most).astype(held_as)


def setup_inputs(seed: int = 0) -> dict:
    keys = jax.random.split(jax.random.key(seed), 8)
    ocean_state = centred(keys[0], (4, LEVELS, LON_CELLS, LAT_CELLS), 1.0, 6.0, ((2, 4), (3, 8)), jnp.float32)
    level_count = draw_level_count(jax.random.fold_in(keys[7], 71), 0)
    mix_rate = jnp.clip(jnp.exp(math.log(5.0) - 4.6051702 * jax.random.uniform(keys[2], (LEVELS, LON_CELLS, LAT_CELLS), jnp.float32) ** shard_levels(keys[2], (LEVELS, LON_CELLS, LAT_CELLS), ((1, 4), (2, 8)), -0.2, 0.2)), 0.05, 5.0)
    atmos_flux = centred(keys[3], (LAT_TILES, N_LON * BLOCKS_DEV, FLUXES, BLOCK_CELLS), 1.0, 6.0, ((0, 8), (1, 4)))
    remap_weight = centred(keys[4], (LAT_TILES, N_LON * BLOCKS_DEV, BLOCK_CELLS, LAT_DEV), BLOCK_CELLS ** -0.5, 0.375, ((0, 8), (1, 4)))
    remap_target = draw_remap_target(jax.random.fold_in(keys[7], 71), 0)
    remap_slot = with_ends(jax.random.randint(keys[6], (LAT_TILES, N_LON * BLOCKS_DEV), 0, LON_DEV), jax.random.fold_in(keys[6], 1), 0, LON_DEV - 1).astype(jnp.int32)
    return dict(ocean_state=ocean_state, level_count=level_count, mix_rate=mix_rate, atmos_flux=atmos_flux, remap_weight=remap_weight, remap_target=remap_target, remap_slot=remap_slot)


DIFFUSE = 0.2
VISCOUS = 0.2
ADVECTION = 0.5
THERMAL = 0.2
HALINE = 0.15
GRAVITY = 0.05
CORIOLIS = 0.3
SURFACE_GAIN = (0.5, 0.4, 0.6, 0.6)


def centre_of(values):
    return values[..., 1:-1, 1:-1]


def east_of(values):
    return values[..., 2:, 1:-1]


def west_of(values):
    return values[..., :-2, 1:-1]


def north_of(values):
    return values[..., 1:-1, 2:]


def south_of(values):
    return values[..., 1:-1, :-2]


def laplace(values, wet_padded):
    middle = centre_of(values)
    total = east_of(wet_padded) * (east_of(values) - middle)
    total = total + west_of(wet_padded) * (west_of(values) - middle)
    total = total + north_of(wet_padded) * (north_of(values) - middle)
    total = total + south_of(wet_padded) * (south_of(values) - middle)
    return total


def vertical_mix(tendency, rate, wet_mask):
    level_total = tendency.shape[1]
    coupling = rate[:-1] * wet_mask[:-1] * wet_mask[1:]
    zero_level = jnp.zeros_like(rate[:1])
    upper = jnp.concatenate([coupling, zero_level], axis=0)
    lower = jnp.concatenate([zero_level, coupling], axis=0)
    diagonal = 1.0 + upper + lower
    ratio_list = []
    value_list = []
    prev_ratio = jnp.zeros_like(rate[0])
    prev_value = jnp.zeros_like(tendency[:, 0])
    for level_at in range(level_total):
        pivot = diagonal[level_at] + lower[level_at] * prev_ratio
        prev_ratio = -upper[level_at] / pivot
        prev_value = (tendency[:, level_at] + lower[level_at] * prev_value) / pivot
        ratio_list.append(prev_ratio)
        value_list.append(prev_value)
    following = prev_value
    solved = [following]
    for level_at in range(level_total - 2, -1, -1):
        following = value_list[level_at] - ratio_list[level_at] * following
        solved.append(following)
    return jnp.stack(solved[::-1], axis=1)


def baroclinic(state_padded, rate_padded, count_padded, forcing, first_row, lat_total):
    level_total = state_padded.shape[1]
    level_ids = jnp.arange(level_total, dtype=jnp.int32).astype(jnp.float32)[:, None, None]
    wet_padded = (level_ids < count_padded[None]).astype(jnp.float32)
    masked = state_padded * wet_padded[None]
    wet_mask = centre_of(wet_padded)
    tracers = masked[:2]
    u_padded = masked[2]
    v_padded = masked[3]
    u_middle = centre_of(u_padded)
    v_middle = centre_of(v_padded)
    carried = u_middle * (east_of(tracers) - west_of(tracers)) + v_middle * (north_of(tracers) - south_of(tracers))
    tracer_next = centre_of(tracers) + DIFFUSE * laplace(tracers, wet_padded) - 0.5 * ADVECTION * carried
    density = HALINE * masked[1] - THERMAL * masked[0]
    pressure = GRAVITY * jnp.cumsum(density, axis=0) * wet_padded
    force_x = 0.5 * (east_of(pressure) - west_of(pressure))
    force_y = 0.5 * (north_of(pressure) - south_of(pressure))
    row_count = wet_mask.shape[-1]
    row_ids = (first_row + jnp.arange(row_count, dtype=jnp.int32)).astype(jnp.float32)
    rotation = CORIOLIS * (2.0 * (row_ids + 0.5) / lat_total - 1.0)
    u_next = u_middle + VISCOUS * laplace(u_padded, wet_padded) + rotation * v_middle - force_x
    v_next = v_middle + VISCOUS * laplace(v_padded, wet_padded) - rotation * u_middle - force_y
    updated = jnp.stack([tracer_next[0], tracer_next[1], u_next, v_next])
    gains = jnp.array(SURFACE_GAIN, dtype=jnp.float32)[:, None, None]
    surface = updated[:, 0] + gains * forcing
    updated = jnp.concatenate([surface[:, None], updated[:, 1:]], axis=1) * wet_mask[None]
    return vertical_mix(updated, centre_of(rate_padded), wet_mask) * wet_mask[None]


def pad_grid(values):
    wrapped = jnp.concatenate([values[..., -1:, :], values, values[..., :1, :]], axis=-2)
    widths = [(0, 0)] * (values.ndim - 1) + [(1, 1)]
    return jnp.pad(wrapped, widths)


def remap_tile(pieces):
    flux_block, weight_block, target_tile, slot_index = pieces
    partial_value = jnp.einsum('bfc,bco->bfo', flux_block.astype(jnp.float32), weight_block.astype(jnp.float32), precision=lax.Precision.HIGHEST)
    column = target_tile * LON_DEV + slot_index
    return jax.ops.segment_sum(partial_value, column, num_segments=LON_CELLS)


def reference(ocean_state, level_count, mix_rate, atmos_flux, remap_weight, remap_target, remap_slot):
    tiles = lax.map(remap_tile, (atmos_flux, remap_weight, remap_target, remap_slot))
    forcing = jnp.transpose(tiles, (2, 1, 0, 3)).reshape(FLUXES, LON_CELLS, LAT_CELLS)
    rate_padded = pad_grid(mix_rate)
    count_padded = pad_grid(level_count.astype(jnp.float32))
    state = ocean_state
    for step_index in range(SUBSTEPS):
        state = baroclinic(pad_grid(state), rate_padded, count_padded, forcing, 0, LAT_CELLS)
    return state
```

```python
import jax
import jax.numpy as jnp
from jax import lax
from jax.experimental import pallas as pl
from jax.experimental.pallas import tpu as pltpu
from jax.sharding import PartitionSpec as P

SUBSTEPS = 2

DIFFUSE = 0.2
VISCOUS = 0.2
ADVECTION = 0.5
THERMAL = 0.2
HALINE = 0.15
GRAVITY = 0.05
CORIOLIS = 0.3
SURFACE_GAIN = (0.5, 0.4, 0.6, 0.6)

FIELDS = 4
SUB = 8
LANE = 128
PAIRS = LANE // 2
GROUP = PAIRS // FIELDS
EXTRA = 8
SLOT_ROW = 4
COUNT_ROW = 5
LAT_AXES = ("lat", "comp")

VMEM_SPEC = pl.BlockSpec(memory_space=pltpu.VMEM)
SMEM_SPEC = pl.BlockSpec(memory_space=pltpu.SMEM)


def sublane_ids():
    return lax.broadcasted_iota(jnp.int32, (SUB, LANE), 0)


def lane_ids():
    return lax.broadcasted_iota(jnp.int32, (SUB, LANE), 1)


def spread(row):
    return jnp.broadcast_to(row, (SUB, LANE))


def tile_at(ref, index):
    return ref[pl.ds(pl.multiple_of(index * SUB, SUB), SUB), :]


def put_tile(ref, index, value):
    ref[pl.ds(pl.multiple_of(index * SUB, SUB), SUB), :] = value


def row_at(ref, index):
    return spread(ref[pl.ds(index, 1), :])


def pack_kernel(levels, lon_total, x_ref, count_ref, flux_ref, weight_ref, target_ref, slot_ref,
                east_ref, west_ref, edge_ref, parts_ref):
    me = lax.axis_index("lon")
    sub = sublane_ids()
    pair = lane_ids() // 2
    count = count_ref[...]
    rows = FIELDS * levels

    for out_ref, column in ((east_ref, SUB - 1), (west_ref, 0)):
        depth = spread(count[column:column + 1, :])
        for field in range(FIELDS):
            for start in range(0, levels, SUB):
                row = field * levels + start
                value = x_ref[pl.ds(row * SUB + column, SUB, stride=SUB), :]
                out_ref[pl.ds(row, SUB), :] = jnp.where(start + sub < depth, value, 0.0)

    blocks = flux_ref.shape[0]
    for block in range(blocks):
        partial = jnp.dot(flux_ref[block], weight_ref[block], preferred_element_type=jnp.float32)
        slot = slot_ref[0, block].astype(jnp.float32)
        tile = jnp.concatenate([partial, jnp.full((SUB - FIELDS, LANE), slot, jnp.float32)], axis=0)
        shift = lax.rem(target_ref[0, block] - me + lon_total, lon_total)
        parts_ref[shift] = tile

    count_f = count.astype(jnp.float32)
    for out_ref, column, shift in ((east_ref, SUB - 1, 1), (west_ref, 0, lon_total - 1)):
        tile = parts_ref[shift]
        out_ref[pl.ds(rows, EXTRA), :] = jnp.where(
            sub == COUNT_ROW, spread(count_f[column:column + 1, :]), tile
        )

    def group_body(group, carry):
        packed = jnp.zeros((SUB, LANE), jnp.float32)
        for inner in range(GROUP):
            level = group * GROUP + inner
            wet = level < count
            for field in range(FIELDS):
                j = inner * FIELDS + field
                value = jnp.where(wet, tile_at(x_ref, field * levels + level), 0.0)
                packed = jnp.where(pair == j, pltpu.roll(value, 2 * j + 1, 1), packed)
        put_tile(edge_ref, group, packed)
        return carry

    lax.fori_loop(0, levels // GROUP, group_body, 0)
    put_tile(edge_ref, levels // GROUP, pltpu.roll(count_f, 1, 1))


def factor_kernel(levels, rate_ref, count_ref, gain_ref, down_ref, up_ref):
    count = count_ref[...]

    def level_body(level, carry):
        lower, prev = carry
        upper = jnp.where(level + 1 < count, rate_ref[level], 0.0)
        upper = jnp.where(level < levels - 1, upper, 0.0)
        pivot = 1.0 + upper + lower - lower * prev
        inverse = 1.0 / pivot
        ratio = upper * inverse
        gain_ref[level] = jnp.where(level < count, inverse, 0.0)
        down_ref[level] = lower * inverse
        up_ref[level] = ratio
        return upper, ratio

    zero = jnp.zeros((SUB, LANE), jnp.float32)
    lax.fori_loop(0, levels, level_body, (zero, zero), unroll=8)


def step_body(levels, first, final, x_ref, depth, depths, gain_ref, down_ref, up_ref,
              from_west, from_east, from_south, from_north, forcing, out_ref, east_ref, west_ref,
              edge_ref, merged_ref):
    sub = sublane_ids()
    lane = lane_ids()
    pair = lane // 2
    groups = levels // GROUP
    lat_dev = LANE
    first_row = (lax.axis_index("lat") * lax.axis_size("comp") + lax.axis_index("comp")) * lat_dev
    lat_total = lat_dev * lax.axis_size("lat") * lax.axis_size("comp")
    row_ids = (first_row + lane).astype(jnp.float32)
    rotation = CORIOLIS * (2.0 * (row_ids + 0.5) / lat_total - 1.0)
    depth_e, depth_w, depth_n, depth_s = depths
    even = lane % 2 == 0
    for group in range(groups):
        merged_ref[group] = jnp.where(even, tile_at(from_south, group), tile_at(from_north, group))

    thermal = THERMAL / HALINE
    push = 0.5 * GRAVITY * HALINE
    zero = jnp.zeros((SUB, LANE), jnp.float32)

    def forward_level(level, inner, halo, carry, surface):
        sum_e, sum_w, sum_n, sum_s, *prev = carry
        here, east, west, north, south = [], [], [], [], []
        for field in range(FIELDS):
            row = field * levels + level
            value = tile_at(x_ref, row)
            if first:
                value = jnp.where(level < depth, value, 0.0)
            j = inner * FIELDS + field
            side = pltpu.roll(halo, (LANE - 1 - 2 * j) % LANE, 1)
            here.append(value)
            east.append(jnp.where(sub == SUB - 1, row_at(from_east, row), pltpu.roll(value, SUB - 1, 0)))
            west.append(jnp.where(sub == 0, row_at(from_west, row), pltpu.roll(value, 1, 0)))
            north.append(pltpu.roll(jnp.where(lane == 0, side, value), LANE - 1, 1))
            south.append(pltpu.roll(jnp.where(lane == LANE - 1, side, value), 1, 1))
        wet_e, wet_w, wet_n, wet_s = level < depth_e, level < depth_w, level < depth_n, level < depth_s
        keep = 1.0 - (
            (jnp.where(wet_e, DIFFUSE, 0.0) + jnp.where(wet_w, DIFFUSE, 0.0))
            + (jnp.where(wet_n, DIFFUSE, 0.0) + jnp.where(wet_s, DIFFUSE, 0.0))
        )
        sum_e = sum_e + (east[1] - thermal * east[0])
        sum_w = sum_w + (west[1] - thermal * west[0])
        sum_n = sum_n + (north[1] - thermal * north[0])
        sum_s = sum_s + (south[1] - thermal * south[0])
        force_x = push * (jnp.where(wet_e, sum_e, 0.0) - jnp.where(wet_w, sum_w, 0.0))
        force_y = push * (jnp.where(wet_n, sum_n, 0.0) - jnp.where(wet_s, sum_s, 0.0))
        u, v = here[2], here[3]
        u_part = (0.5 * ADVECTION) * u
        v_part = (0.5 * ADVECTION) * v
        explicit = []
        for field in range(FIELDS):
            spread_sum = (east[field] + west[field]) + (north[field] + south[field])
            value = keep * here[field] + DIFFUSE * spread_sum
            if field < 2:
                value = value - (
                    u_part * (east[field] - west[field]) + v_part * (north[field] - south[field])
                )
            elif field == 2:
                value = value + (rotation * v - force_x)
            else:
                value = value - (rotation * u + force_y)
            if surface:
                value = value + SURFACE_GAIN[field] * forcing[field]
            explicit.append(value)
        gain = gain_ref[level]
        down = down_ref[level]
        done = []
        for field in range(FIELDS):
            value = explicit[field] * gain + down * prev[field]
            put_tile(out_ref, field * levels + level, value)
            done.append(value)
        return (sum_e, sum_w, sum_n, sum_s, *done)

    carry = (zero,) * 8
    halo = merged_ref[0]
    for inner in range(GROUP):
        carry = forward_level(inner, inner, halo, carry, inner == 0)

    def forward_group(group, carry):
        halo = merged_ref[group]
        for inner in range(GROUP):
            carry = forward_level(group * GROUP + inner, inner, halo, carry, False)
        return carry

    carry = lax.fori_loop(1, groups, forward_group, carry)

    def backward_group(step, following):
        group = groups - 1 - step
        packed = zero
        for inner in range(GROUP - 1, -1, -1):
            level = group * GROUP + inner
            ratio = up_ref[level]
            now = []
            for field in range(FIELDS):
                value = tile_at(out_ref, field * levels + level) + ratio * following[field]
                put_tile(out_ref, field * levels + level, value)
                now.append(value)
                if not final:
                    j = inner * FIELDS + field
                    packed = jnp.where(pair == j, pltpu.roll(value, 2 * j + 1, 1), packed)
            following = tuple(now)
        if not final:
            put_tile(edge_ref, group, packed)
        return following

    lax.fori_loop(0, groups, backward_group, (zero,) * FIELDS)
    if not final:
        rows = FIELDS * levels
        for out_col, column in ((east_ref, SUB - 1), (west_ref, 0)):
            for row in range(0, rows, SUB):
                out_col[pl.ds(row, SUB), :] = out_ref[pl.ds(row * SUB + column, SUB, stride=SUB), :]


def first_kernel(levels, lon_total, x_ref, count_ref, gain_ref, down_ref, up_ref, west_in, east_in,
                 south_in, north_in, parts_ref, *rest):
    others = rest[:lon_total - 3]
    out_ref, east_ref, west_ref, edge_ref, depth_ref, merged_ref = rest[lon_total - 3:]
    sub = sublane_ids()
    lane = lane_ids()
    rows = FIELDS * levels
    depth = count_ref[...]
    count_f = depth.astype(jnp.float32)
    extra_w = west_in[pl.ds(rows, EXTRA), :]
    extra_e = east_in[pl.ds(rows, EXTRA), :]
    groups = levels // GROUP
    side_s = tile_at(south_in, groups)
    side_n = tile_at(north_in, groups)
    depth_e = jnp.where(sub == SUB - 1, spread(extra_e[COUNT_ROW:COUNT_ROW + 1]), pltpu.roll(count_f, SUB - 1, 0))
    depth_w = jnp.where(sub == 0, spread(extra_w[COUNT_ROW:COUNT_ROW + 1]), pltpu.roll(count_f, 1, 0))
    depth_n = pltpu.roll(jnp.where(lane == 0, pltpu.roll(side_n, LANE - 1, 1), count_f), LANE - 1, 1)
    depth_s = pltpu.roll(jnp.where(lane == LANE - 1, pltpu.roll(side_s, LANE - 1, 1), count_f), 1, 1)
    depths = []
    for at, value in enumerate((depth_e, depth_w, depth_n, depth_s)):
        value = value.astype(jnp.int32)
        put_tile(depth_ref, at, value)
        depths.append(value)
    forcing = [jnp.zeros((SUB, LANE), jnp.float32)] * FIELDS
    for tile in [parts_ref[0], extra_w, extra_e] + [other[...] for other in others]:
        mine = sub == spread(tile[SLOT_ROW:SLOT_ROW + 1]).astype(jnp.int32)
        for field in range(FIELDS):
            forcing[field] = forcing[field] + jnp.where(mine, spread(tile[field:field + 1]), 0.0)
    step_body(levels, True, False, x_ref, depth, depths, gain_ref, down_ref, up_ref, west_in, east_in,
              south_in, north_in, forcing, out_ref, east_ref, west_ref, edge_ref, merged_ref)
    put_tile(edge_ref, groups, jnp.zeros((SUB, LANE), jnp.float32))


def second_kernel(levels, lon_total, x_ref, gain_ref, down_ref, up_ref, west_in, east_in, south_in, north_in,
                  depth_ref, extra_w_ref, extra_e_ref, parts_ref, *rest):
    others = rest[:lon_total - 3]
    out_ref, merged_ref = rest[lon_total - 3:]
    sub = sublane_ids()
    rows = FIELDS * levels
    extra_w = extra_w_ref[pl.ds(rows, EXTRA), :]
    extra_e = extra_e_ref[pl.ds(rows, EXTRA), :]
    depths = [tile_at(depth_ref, at) for at in range(4)]
    forcing = [jnp.zeros((SUB, LANE), jnp.float32)] * FIELDS
    for tile in [parts_ref[0], extra_w, extra_e] + [other[...] for other in others]:
        mine = sub == spread(tile[SLOT_ROW:SLOT_ROW + 1]).astype(jnp.int32)
        for field in range(FIELDS):
            forcing[field] = forcing[field] + jnp.where(mine, spread(tile[field:field + 1]), 0.0)
    step_body(levels, False, True, x_ref, None, depths, gain_ref, down_ref, up_ref, west_in, east_in,
              south_in, north_in, forcing, out_ref, None, None, None, merged_ref)


def call(kernel, outs, args, specs=None, scratch=()):
    return pl.pallas_call(
        kernel,
        out_shape=[jax.ShapeDtypeStruct(shape, dtype) for shape, dtype in outs],
        in_specs=specs or [VMEM_SPEC] * len(args),
        out_specs=[VMEM_SPEC] * len(outs),
        scratch_shapes=list(scratch),
    )(*args)


def shift_by(value, axis, amount, periodic):
    count = lax.axis_size(axis)
    if periodic:
        pairs = [(i, (i + amount) % count) for i in range(count)]
    else:
        pairs = [(i, i + amount) for i in range(count) if 0 <= i + amount < count]
    return lax.ppermute(value, axis, pairs)


def bind(kernel, *head):
    def bound(*refs):
        return kernel(*head, *refs)
    bound.__name__ = kernel.__name__
    return bound


def local(ocean_state, level_count, mix_rate, atmos_flux, remap_weight, remap_target, remap_slot):
    field_total, levels, lon_dev, lat_dev = ocean_state.shape
    lon_total = lax.axis_size("lon")
    rows = field_total * levels
    groups = levels // GROUP
    f32 = jnp.float32
    x = ocean_state.reshape(rows * lon_dev, lat_dev)
    message = ((rows + EXTRA, lat_dev), f32)
    edges = (((groups + 1) * SUB, lat_dev), f32)
    table = ((levels, lon_dev, lat_dev), f32)

    east, west, edge, parts = call(
        bind(pack_kernel, levels, lon_total),
        [message, message, edges, ((lon_total, SUB, lat_dev), f32)],
        (x, level_count, atmos_flux[0], remap_weight[0], remap_target, remap_slot),
        [VMEM_SPEC] * 4 + [SMEM_SPEC] * 2,
    )
    from_west = shift_by(east, "lon", 1, True)
    from_east = shift_by(west, "lon", -1, True)
    from_south = shift_by(edge, LAT_AXES, 1, False)
    from_north = shift_by(edge, LAT_AXES, -1, False)
    others = [shift_by(parts[s], "lon", s, True) for s in range(2, lon_total - 1)]
    gain, down, up = call(bind(factor_kernel, levels), [table] * 3, (mix_rate, level_count))
    scratch = [pltpu.VMEM((groups, SUB, LANE), f32)]
    next_message = ((rows, lat_dev), f32)
    state, east, west, edge, depths = call(
        bind(first_kernel, levels, lon_total),
        [((rows * lon_dev, lat_dev), f32), next_message, next_message, edges, ((4 * SUB, LANE), jnp.int32)],
        (x, level_count, gain, down, up, from_west, from_east, from_south, from_north, parts, *others),
        scratch=scratch,
    )
    second_west = shift_by(east, "lon", 1, True)
    second_east = shift_by(west, "lon", -1, True)
    second_south = shift_by(edge, LAT_AXES, 1, False)
    second_north = shift_by(edge, LAT_AXES, -1, False)
    (state,) = call(
        bind(second_kernel, levels, lon_total),
        [((rows * lon_dev, lat_dev), f32)],
        (state, gain, down, up, second_west, second_east, second_south, second_north, depths,
         from_west, from_east, parts, *others),
        scratch=scratch,
    )
    return state.reshape(ocean_state.shape)


def solution(mesh):
    placed = (
        P(None, None, "lon", LAT_AXES),
        P("lon", LAT_AXES),
        P(None, "lon", LAT_AXES),
        P(LAT_AXES, "lon", None, None),
        P(LAT_AXES, "lon", None, None),
        P(LAT_AXES, "lon"),
        P(LAT_AXES, "lon"),
    )
    return jax.shard_map(
        local,
        mesh=mesh,
        in_specs=placed,
        out_specs=P(None, None, "lon", LAT_AXES),
        check_vma=False,
    )
```

```python
import jax
import jax.numpy as jnp
from jax import lax
from jax.experimental import pallas as pl
from jax.experimental.pallas import tpu as pltpu
from jax.sharding import PartitionSpec as P


DIFFUSE = 0.2
ADVECTION = 0.5
THERMAL = 0.2
HALINE = 0.15
GRAVITY = 0.05
CORIOLIS = 0.3
SURFACE_GAIN = (0.5, 0.4, 0.6, 0.6)

FIELDS = 4
SUB = 8
LANE = 128
PAIRS = LANE // 2
GROUP = PAIRS // FIELDS
EXTRA = 8
SLOT_ROW = 4
COUNT_ROW = 5
LAT_AXES = ("lat", "comp")

VMEM_SPEC = pl.BlockSpec(memory_space=pltpu.VMEM)
ANY_SPEC = pl.BlockSpec(memory_space=pl.ANY)
SMEM_SPEC = pl.BlockSpec(memory_space=pltpu.SMEM)


def sublane_ids():
    return lax.broadcasted_iota(jnp.int32, (SUB, LANE), 0)


def lane_ids():
    return lax.broadcasted_iota(jnp.int32, (SUB, LANE), 1)


def spread(row):
    return jnp.broadcast_to(row, (SUB, LANE))


def lat_place():
    return lax.axis_index("lat") * lax.axis_size("comp") + lax.axis_index("comp")


def lat_sides(swap_a, swap_b, index):
    place = lat_place()
    total = lax.axis_size("lat") * lax.axis_size("comp")
    tile_a, tile_b = tile_at(swap_a, index), tile_at(swap_b, index)
    evenly = place % 2 == 0
    north = jnp.where(jnp.logical_and(place < total - 1, evenly), tile_a, 0.0)
    north = jnp.where(jnp.logical_and(place < total - 1, jnp.logical_not(evenly)), tile_b, north)
    south = jnp.where(jnp.logical_and(place > 0, evenly), tile_b, 0.0)
    south = jnp.where(jnp.logical_and(place > 0, jnp.logical_not(evenly)), tile_a, south)
    return south, north


def tile_at(ref, index):
    return ref[pl.ds(pl.multiple_of(index * SUB, SUB), SUB), :]


def put_tile(ref, index, value):
    ref[pl.ds(pl.multiple_of(index * SUB, SUB), SUB), :] = value


def row_at(ref, index):
    return spread(ref[pl.ds(index, 1), :])


def pack_kernel(levels, lon_total, x_ref, count_ref, flux_ref, weight_ref, target_ref, slot_ref,
                east_ref, west_ref, parts_ref):
    me = lax.axis_index("lon")
    sub = sublane_ids()
    count = count_ref[...]
    rows = FIELDS * levels

    for out_ref, column in ((east_ref, SUB - 1), (west_ref, 0)):
        depth = spread(count[column:column + 1, :])
        for field in range(FIELDS):
            for start in range(0, levels, SUB):
                row = field * levels + start
                value = x_ref[pl.ds(row * SUB + column, SUB, stride=SUB), :]
                out_ref[pl.ds(row, SUB), :] = jnp.where(start + sub < depth, value, 0.0)

    blocks = flux_ref.shape[0]
    for block in range(blocks):
        partial = jnp.dot(flux_ref[block], weight_ref[block], preferred_element_type=jnp.float32)
        slot = slot_ref[0, block].astype(jnp.float32)
        tile = jnp.concatenate([partial, jnp.full((SUB - FIELDS, LANE), slot, jnp.float32)], axis=0)
        shift = lax.rem(target_ref[0, block] - me + lon_total, lon_total)
        parts_ref[shift] = tile

    count_f = count.astype(jnp.float32)
    for out_ref, column, shift in ((east_ref, SUB - 1, 1), (west_ref, 0, lon_total - 1)):
        tile = parts_ref[shift]
        out_ref[pl.ds(rows, EXTRA), :] = jnp.where(
            sub == COUNT_ROW, spread(count_f[column:column + 1, :]), tile
        )


def edge_kernel(levels, x_ref, count_ref, after_ref, edge_ref):
    del after_ref
    pair = ((lane_ids() + 1) % LANE) // 2
    count = count_ref[...]
    count_f = count.astype(jnp.float32)

    def group_body(group, carry):
        packed = jnp.zeros((SUB, LANE), jnp.float32)
        for inner in range(GROUP):
            level = group * GROUP + inner
            wet = level < count
            for field in range(FIELDS):
                j = inner * FIELDS + field
                value = jnp.where(wet, tile_at(x_ref, field * levels + level), 0.0)
                packed = jnp.where(pair == j, pltpu.roll(value, 2 * j, 1) if j else value, packed)
        put_tile(edge_ref, group, packed)
        return carry

    lax.fori_loop(0, levels // GROUP, group_body, 0)
    put_tile(edge_ref, levels // GROUP, count_f)


def factor_kernel(levels, rate_ref, count_ref, gain_ref, down_ref, up_ref):
    count = count_ref[...]

    def level_body(level, carry):
        lower, prev = carry
        upper = jnp.where(level + 1 < count, rate_ref[level], 0.0)
        upper = jnp.where(level < levels - 1, upper, 0.0)
        pivot = 1.0 + upper + lower - lower * prev
        inverse = 1.0 / pivot
        ratio = upper * inverse
        gain_ref[level] = jnp.where(level < count, inverse, 0.0)
        down_ref[level] = lower * inverse
        up_ref[level] = ratio
        return upper, ratio

    zero = jnp.zeros((SUB, LANE), jnp.float32)
    lax.fori_loop(0, levels, level_body, (zero, zero), unroll=8)


def step_body(levels, first, final, x_ref, depth, depths, gain_ref, down_ref, up_ref,
              from_west, from_east, swap_a, swap_b, forcing, out_ref, east_ref, west_ref,
              edge_ref, merged_ref, result_ref=None, sem_ref=None):
    sub = sublane_ids()
    lane = lane_ids()
    pair = ((lane + 1) % LANE) // 2
    groups = levels // GROUP
    lat_dev = LANE
    first_row = lat_place() * lat_dev
    lat_total = lat_dev * lax.axis_size("lat") * lax.axis_size("comp")
    row_ids = (first_row + lane).astype(jnp.float32)
    rotation = CORIOLIS * (2.0 * (row_ids + 0.5) / lat_total - 1.0)
    depth_e, depth_w, depth_n, depth_s = depths
    even = lane % 2 == 0
    for group in range(groups):
        south, north = lat_sides(swap_a, swap_b, group)
        merged_ref[group] = jnp.where(even, north, pltpu.roll(south, 2, 1))

    thermal = THERMAL / HALINE
    push = 0.5 * GRAVITY * HALINE
    zero = jnp.zeros((SUB, LANE), jnp.float32)

    def forward_level(level, inner, halo, carry, surface):
        sum_e, sum_w, sum_n, sum_s, *prev = carry
        here, east, west, north, south = [], [], [], [], []
        for field in range(FIELDS):
            row = field * levels + level
            value = tile_at(x_ref, row)
            if first:
                value = jnp.where(level < depth, value, 0.0)
            j = inner * FIELDS + field
            side = pltpu.roll(halo, (LANE - 1 - 2 * j) % LANE, 1)
            here.append(value)
            east.append(jnp.where(sub == SUB - 1, row_at(from_east, row), pltpu.roll(value, SUB - 1, 0)))
            west.append(jnp.where(sub == 0, row_at(from_west, row), pltpu.roll(value, 1, 0)))
            north.append(jnp.where(lane == LANE - 1, side, pltpu.roll(value, LANE - 1, 1)))
            south.append(jnp.where(lane == 0, side, pltpu.roll(value, 1, 1)))
        wet_e, wet_w, wet_n, wet_s = level < depth_e, level < depth_w, level < depth_n, level < depth_s
        keep = 1.0 - (
            (jnp.where(wet_e, DIFFUSE, 0.0) + jnp.where(wet_w, DIFFUSE, 0.0))
            + (jnp.where(wet_n, DIFFUSE, 0.0) + jnp.where(wet_s, DIFFUSE, 0.0))
        )
        sum_e = sum_e + (east[1] - thermal * east[0])
        sum_w = sum_w + (west[1] - thermal * west[0])
        sum_n = sum_n + (north[1] - thermal * north[0])
        sum_s = sum_s + (south[1] - thermal * south[0])
        force_x = push * (jnp.where(wet_e, sum_e, 0.0) - jnp.where(wet_w, sum_w, 0.0))
        force_y = push * (jnp.where(wet_n, sum_n, 0.0) - jnp.where(wet_s, sum_s, 0.0))
        u, v = here[2], here[3]
        u_part = (0.5 * ADVECTION) * u
        v_part = (0.5 * ADVECTION) * v
        explicit = []
        for field in range(FIELDS):
            spread_sum = (east[field] + west[field]) + (north[field] + south[field])
            value = keep * here[field] + DIFFUSE * spread_sum
            if field < 2:
                value = value - (
                    u_part * (east[field] - west[field]) + v_part * (north[field] - south[field])
                )
            elif field == 2:
                value = value + (rotation * v - force_x)
            else:
                value = value - (rotation * u + force_y)
            if surface:
                value = value + SURFACE_GAIN[field] * forcing[field]
            explicit.append(value)
        gain = gain_ref[level]
        down = down_ref[level]
        done = []
        for field in range(FIELDS):
            value = explicit[field] * gain + down * prev[field]
            put_tile(out_ref, field * levels + level, value)
            done.append(value)
        return (sum_e, sum_w, sum_n, sum_s, *done)

    carry = (zero,) * 8
    halo = merged_ref[0]
    for inner in range(GROUP):
        carry = forward_level(inner, inner, halo, carry, inner == 0)

    def forward_group(group, carry):
        halo = merged_ref[group]
        for inner in range(GROUP):
            carry = forward_level(group * GROUP + inner, inner, halo, carry, False)
        return carry

    carry = lax.fori_loop(1, groups, forward_group, carry)

    def backward_group(step, following):
        group = groups - 1 - step
        packed = zero
        for inner in range(GROUP - 1, -1, -1):
            level = group * GROUP + inner
            ratio = up_ref[level]
            now = []
            for field in range(FIELDS):
                value = tile_at(out_ref, field * levels + level) + ratio * following[field]
                put_tile(out_ref, field * levels + level, value)
                now.append(value)
                if not final:
                    j = inner * FIELDS + field
                    packed = jnp.where(pair == j, pltpu.roll(value, 2 * j, 1) if j else value, packed)
            following = tuple(now)
        if not final:
            put_tile(edge_ref, group, packed)
        else:
            for copy in copies_of(group):
                copy.start()
        return following

    def copies_of(group):
        size = GROUP * SUB
        for field in range(FIELDS):
            start = pl.multiple_of(field * levels * SUB + group * size, size)
            yield pltpu.make_async_copy(
                out_ref.at[pl.ds(start, size), :], result_ref.at[pl.ds(start, size), :], sem_ref.at[group, field]
            )

    lax.fori_loop(0, groups, backward_group, (zero,) * FIELDS)
    if final:
        for group in range(groups):
            for copy in copies_of(group):
                copy.wait()
    if not final:
        rows = FIELDS * levels
        for out_col, column in ((east_ref, SUB - 1), (west_ref, 0)):
            for row in range(0, rows, SUB):
                out_col[pl.ds(row, SUB), :] = out_ref[pl.ds(row * SUB + column, SUB, stride=SUB), :]


def first_kernel(levels, lon_total, x_ref, count_ref, gain_ref, down_ref, up_ref, west_in, east_in,
                 swap_a, swap_b, parts_ref, *rest):
    others = rest[:lon_total - 3]
    out_ref, east_ref, west_ref, edge_ref, depth_ref, merged_ref = rest[lon_total - 3:]
    sub = sublane_ids()
    lane = lane_ids()
    rows = FIELDS * levels
    depth = count_ref[...]
    count_f = depth.astype(jnp.float32)
    extra_w = west_in[pl.ds(rows, EXTRA), :]
    extra_e = east_in[pl.ds(rows, EXTRA), :]
    groups = levels // GROUP
    side_s, side_n = lat_sides(swap_a, swap_b, groups)
    depth_e = jnp.where(sub == SUB - 1, spread(extra_e[COUNT_ROW:COUNT_ROW + 1]), pltpu.roll(count_f, SUB - 1, 0))
    depth_w = jnp.where(sub == 0, spread(extra_w[COUNT_ROW:COUNT_ROW + 1]), pltpu.roll(count_f, 1, 0))
    depth_n = jnp.where(lane == LANE - 1, pltpu.roll(side_n, LANE - 1, 1), pltpu.roll(count_f, LANE - 1, 1))
    depth_s = jnp.where(lane == 0, pltpu.roll(side_s, 1, 1), pltpu.roll(count_f, 1, 1))
    depths = []
    for at, value in enumerate((depth_e, depth_w, depth_n, depth_s)):
        value = value.astype(jnp.int32)
        put_tile(depth_ref, at, value)
        depths.append(value)
    forcing = [jnp.zeros((SUB, LANE), jnp.float32)] * FIELDS
    for tile in [parts_ref[0], extra_w, extra_e] + [other[...] for other in others]:
        mine = sub == spread(tile[SLOT_ROW:SLOT_ROW + 1]).astype(jnp.int32)
        for field in range(FIELDS):
            forcing[field] = forcing[field] + jnp.where(mine, spread(tile[field:field + 1]), 0.0)
    step_body(levels, True, False, x_ref, depth, depths, gain_ref, down_ref, up_ref, west_in, east_in,
              swap_a, swap_b, forcing, out_ref, east_ref, west_ref, edge_ref, merged_ref)
    put_tile(edge_ref, groups, jnp.zeros((SUB, LANE), jnp.float32))


def second_kernel(levels, lon_total, x_ref, gain_ref, down_ref, up_ref, west_in, east_in, swap_a, swap_b,
                  depth_ref, extra_w_ref, extra_e_ref, parts_ref, *rest):
    others = rest[:lon_total - 3]
    result_ref, merged_ref, out_ref, sem_ref = rest[lon_total - 3:]
    sub = sublane_ids()
    rows = FIELDS * levels
    extra_w = extra_w_ref[pl.ds(rows, EXTRA), :]
    extra_e = extra_e_ref[pl.ds(rows, EXTRA), :]
    depths = [tile_at(depth_ref, at) for at in range(4)]
    forcing = [jnp.zeros((SUB, LANE), jnp.float32)] * FIELDS
    for tile in [parts_ref[0], extra_w, extra_e] + [other[...] for other in others]:
        mine = sub == spread(tile[SLOT_ROW:SLOT_ROW + 1]).astype(jnp.int32)
        for field in range(FIELDS):
            forcing[field] = forcing[field] + jnp.where(mine, spread(tile[field:field + 1]), 0.0)
    step_body(levels, False, True, x_ref, None, depths, gain_ref, down_ref, up_ref, west_in, east_in,
              swap_a, swap_b, forcing, out_ref, None, None, None, merged_ref, result_ref, sem_ref)


VMEM_BYTES = 16 << 20


def call(kernel, outs, args, specs=None, scratch=(), to_hbm=False):
    specs = specs or [VMEM_SPEC] * len(args)
    held = [
        pltpu.with_memory_space_constraint(arg, pltpu.VMEM) if spec is VMEM_SPEC else arg
        for arg, spec in zip(args, specs)
    ]
    kind = jax.ShapeDtypeStruct if to_hbm else pltpu.VMEM
    return pl.pallas_call(
        kernel,
        out_shape=[kind(shape, dtype) for shape, dtype in outs],
        in_specs=specs,
        out_specs=[ANY_SPEC if to_hbm else VMEM_SPEC] * len(outs),
        scratch_shapes=list(scratch),
        compiler_params=pltpu.CompilerParams(vmem_limit_bytes=VMEM_BYTES),
    )(*held)


def ring_shift(value, axis, amount):
    count = lax.axis_size(axis)
    return lax.ppermute(value, axis, [(i, (i + amount) % count) for i in range(count)])


def pair_swap(value, axis, first):
    count = lax.axis_size(axis)
    pairs = []
    for low in range(first, count, 2):
        high = (low + 1) % count
        pairs += [(low, high), (high, low)]
    return lax.ppermute(value, axis, pairs)


def bind(kernel, *head):
    def bound(*refs):
        return kernel(*head, *refs)

    bound.__name__ = kernel.__name__
    return bound


def local(ocean_state, level_count, mix_rate, atmos_flux, remap_weight, remap_target, remap_slot):
    field_total, levels, lon_dev, lat_dev = ocean_state.shape
    lon_total = lax.axis_size("lon")
    rows = field_total * levels
    groups = levels // GROUP
    f32 = jnp.float32
    x = ocean_state.reshape(rows * lon_dev, lat_dev)
    message = ((rows + EXTRA, lat_dev), f32)
    edges = (((groups + 1) * SUB, lat_dev), f32)
    table = ((levels, lon_dev, lat_dev), f32)

    east, west, parts = call(
        bind(pack_kernel, levels, lon_total),
        [message, message, ((lon_total, SUB, lat_dev), f32)],
        (x, level_count, atmos_flux[0], remap_weight[0], remap_target, remap_slot),
        [VMEM_SPEC] * 4 + [SMEM_SPEC] * 2,
    )
    from_west = ring_shift(east, "lon", 1)
    from_east = ring_shift(west, "lon", -1)
    others = [ring_shift(parts[s], "lon", s) for s in range(2, lon_total - 1)]
    (edge,) = call(bind(edge_kernel, levels), [edges], (x, level_count, parts))
    swap_a = pair_swap(edge, LAT_AXES, 0)
    swap_b = pair_swap(edge, LAT_AXES, 1)
    gain, down, up = call(bind(factor_kernel, levels), [table] * 3, (mix_rate, level_count))
    scratch = [pltpu.VMEM((groups, SUB, LANE), f32)]
    next_message = ((rows, lat_dev), f32)
    state, east, west, edge, depths = call(
        bind(first_kernel, levels, lon_total),
        [((rows * lon_dev, lat_dev), f32), next_message, next_message, edges, ((4 * SUB, LANE), jnp.int32)],
        (x, level_count, gain, down, up, from_west, from_east, swap_a, swap_b, parts, *others),
        scratch=scratch,
    )
    second_west = ring_shift(east, "lon", 1)
    second_east = ring_shift(west, "lon", -1)
    second_a = pair_swap(edge, LAT_AXES, 0)
    second_b = pair_swap(edge, LAT_AXES, 1)
    (state,) = call(
        bind(second_kernel, levels, lon_total),
        [((rows * lon_dev, lat_dev), f32)],
        (state, gain, down, up, second_west, second_east, second_a, second_b, depths,
         from_west, from_east, parts, *others),
        scratch=scratch + [pltpu.VMEM((rows * lon_dev, lat_dev), f32), pltpu.SemaphoreType.DMA((groups, FIELDS))],
        to_hbm=True,
    )
    return state.reshape(ocean_state.shape)


def solution(mesh):
    placed = (
        P(None, None, "lon", LAT_AXES),
        P("lon", LAT_AXES),
        P(None, "lon", LAT_AXES),
        P(LAT_AXES, "lon", None, None),
        P(LAT_AXES, "lon", None, None),
        P(LAT_AXES, "lon"),
        P(LAT_AXES, "lon"),
    )

    return jax.shard_map(
        local,
        mesh=mesh,
        in_specs=placed,
        out_specs=P(None, None, "lon", LAT_AXES),
        check_vma=False,
    )
```

```python
import jax
import jax.numpy as jnp
from jax import lax
from jax.experimental import pallas as pl
from jax.experimental.pallas import tpu as pltpu
from jax.sharding import PartitionSpec as P


DIFFUSE = 0.2
ADVECTION = 0.5
THERMAL = 0.2
HALINE = 0.15
GRAVITY = 0.05
CORIOLIS = 0.3
SURFACE_GAIN = (0.5, 0.4, 0.6, 0.6)

FIELDS = 4
SUB = 8
LANE = 128
PAIRS = LANE // 2
GROUP = PAIRS // FIELDS
EXTRA = 8
SLOT_ROW = 4
COUNT_ROW = 5
LAT_AXES = ("lat", "comp")
QUARTER = 0.5 * ADVECTION
WARMTH = THERMAL / HALINE
PUSH = 0.5 * GRAVITY * HALINE

VMEM_SPEC = pl.BlockSpec(memory_space=pltpu.VMEM)
HBM_SPEC = pl.BlockSpec(memory_space=pltpu.HBM)
VMEM_BYTES = 16 << 20


def sublane_ids():
    return lax.broadcasted_iota(jnp.int32, (SUB, LANE), 0)


def lane_ids():
    return lax.broadcasted_iota(jnp.int32, (SUB, LANE), 1)


def zeros():
    return jnp.zeros((SUB, LANE), jnp.float32)


def spread(row):
    return jnp.broadcast_to(row, (SUB, LANE))


def tile_at(ref, index):
    return ref[pl.ds(pl.multiple_of(index * SUB, SUB), SUB), :]


def put_tile(ref, index, value):
    ref[pl.ds(pl.multiple_of(index * SUB, SUB), SUB), :] = value


def lat_place():
    return lax.axis_index("lat") * lax.axis_size("comp") + lax.axis_index("comp")


def lat_sides(swap_a, swap_b, index):
    place = lat_place()
    total = lax.axis_size("lat") * lax.axis_size("comp")
    tile_a, tile_b = tile_at(swap_a, index), tile_at(swap_b, index)
    evenly = place % 2 == 0
    north = jnp.where(jnp.logical_and(place < total - 1, evenly), tile_a, 0.0)
    north = jnp.where(jnp.logical_and(place < total - 1, jnp.logical_not(evenly)), tile_b, north)
    south = jnp.where(jnp.logical_and(place > 0, evenly), tile_b, 0.0)
    south = jnp.where(jnp.logical_and(place > 0, jnp.logical_not(evenly)), tile_a, south)
    return south, north


def column_tiles(levels, level, east_ref, west_ref, even):
    half = levels // 2
    if level < half:
        return jnp.where(even, tile_at(east_ref, level), pltpu.roll(tile_at(west_ref, level), 1, 0))
    at = level - half
    return jnp.where(even, pltpu.roll(tile_at(east_ref, at), SUB - 1, 0), tile_at(west_ref, at))


def column_kernel(levels, lon_total, x_ref, count_hbm, flux_hbm, weight_hbm, target_hbm, slot_hbm,
                  east_ref, west_ref, parts_ref, count_ref,
                  columns, flux_ref, weight_ref, target_ref, slot_ref, sems):
    me = lax.axis_index("lon")
    half = levels // 2
    sub = sublane_ids()
    copies = [
        pltpu.make_async_copy(count_hbm, count_ref, sems.at[2]),
        pltpu.make_async_copy(flux_hbm, flux_ref, sems.at[3]),
        pltpu.make_async_copy(weight_hbm, weight_ref, sems.at[4]),
        pltpu.make_async_copy(target_hbm, target_ref, sems.at[5]),
        pltpu.make_async_copy(slot_hbm, slot_ref, sems.at[6]),
    ]
    sides = [
        pltpu.make_async_copy(x_ref.at[:, SUB - 1, :], columns.at[0], sems.at[0]),
        pltpu.make_async_copy(x_ref.at[:, 0, :], columns.at[1], sems.at[1]),
    ]
    for copy in sides + copies:
        copy.start()
    for copy in copies:
        copy.wait()

    blocks = flux_ref.shape[0]
    for block in range(blocks):
        partial = jnp.dot(flux_ref[block], weight_ref[block], preferred_element_type=jnp.float32)
        slot = slot_ref[0, block].astype(jnp.float32)
        tile = jnp.concatenate([partial, jnp.full((SUB - FIELDS, LANE), slot, jnp.float32)], axis=0)
        shift = lax.rem(target_ref[0, block] - me + lon_total, lon_total)
        parts_ref[shift] = tile

    count = count_ref[...]
    count_f = count.astype(jnp.float32)
    for side, (out_ref, column, shift) in enumerate(
        ((east_ref, SUB - 1, 1), (west_ref, 0, lon_total - 1))
    ):
        sides[side].wait()
        depth = spread(count[column:column + 1, :])
        for field in range(FIELDS):
            for start in range(0, levels, SUB):
                value = columns[side, pl.ds(field * levels + start, SUB), :]
                value = jnp.where(start + sub < depth, value, 0.0)
                upper = start // half
                row = (start - upper * half) * SUB + 2 * field + upper
                out_ref[pl.ds(row, SUB, stride=SUB), :] = value
        out_ref[pl.ds(half * SUB, EXTRA), :] = jnp.where(
            sub == COUNT_ROW, spread(count_f[column:column + 1, :]), parts_ref[shift]
        )


def edge_kernel(levels, x_ref, count_ref, edge_ref):
    pair = ((lane_ids() + 1) % LANE) // 2
    count = count_ref[...]

    def group_body(group, carry):
        packed = zeros()
        for inner in range(GROUP):
            level = group * GROUP + inner
            wet = level < count
            for field in range(FIELDS):
                j = inner * FIELDS + field
                value = jnp.where(wet, tile_at(x_ref, field * levels + level), 0.0)
                packed = jnp.where(pair == j, pltpu.roll(value, 2 * j, 1) if j else value, packed)
        put_tile(edge_ref, group, packed)
        return carry

    lax.fori_loop(0, levels // GROUP, group_body, 0)
    put_tile(edge_ref, levels // GROUP, count.astype(jnp.float32))


def factor_kernel(levels, rate_ref, count_ref, gain_ref, down_ref, up_ref, reply_ref,
                  edge_gain_ref, edge_down_ref, edge_up_ref):
    count = count_ref[...]

    def level_body(level, carry):
        lower, prev, reply = carry
        upper = jnp.where(level + 1 < count, tile_at(rate_ref, level), 0.0)
        upper = jnp.where(level < levels - 1, upper, 0.0)
        pivot = 1.0 + upper + lower - lower * prev
        inverse = 1.0 / pivot
        ratio = upper * inverse
        gain = jnp.where(level < count, inverse, 0.0)
        down = lower * inverse
        put_tile(gain_ref, level, gain)
        put_tile(down_ref, level, down)
        put_tile(up_ref, level, ratio)
        reply = jnp.where(level == 0, gain, down * reply)
        put_tile(reply_ref, level, reply)
        return upper, ratio, reply

    lax.fori_loop(0, levels, level_body, (zeros(), zeros(), zeros()), unroll=8)

    def back_body(step, following):
        level = levels - 1 - step
        value = tile_at(reply_ref, level) + tile_at(up_ref, level) * following
        put_tile(reply_ref, level, value)
        return value

    lax.fori_loop(0, levels, back_body, zeros(), unroll=8)
    for source_ref, out_ref in ((gain_ref, edge_gain_ref), (down_ref, edge_down_ref), (up_ref, edge_up_ref)):
        pack_edges(levels, 1, source_ref, out_ref)


def pack_edges(levels, fields, source_ref, out_ref):
    for side, column in ((0, SUB - 1), (1, 0)):
        for start in range(0, levels, SUB):
            for field in range(FIELDS):
                if field < fields:
                    row = (field * levels + start) * SUB + column
                    value = source_ref[pl.ds(row, SUB, stride=SUB), :]
                out_ref[pl.ds(start * SUB + 2 * field + side, SUB, stride=SUB), :] = value


def inner_step(levels, first, x_ref, depth, depths, gain_ref, down_ref, up_ref, swap_a, swap_b,
               out_ref, merged_ref, group_done, force_ref=None):
    sub = sublane_ids()
    lane = lane_ids()
    even = lane % 2 == 0
    groups = levels // GROUP
    lat_total = LANE * lax.axis_size("lat") * lax.axis_size("comp")
    row_ids = (lat_place() * LANE + lane).astype(jnp.float32)
    rotation = CORIOLIS * (2.0 * (row_ids + 0.5) / lat_total - 1.0)
    depth_e, depth_w, depth_n, depth_s = depths
    for group in range(groups):
        south, north = lat_sides(swap_a, swap_b, group)
        merged_ref[group] = jnp.where(even, north, pltpu.roll(south, 2, 1))

    def forward_level(level, inner, halo, carry):
        sum_e, sum_w, sum_n, sum_s, *prev = carry
        here, east, west, north, south = [], [], [], [], []
        for field in range(FIELDS):
            value = tile_at(x_ref, field * levels + level)
            if first:
                value = jnp.where(level < depth, value, 0.0)
            j = inner * FIELDS + field
            side = pltpu.roll(halo, (LANE - 1 - 2 * j) % LANE, 1)
            here.append(value)
            east.append(jnp.where(sub == SUB - 1, 0.0, pltpu.roll(value, SUB - 1, 0)))
            west.append(jnp.where(sub == 0, 0.0, pltpu.roll(value, 1, 0)))
            north.append(jnp.where(lane == LANE - 1, side, pltpu.roll(value, LANE - 1, 1)))
            south.append(jnp.where(lane == 0, side, pltpu.roll(value, 1, 1)))
        wet_e, wet_w, wet_n, wet_s = level < depth_e, level < depth_w, level < depth_n, level < depth_s
        keep = 1.0 - (
            (jnp.where(wet_e, DIFFUSE, 0.0) + jnp.where(wet_w, DIFFUSE, 0.0))
            + (jnp.where(wet_n, DIFFUSE, 0.0) + jnp.where(wet_s, DIFFUSE, 0.0))
        )
        sum_e = sum_e + (east[1] - WARMTH * east[0])
        sum_w = sum_w + (west[1] - WARMTH * west[0])
        sum_n = sum_n + (north[1] - WARMTH * north[0])
        sum_s = sum_s + (south[1] - WARMTH * south[0])
        force_x = PUSH * (jnp.where(wet_e, sum_e, 0.0) - jnp.where(wet_w, sum_w, 0.0))
        force_y = PUSH * (jnp.where(wet_n, sum_n, 0.0) - jnp.where(wet_s, sum_s, 0.0))
        u, v = here[2], here[3]
        u_part = QUARTER * u
        v_part = QUARTER * v
        gain = tile_at(gain_ref, level)
        down = tile_at(down_ref, level)
        done = []
        for field in range(FIELDS):
            around = (east[field] + west[field]) + (north[field] + south[field])
            value = keep * here[field] + DIFFUSE * around
            if field < 2:
                value = value - (
                    u_part * (east[field] - west[field]) + v_part * (north[field] - south[field])
                )
            elif field == 2:
                value = value + (rotation * v - force_x)
            else:
                value = value - (rotation * u + force_y)
            if inner == 0 and force_ref is not None:
                value = value + jnp.where(level == 0, tile_at(force_ref, FIELDS + field), 0.0)
            value = value * gain + down * prev[field]
            put_tile(out_ref, field * levels + level, value)
            done.append(value)
        return (sum_e, sum_w, sum_n, sum_s, *done)

    def forward_group(group, carry):
        halo = merged_ref[group]
        for inner in range(GROUP):
            carry = forward_level(group * GROUP + inner, inner, halo, carry)
        return carry

    lax.fori_loop(0, groups, forward_group, (zeros(),) * 8)

    def backward_group(step, following):
        group = groups - 1 - step
        for inner in range(GROUP - 1, -1, -1):
            level = group * GROUP + inner
            ratio = tile_at(up_ref, level)
            now = []
            for field in range(FIELDS):
                value = tile_at(out_ref, field * levels + level) + ratio * following[field]
                put_tile(out_ref, field * levels + level, value)
                now.append(value)
            following = tuple(now)
        group_done(group)
        return following

    lax.fori_loop(0, groups, backward_group, (zeros(),) * FIELDS)


def first_kernel(levels, x_ref, count_ref, gain_ref, down_ref, up_ref, swap_a, swap_b,
                 out_ref, packed_ref, depth_ref, merged_ref):
    sub = sublane_ids()
    lane = lane_ids()
    depth = count_ref[...]
    count_f = depth.astype(jnp.float32)
    side_s, side_n = lat_sides(swap_a, swap_b, levels // GROUP)
    depths = []
    for at, value in enumerate((
        jnp.where(sub == SUB - 1, 0.0, pltpu.roll(count_f, SUB - 1, 0)),
        jnp.where(sub == 0, 0.0, pltpu.roll(count_f, 1, 0)),
        jnp.where(lane == LANE - 1, pltpu.roll(side_n, LANE - 1, 1), pltpu.roll(count_f, LANE - 1, 1)),
        jnp.where(lane == 0, pltpu.roll(side_s, 1, 1), pltpu.roll(count_f, 1, 1)),
    )):
        value = value.astype(jnp.int32)
        put_tile(depth_ref, at, value)
        depths.append(value)
    inner_step(levels, True, x_ref, depth, depths, gain_ref, down_ref, up_ref, swap_a, swap_b,
               out_ref, merged_ref, lambda group: None)
    pack_edges(levels, FIELDS, out_ref, packed_ref)


def second_kernel(levels, x_ref, depth_ref, gain_ref, down_ref, up_ref, swap_a, swap_b, force_ref,
                  result_ref, packed_ref, merged_ref, out_ref, sem_ref):
    groups = levels // GROUP
    size = GROUP * SUB
    depths = [tile_at(depth_ref, at) for at in range(4)]

    def copies_of(group):
        for field in range(FIELDS):
            start = pl.multiple_of(field * levels * SUB + group * size, size)
            yield pltpu.make_async_copy(
                out_ref.at[pl.ds(start, size), :], result_ref.at[pl.ds(start, size), :], sem_ref.at[group, field]
            )

    def group_done(group):
        for copy in copies_of(group):
            copy.start()

    inner_step(levels, False, x_ref, None, depths, gain_ref, down_ref, up_ref, swap_a, swap_b,
               out_ref, merged_ref, group_done, force_ref)
    pack_edges(levels, FIELDS, out_ref, packed_ref)
    for group in range(groups):
        for copy in copies_of(group):
            copy.wait()


def edge_change(levels, halo_at, own_at, halo_depth, gain_ref, down_ref, up_ref, surface, change_ref, finish):
    sub = sublane_ids()
    even = sub % 2 == 0
    field = sub // 2
    sign = jnp.where(even, 1.0, -1.0)
    carry_by = jnp.where(field < 2, -QUARTER * sign, 0.0)
    push_by = jnp.where(field == 2, -PUSH * sign, 0.0)
    total = zeros()
    value = zeros()
    for level in range(levels):
        halo = halo_at(level)
        own = own_at(level)
        wet = level < halo_depth
        speed = jnp.where(field == 0, pltpu.roll(own, 4, 0), pltpu.roll(own, 6, 0))
        total = total + (pltpu.roll(halo, 2, 0) - WARMTH * pltpu.roll(halo, 4, 0))
        change = DIFFUSE * (halo - jnp.where(wet, own, 0.0)) + (carry_by * speed) * halo
        change = change + push_by * jnp.where(wet, total, 0.0)
        if level == 0 and surface is not None:
            change = change + surface
        value = change * tile_at(gain_ref, level) + tile_at(down_ref, level) * value
        put_tile(change_ref, level, value)
    following = zeros()
    for level in range(levels - 1, -1, -1):
        following = tile_at(change_ref, level) + tile_at(up_ref, level) * following
        put_tile(change_ref, level, following)
        finish(level, following)


def first_edge_kernel(levels, lon_total, west_in, east_in, east_own, west_own, packed_ref,
                      gain_ref, down_ref, up_ref, parts_ref, *rest):
    others = rest[:lon_total - 3]
    east_ref, west_ref, full_ref, change_ref, force_ref, depth_ref = rest[lon_total - 3:]
    sub = sublane_ids()
    even = sub % 2 == 0
    half = levels // 2
    extra_w = west_in[pl.ds(half * SUB, EXTRA), :]
    extra_e = east_in[pl.ds(half * SUB, EXTRA), :]
    depth_f = jnp.where(even, spread(extra_e[COUNT_ROW:COUNT_ROW + 1]), spread(extra_w[COUNT_ROW:COUNT_ROW + 1]))
    halo_depth = depth_f.astype(jnp.int32)
    depth_ref[...] = halo_depth
    forcing = [zeros()] * FIELDS
    for tile in [parts_ref[0], extra_w, extra_e] + [other[...] for other in others]:
        mine = sub == spread(tile[SLOT_ROW:SLOT_ROW + 1]).astype(jnp.int32)
        for field in range(FIELDS):
            forcing[field] = forcing[field] + jnp.where(mine, spread(tile[field:field + 1]), 0.0)
    surface = zeros()
    rim = jnp.logical_or(sub == 0, sub == SUB - 1)
    for field in range(FIELDS):
        value = SURFACE_GAIN[field] * forcing[field]
        surface = jnp.where(sub == 2 * field, spread(value[SUB - 1:SUB]), surface)
        surface = jnp.where(sub == 2 * field + 1, spread(value[0:1]), surface)
        put_tile(force_ref, field, jnp.where(rim, 0.0, value))
        put_tile(force_ref, FIELDS + field, value)

    def finish(level, change):
        full = tile_at(packed_ref, level) + change
        put_tile(full_ref, level, full)
        if level < half:
            later = tile_at(full_ref, level + half)
            put_tile(east_ref, level, jnp.where(even, full, pltpu.roll(later, 1, 0)))
            put_tile(west_ref, level, jnp.where(even, pltpu.roll(full, SUB - 1, 0), later))

    edge_change(
        levels,
        lambda level: column_tiles(levels, level, east_in, west_in, even),
        lambda level: column_tiles(levels, level, east_own, west_own, even),
        halo_depth, gain_ref, down_ref, up_ref, surface, change_ref, finish,
    )


def merge_kernel(levels, inner_ref, reply_ref, change_ref, force_ref, out_ref, edge_ref):
    sub = sublane_ids()
    pair = ((lane_ids() + 1) % LANE) // 2
    forces = [tile_at(force_ref, field) for field in range(FIELDS)]

    def group_body(group, carry):
        packed = zeros()
        for inner in range(GROUP):
            level = group * GROUP + inner
            reply = tile_at(reply_ref, level)
            change = tile_at(change_ref, level)
            for field in range(FIELDS):
                j = inner * FIELDS + field
                side = pltpu.roll(change, SUB - 1 - 2 * field, 0)
                rim = jnp.logical_or(sub == 0, sub == SUB - 1)
                value = tile_at(inner_ref, field * levels + level) + jnp.where(rim, side, forces[field] * reply)
                put_tile(out_ref, field * levels + level, value)
                packed = jnp.where(pair == j, pltpu.roll(value, 2 * j, 1) if j else value, packed)
        put_tile(edge_ref, group, packed)
        return carry

    lax.fori_loop(0, levels // GROUP, group_body, 0)


def second_edge_kernel(levels, west_in, east_in, full_ref, packed_ref, gain_ref, down_ref, up_ref, depth_ref,
                       inner_ref, result_ref, change_ref, columns, sems):
    del inner_ref
    even = sublane_ids() % 2 == 0

    def finish(level, change):
        columns[level] = tile_at(packed_ref, level) + change

    edge_change(
        levels,
        lambda level: column_tiles(levels, level, east_in, west_in, even),
        lambda level: tile_at(full_ref, level),
        depth_ref[...], gain_ref, down_ref, up_ref, None, change_ref, finish,
    )
    copies = []
    for field in range(FIELDS):
        for side, column in ((0, SUB - 1), (1, 0)):
            copies.append(pltpu.make_async_copy(
                columns.at[:, 2 * field + side, :],
                result_ref.at[pl.ds(field * levels, levels), column, :],
                sems.at[field, side],
            ))
    for copy in copies:
        copy.start()
    for copy in copies:
        copy.wait()


def in_vmem(value):
    return pltpu.with_memory_space_constraint(value, pltpu.VMEM)


def in_hbm(value):
    return pltpu.with_memory_space_constraint(value, pltpu.HBM)


def call(kernel, outs, args, scratch=(), hbm_in=(), hbm_out=(), aliases=None):
    return pl.pallas_call(
        kernel,
        out_shape=[
            (pltpu.HBM if at in hbm_out else pltpu.VMEM)(shape, dtype)
            for at, (shape, dtype) in enumerate(outs)
        ],
        in_specs=[HBM_SPEC if at in hbm_in else VMEM_SPEC for at in range(len(args))],
        out_specs=[HBM_SPEC if at in hbm_out else VMEM_SPEC for at in range(len(outs))],
        scratch_shapes=list(scratch),
        input_output_aliases=aliases or {},
        compiler_params=pltpu.CompilerParams(vmem_limit_bytes=VMEM_BYTES),
    )(*[in_hbm(arg) if at in hbm_in else in_vmem(arg) for at, arg in enumerate(args)])


def ring_shift(value, axis, amount):
    count = lax.axis_size(axis)
    return lax.ppermute(value, axis, [(i, (i + amount) % count) for i in range(count)])


def pair_swap(value, axis, first):
    count = lax.axis_size(axis)
    pairs = []
    for low in range(first, count, 2):
        high = (low + 1) % count
        pairs += [(low, high), (high, low)]
    return lax.ppermute(value, axis, pairs)


def bind(kernel, *head):
    def bound(*refs):
        return kernel(*head, *refs)

    bound.__name__ = kernel.__name__
    return bound


def local(ocean_state, level_count, mix_rate, atmos_flux, remap_weight, remap_target, remap_slot):
    field_total, levels, lon_dev, lat_dev = ocean_state.shape
    lon_total = lax.axis_size("lon")
    rows = field_total * levels
    groups = levels // GROUP
    f32, i32 = jnp.float32, jnp.int32
    state_shape = ((rows * lon_dev, lat_dev), f32)
    message = ((rows, lat_dev), f32)
    long_message = ((rows + EXTRA, lat_dev), f32)
    table = ((levels * lon_dev, lat_dev), f32)
    dma = pltpu.SemaphoreType.DMA
    merged = pltpu.VMEM((groups, SUB, LANE), f32)
    x = in_vmem(ocean_state.reshape(rows * lon_dev, lat_dev))

    east, west, parts, count = call(
        bind(column_kernel, levels, lon_total),
        [long_message, long_message, ((lon_total, SUB, lat_dev), f32), ((lon_dev, lat_dev), i32)],
        (ocean_state.reshape(rows, lon_dev, lat_dev), level_count, atmos_flux[0], remap_weight[0],
         remap_target, remap_slot),
        scratch=[
            pltpu.VMEM((2, rows, lat_dev), f32),
            pltpu.VMEM(atmos_flux.shape[1:], atmos_flux.dtype),
            pltpu.VMEM(remap_weight.shape[1:], remap_weight.dtype),
            pltpu.SMEM(remap_target.shape, i32),
            pltpu.SMEM(remap_slot.shape, i32),
            dma((7,)),
        ],
        hbm_in=range(6),
    )
    from_west = ring_shift(east, "lon", 1)
    from_east = ring_shift(west, "lon", -1)
    (edge,) = call(bind(edge_kernel, levels), [(((groups + 1) * SUB, lat_dev), f32)], (x, count))
    swap_a = pair_swap(edge, LAT_AXES, 0)
    swap_b = pair_swap(edge, LAT_AXES, 1)
    others = [ring_shift(parts[s], "lon", s) for s in range(2, lon_total - 1)]
    gain, down, up, reply, edge_gain, edge_down, edge_up = call(
        bind(factor_kernel, levels), [table] * 7, (mix_rate.reshape(levels * lon_dev, lat_dev), count)
    )
    inner, packed, depths = call(
        bind(first_kernel, levels),
        [state_shape, table, ((4 * SUB, LANE), i32)],
        (x, count, gain, down, up, swap_a, swap_b),
        scratch=[merged],
    )
    east_next, west_next, full, change, force, halo_depth = call(
        bind(first_edge_kernel, levels, lon_total),
        [message, message, table, table, ((2 * FIELDS * SUB, LANE), f32), ((SUB, LANE), i32)],
        (from_west, from_east, east, west, packed, edge_gain, edge_down, edge_up, parts, *others),
    )
    from_west = ring_shift(east_next, "lon", 1)
    from_east = ring_shift(west_next, "lon", -1)
    state, edge = call(
        bind(merge_kernel, levels),
        [state_shape, ((groups * SUB, lat_dev), f32)],
        (inner, reply, change, force),
    )
    swap_a = pair_swap(edge, LAT_AXES, 0)
    swap_b = pair_swap(edge, LAT_AXES, 1)
    result, packed = call(
        bind(second_kernel, levels),
        [state_shape, table],
        (state, depths, gain, down, up, swap_a, swap_b, force),
        scratch=[merged, pltpu.VMEM(*state_shape), dma((groups, FIELDS))],
        hbm_out=(0,),
    )
    (result,) = call(
        bind(second_edge_kernel, levels),
        [((rows, lon_dev, lat_dev), f32)],
        (from_west, from_east, full, packed, edge_gain, edge_down, edge_up, halo_depth,
         result.reshape(rows, lon_dev, lat_dev)),
        scratch=[pltpu.VMEM(*table), pltpu.VMEM((levels, SUB, LANE), f32), dma((FIELDS, 2))],
        hbm_in=(8,), hbm_out=(0,), aliases={8: 0},
    )
    return result.reshape(ocean_state.shape)


def solution(mesh):
    placed = (
        P(None, None, "lon", LAT_AXES),
        P("lon", LAT_AXES),
        P(None, "lon", LAT_AXES),
        P(LAT_AXES, "lon", None, None),
        P(LAT_AXES, "lon", None, None),
        P(LAT_AXES, "lon"),
        P(LAT_AXES, "lon"),
    )

    return jax.shard_map(
        local,
        mesh=mesh,
        in_specs=placed,
        out_specs=P(None, None, "lon", LAT_AXES),
        check_vma=False,
    )
```

```python
import jax
import jax.numpy as jnp
from jax import lax
from jax.experimental import pallas as pl
from jax.experimental.pallas import tpu as pltpu
from jax.sharding import PartitionSpec as P


DIFFUSE = 0.2
ADVECTION = 0.5
THERMAL = 0.2
HALINE = 0.15
GRAVITY = 0.05
CORIOLIS = 0.3
SURFACE_GAIN = (0.5, 0.4, 0.6, 0.6)

FIELDS = 4
SUB = 8
LANE = 128
PAIRS = LANE // 2
GROUP = PAIRS // FIELDS
EXTRA = 8
SLOT_ROW = 4
COUNT_ROW = 5
LAT_AXES = ("lat", "comp")
QUARTER = 0.5 * ADVECTION
WARMTH = THERMAL / HALINE
PUSH = 0.5 * GRAVITY * HALINE

VMEM_SPEC = pl.BlockSpec(memory_space=pltpu.VMEM)
HBM_SPEC = pl.BlockSpec(memory_space=pltpu.HBM)
VMEM_BYTES = 16 << 20


def sublane_ids():
    return lax.broadcasted_iota(jnp.int32, (SUB, LANE), 0)


def lane_ids():
    return lax.broadcasted_iota(jnp.int32, (SUB, LANE), 1)


def zeros():
    return jnp.zeros((SUB, LANE), jnp.float32)


def spread(row):
    return jnp.broadcast_to(row, (SUB, LANE))


def tile_at(ref, index):
    return ref[pl.ds(pl.multiple_of(index * SUB, SUB), SUB), :]


def put_tile(ref, index, value):
    ref[pl.ds(pl.multiple_of(index * SUB, SUB), SUB), :] = value


def lat_place():
    return lax.axis_index("lat") * lax.axis_size("comp") + lax.axis_index("comp")


def lat_sides(swap_a, swap_b, index):
    place = lat_place()
    total = lax.axis_size("lat") * lax.axis_size("comp")
    tile_a, tile_b = tile_at(swap_a, index), tile_at(swap_b, index)
    evenly = place % 2 == 0
    north = jnp.where(jnp.logical_and(place < total - 1, evenly), tile_a, 0.0)
    north = jnp.where(jnp.logical_and(place < total - 1, jnp.logical_not(evenly)), tile_b, north)
    south = jnp.where(jnp.logical_and(place > 0, evenly), tile_b, 0.0)
    south = jnp.where(jnp.logical_and(place > 0, jnp.logical_not(evenly)), tile_a, south)
    return south, north


def column_tiles(levels, level, east_ref, west_ref, even):
    half = levels // 2
    if level < half:
        return jnp.where(even, tile_at(east_ref, level), pltpu.roll(tile_at(west_ref, level), 1, 0))
    at = level - half
    return jnp.where(even, pltpu.roll(tile_at(east_ref, at), SUB - 1, 0), tile_at(west_ref, at))


def column_kernel(levels, lon_total, x_ref, count_hbm, flux_hbm, weight_hbm, target_hbm, slot_hbm,
                  rate_hbm, east_ref, west_ref, parts_ref, count_ref, rate_ref,
                  columns, flux_ref, weight_ref, target_ref, slot_ref, sems):
    me = lax.axis_index("lon")
    half = levels // 2
    sub = sublane_ids()
    copies = [
        pltpu.make_async_copy(count_hbm, count_ref, sems.at[2]),
        pltpu.make_async_copy(flux_hbm, flux_ref, sems.at[3]),
        pltpu.make_async_copy(weight_hbm, weight_ref, sems.at[4]),
        pltpu.make_async_copy(target_hbm, target_ref, sems.at[5]),
        pltpu.make_async_copy(slot_hbm, slot_ref, sems.at[6]),
    ]
    sides = [
        pltpu.make_async_copy(x_ref.at[:, SUB - 1, :], columns.at[0], sems.at[0]),
        pltpu.make_async_copy(x_ref.at[:, 0, :], columns.at[1], sems.at[1]),
    ]
    later = pltpu.make_async_copy(rate_hbm, rate_ref, sems.at[7])
    for copy in sides + copies + [later]:
        copy.start()
    for copy in copies:
        copy.wait()

    blocks = flux_ref.shape[0]
    for block in range(blocks):
        partial = jnp.dot(flux_ref[block], weight_ref[block], preferred_element_type=jnp.float32)
        slot = slot_ref[0, block].astype(jnp.float32)
        tile = jnp.concatenate([partial, jnp.full((SUB - FIELDS, LANE), slot, jnp.float32)], axis=0)
        shift = lax.rem(target_ref[0, block] - me + lon_total, lon_total)
        parts_ref[shift] = tile

    count = count_ref[...]
    count_f = count.astype(jnp.float32)
    for side, (out_ref, column, shift) in enumerate(
        ((east_ref, SUB - 1, 1), (west_ref, 0, lon_total - 1))
    ):
        sides[side].wait()
        depth = spread(count[column:column + 1, :])
        for field in range(FIELDS):
            for start in range(0, levels, SUB):
                value = columns[side, pl.ds(field * levels + start, SUB), :]
                value = jnp.where(start + sub < depth, value, 0.0)
                upper = start // half
                row = (start - upper * half) * SUB + 2 * field + upper
                out_ref[pl.ds(row, SUB, stride=SUB), :] = value
        out_ref[pl.ds(half * SUB, EXTRA), :] = jnp.where(
            sub == COUNT_ROW, spread(count_f[column:column + 1, :]), parts_ref[shift]
        )
    later.wait()


def prepare_kernel(levels, x_ref, count_ref, rate_ref, edge_ref, gain_ref, down_ref, up_ref, reply_ref,
                   edge_gain_ref, edge_down_ref, edge_up_ref):
    pair = ((lane_ids() + 1) % LANE) // 2
    count = count_ref[...]

    def group_body(group, carry):
        packed = zeros()
        lower, prev, reply = carry
        for inner in range(GROUP):
            level = group * GROUP + inner
            wet = level < count
            for field in range(FIELDS):
                j = inner * FIELDS + field
                value = jnp.where(wet, tile_at(x_ref, field * levels + level), 0.0)
                packed = jnp.where(pair == j, pltpu.roll(value, 2 * j, 1) if j else value, packed)
            upper = jnp.where(level + 1 < count, tile_at(rate_ref, level), 0.0)
            upper = jnp.where(level < levels - 1, upper, 0.0)
            inverse = 1.0 / (1.0 + upper + lower - lower * prev)
            prev = upper * inverse
            gain = jnp.where(wet, inverse, 0.0)
            down = lower * inverse
            reply = jnp.where(level == 0, gain, down * reply)
            put_tile(gain_ref, level, gain)
            put_tile(down_ref, level, down)
            put_tile(up_ref, level, prev)
            put_tile(reply_ref, level, reply)
            lower = upper
        put_tile(edge_ref, group, packed)
        return lower, prev, reply

    lax.fori_loop(0, levels // GROUP, group_body, (zeros(), zeros(), zeros()))
    put_tile(edge_ref, levels // GROUP, count.astype(jnp.float32))

    def back_body(step, following):
        level = levels - 1 - step
        value = tile_at(reply_ref, level) + tile_at(up_ref, level) * following
        put_tile(reply_ref, level, value)
        return value

    lax.fori_loop(0, levels, back_body, zeros(), unroll=16)
    for source_ref, out_ref in ((gain_ref, edge_gain_ref), (down_ref, edge_down_ref), (up_ref, edge_up_ref)):
        pack_edges(levels, 1, source_ref, out_ref)


def pack_edges(levels, fields, source_ref, out_ref):
    for side, column in ((0, SUB - 1), (1, 0)):
        for start in range(0, levels, SUB):
            for field in range(FIELDS):
                if field < fields:
                    row = (field * levels + start) * SUB + column
                    value = source_ref[pl.ds(row, SUB, stride=SUB), :]
                out_ref[pl.ds(start * SUB + 2 * field + side, SUB, stride=SUB), :] = value


def inner_step(levels, first, x_ref, depth, depths, gain_ref, down_ref, up_ref, swap_a, swap_b,
               out_ref, merged_ref, force_ref=None):
    sub = sublane_ids()
    lane = lane_ids()
    even = lane % 2 == 0
    groups = levels // GROUP
    lat_total = LANE * lax.axis_size("lat") * lax.axis_size("comp")
    row_ids = (lat_place() * LANE + lane).astype(jnp.float32)
    rotation = CORIOLIS * (2.0 * (row_ids + 0.5) / lat_total - 1.0)
    depth_e, depth_w, depth_n, depth_s = depths
    for group in range(groups):
        south, north = lat_sides(swap_a, swap_b, group)
        merged_ref[group] = jnp.where(even, north, pltpu.roll(south, 2, 1))

    def forward_level(level, inner, halo, carry):
        sum_e, sum_w, sum_n, sum_s, *prev = carry
        here, east, west, north, south = [], [], [], [], []
        for field in range(FIELDS):
            value = tile_at(x_ref, field * levels + level)
            if first:
                value = jnp.where(level < depth, value, 0.0)
            j = inner * FIELDS + field
            side = pltpu.roll(halo, (LANE - 1 - 2 * j) % LANE, 1)
            here.append(value)
            east.append(jnp.where(sub == SUB - 1, 0.0, pltpu.roll(value, SUB - 1, 0)))
            west.append(jnp.where(sub == 0, 0.0, pltpu.roll(value, 1, 0)))
            north.append(jnp.where(lane == LANE - 1, side, pltpu.roll(value, LANE - 1, 1)))
            south.append(jnp.where(lane == 0, side, pltpu.roll(value, 1, 1)))
        wet_e, wet_w, wet_n, wet_s = level < depth_e, level < depth_w, level < depth_n, level < depth_s
        keep = 1.0 - (
            (jnp.where(wet_e, DIFFUSE, 0.0) + jnp.where(wet_w, DIFFUSE, 0.0))
            + (jnp.where(wet_n, DIFFUSE, 0.0) + jnp.where(wet_s, DIFFUSE, 0.0))
        )
        sum_e = sum_e + (east[1] - WARMTH * east[0])
        sum_w = sum_w + (west[1] - WARMTH * west[0])
        sum_n = sum_n + (north[1] - WARMTH * north[0])
        sum_s = sum_s + (south[1] - WARMTH * south[0])
        force_x = PUSH * (jnp.where(wet_e, sum_e, 0.0) - jnp.where(wet_w, sum_w, 0.0))
        force_y = PUSH * (jnp.where(wet_n, sum_n, 0.0) - jnp.where(wet_s, sum_s, 0.0))
        u, v = here[2], here[3]
        u_part = QUARTER * u
        v_part = QUARTER * v
        gain = tile_at(gain_ref, level)
        down = tile_at(down_ref, level)
        done = []
        for field in range(FIELDS):
            around = (east[field] + west[field]) + (north[field] + south[field])
            value = keep * here[field] + DIFFUSE * around
            if field < 2:
                value = value - (
                    u_part * (east[field] - west[field]) + v_part * (north[field] - south[field])
                )
            elif field == 2:
                value = value + (rotation * v - force_x)
            else:
                value = value - (rotation * u + force_y)
            if inner == 0 and force_ref is not None:
                value = value + jnp.where(level == 0, tile_at(force_ref, FIELDS + field), 0.0)
            value = value * gain + down * prev[field]
            put_tile(out_ref, field * levels + level, value)
            done.append(value)
        return (sum_e, sum_w, sum_n, sum_s, *done)

    def forward_group(group, carry):
        halo = merged_ref[group]
        for inner in range(GROUP):
            carry = forward_level(group * GROUP + inner, inner, halo, carry)
        return carry

    lax.fori_loop(0, groups, forward_group, (zeros(),) * 8)

    def backward_group(step, following):
        group = groups - 1 - step
        for inner in range(GROUP - 1, -1, -1):
            level = group * GROUP + inner
            ratio = tile_at(up_ref, level)
            now = []
            for field in range(FIELDS):
                value = tile_at(out_ref, field * levels + level) + ratio * following[field]
                put_tile(out_ref, field * levels + level, value)
                now.append(value)
            following = tuple(now)
        return following

    lax.fori_loop(0, groups, backward_group, (zeros(),) * FIELDS)


def first_kernel(levels, x_ref, count_ref, gain_ref, down_ref, up_ref, swap_a, swap_b,
                 out_ref, packed_ref, depth_ref, merged_ref):
    sub = sublane_ids()
    lane = lane_ids()
    depth = count_ref[...]
    count_f = depth.astype(jnp.float32)
    side_s, side_n = lat_sides(swap_a, swap_b, levels // GROUP)
    depths = []
    for at, value in enumerate((
        jnp.where(sub == SUB - 1, 0.0, pltpu.roll(count_f, SUB - 1, 0)),
        jnp.where(sub == 0, 0.0, pltpu.roll(count_f, 1, 0)),
        jnp.where(lane == LANE - 1, pltpu.roll(side_n, LANE - 1, 1), pltpu.roll(count_f, LANE - 1, 1)),
        jnp.where(lane == 0, pltpu.roll(side_s, 1, 1), pltpu.roll(count_f, 1, 1)),
    )):
        value = value.astype(jnp.int32)
        put_tile(depth_ref, at, value)
        depths.append(value)
    inner_step(levels, True, x_ref, depth, depths, gain_ref, down_ref, up_ref, swap_a, swap_b,
               out_ref, merged_ref)
    pack_edges(levels, FIELDS, out_ref, packed_ref)


def second_kernel(levels, x_ref, depth_ref, gain_ref, down_ref, up_ref, swap_a, swap_b, force_ref,
                  out_ref, packed_ref, merged_ref):
    depths = [tile_at(depth_ref, at) for at in range(4)]
    inner_step(levels, False, x_ref, None, depths, gain_ref, down_ref, up_ref, swap_a, swap_b,
               out_ref, merged_ref, force_ref)
    pack_edges(levels, FIELDS, out_ref, packed_ref)


def edge_change(levels, halo_at, own_at, halo_depth, gain_ref, down_ref, up_ref, surface, change_ref, finish):
    sub = sublane_ids()
    even = sub % 2 == 0
    field = sub // 2
    sign = jnp.where(even, 1.0, -1.0)
    carry_by = jnp.where(field < 2, -QUARTER * sign, 0.0)
    push_by = jnp.where(field == 2, -PUSH * sign, 0.0)
    total = zeros()
    value = zeros()
    for level in range(levels):
        halo = halo_at(level)
        own = own_at(level)
        wet = level < halo_depth
        speed = jnp.where(field == 0, pltpu.roll(own, 4, 0), pltpu.roll(own, 6, 0))
        total = total + (pltpu.roll(halo, 2, 0) - WARMTH * pltpu.roll(halo, 4, 0))
        change = DIFFUSE * (halo - jnp.where(wet, own, 0.0)) + (carry_by * speed) * halo
        change = change + push_by * jnp.where(wet, total, 0.0)
        if level == 0 and surface is not None:
            change = change + surface
        value = change * tile_at(gain_ref, level) + tile_at(down_ref, level) * value
        put_tile(change_ref, level, value)
    following = zeros()
    for level in range(levels - 1, -1, -1):
        following = tile_at(change_ref, level) + tile_at(up_ref, level) * following
        put_tile(change_ref, level, following)
        finish(level, following)


def first_edge_kernel(levels, lon_total, west_in, east_in, east_own, west_own, packed_ref,
                      gain_ref, down_ref, up_ref, parts_ref, *rest):
    others = rest[:lon_total - 3]
    east_ref, west_ref, full_ref, change_ref, force_ref, depth_ref = rest[lon_total - 3:]
    sub = sublane_ids()
    even = sub % 2 == 0
    half = levels // 2
    extra_w = west_in[pl.ds(half * SUB, EXTRA), :]
    extra_e = east_in[pl.ds(half * SUB, EXTRA), :]
    depth_f = jnp.where(even, spread(extra_e[COUNT_ROW:COUNT_ROW + 1]), spread(extra_w[COUNT_ROW:COUNT_ROW + 1]))
    halo_depth = depth_f.astype(jnp.int32)
    depth_ref[...] = halo_depth
    forcing = [zeros()] * FIELDS
    for tile in [parts_ref[0], extra_w, extra_e] + [other[...] for other in others]:
        mine = sub == spread(tile[SLOT_ROW:SLOT_ROW + 1]).astype(jnp.int32)
        for field in range(FIELDS):
            forcing[field] = forcing[field] + jnp.where(mine, spread(tile[field:field + 1]), 0.0)
    surface = zeros()
    rim = jnp.logical_or(sub == 0, sub == SUB - 1)
    for field in range(FIELDS):
        value = SURFACE_GAIN[field] * forcing[field]
        surface = jnp.where(sub == 2 * field, spread(value[SUB - 1:SUB]), surface)
        surface = jnp.where(sub == 2 * field + 1, spread(value[0:1]), surface)
        put_tile(force_ref, field, jnp.where(rim, 0.0, value))
        put_tile(force_ref, FIELDS + field, value)

    def finish(level, change):
        full = tile_at(packed_ref, level) + change
        put_tile(full_ref, level, full)
        if level < half:
            later = tile_at(full_ref, level + half)
            put_tile(east_ref, level, jnp.where(even, full, pltpu.roll(later, 1, 0)))
            put_tile(west_ref, level, jnp.where(even, pltpu.roll(full, SUB - 1, 0), later))

    edge_change(
        levels,
        lambda level: column_tiles(levels, level, east_in, west_in, even),
        lambda level: column_tiles(levels, level, east_own, west_own, even),
        halo_depth, gain_ref, down_ref, up_ref, surface, change_ref, finish,
    )


def merge_kernel(levels, inner_ref, reply_ref, change_ref, force_ref, out_ref, edge_ref):
    sub = sublane_ids()
    pair = ((lane_ids() + 1) % LANE) // 2
    forces = [tile_at(force_ref, field) for field in range(FIELDS)]

    def group_body(group, carry):
        packed = zeros()
        for inner in range(GROUP):
            level = group * GROUP + inner
            reply = tile_at(reply_ref, level)
            change = tile_at(change_ref, level)
            for field in range(FIELDS):
                j = inner * FIELDS + field
                side = pltpu.roll(change, SUB - 1 - 2 * field, 0)
                rim = jnp.logical_or(sub == 0, sub == SUB - 1)
                value = tile_at(inner_ref, field * levels + level) + jnp.where(rim, side, forces[field] * reply)
                put_tile(out_ref, field * levels + level, value)
                packed = jnp.where(pair == j, pltpu.roll(value, 2 * j, 1) if j else value, packed)
        put_tile(edge_ref, group, packed)
        return carry

    lax.fori_loop(0, levels // GROUP, group_body, 0)


def second_edge_kernel(levels, west_in, east_in, full_ref, packed_ref, gain_ref, down_ref, up_ref, depth_ref,
                       inner_ref, result_ref, state_ref, change_ref, sems):
    even = sublane_ids() % 2 == 0
    sub = sublane_ids()
    copies = []

    def finish(level, change):
        edge = tile_at(packed_ref, level) + change
        for field in range(FIELDS):
            side = pltpu.roll(edge, SUB - 1 - 2 * field, 0)
            rim = jnp.logical_or(sub == 0, sub == SUB - 1)
            row = field * levels + level
            put_tile(state_ref, row, jnp.where(rim, side, tile_at(inner_ref, row)))
        if level % GROUP == 0:
            for field in range(FIELDS):
                piece = pl.ds((field * levels + level) * SUB, GROUP * SUB)
                copy = pltpu.make_async_copy(
                    state_ref.at[piece, :], result_ref.at[piece, :], sems.at[level // GROUP, field]
                )
                copy.start()
                copies.append(copy)

    edge_change(
        levels,
        lambda level: column_tiles(levels, level, east_in, west_in, even),
        lambda level: tile_at(full_ref, level),
        depth_ref[...], gain_ref, down_ref, up_ref, None, change_ref, finish,
    )
    for copy in copies:
        copy.wait()


def in_vmem(value):
    return pltpu.with_memory_space_constraint(value, pltpu.VMEM)


def in_hbm(value):
    return pltpu.with_memory_space_constraint(value, pltpu.HBM)


def call(kernel, outs, args, scratch=(), hbm_in=(), hbm_out=(), aliases=None):
    return pl.pallas_call(
        kernel,
        out_shape=[
            (pltpu.HBM if at in hbm_out else pltpu.VMEM)(shape, dtype)
            for at, (shape, dtype) in enumerate(outs)
        ],
        in_specs=[HBM_SPEC if at in hbm_in else VMEM_SPEC for at in range(len(args))],
        out_specs=[HBM_SPEC if at in hbm_out else VMEM_SPEC for at in range(len(outs))],
        scratch_shapes=list(scratch),
        input_output_aliases=aliases or {},
        compiler_params=pltpu.CompilerParams(vmem_limit_bytes=VMEM_BYTES),
    )(*[in_hbm(arg) if at in hbm_in else in_vmem(arg) for at, arg in enumerate(args)])


def ring_shift(value, axis, amount):
    count = lax.axis_size(axis)
    return lax.ppermute(value, axis, [(i, (i + amount) % count) for i in range(count)])


def pair_swap(value, axis, first):
    count = lax.axis_size(axis)
    pairs = [(at, at) for at in range(first)]
    for low in range(first, count - 1, 2):
        pairs += [(low, low + 1), (low + 1, low)]
    pairs += [(at, at) for at in range(len(pairs), count)]
    return lax.ppermute(value, axis, pairs)


def lat_exchange(edge):
    swap_a = pair_swap(edge, LAT_AXES, 0)
    swap_b = pair_swap(edge, LAT_AXES, 1)
    return swap_a, swap_b


def bind(kernel, *head):
    def bound(*refs):
        return kernel(*head, *refs)

    bound.__name__ = kernel.__name__
    return bound


def local(ocean_state, level_count, mix_rate, atmos_flux, remap_weight, remap_target, remap_slot):
    field_total, levels, lon_dev, lat_dev = ocean_state.shape
    lon_total = lax.axis_size("lon")
    rows = field_total * levels
    groups = levels // GROUP
    f32, i32 = jnp.float32, jnp.int32
    state_shape = ((rows * lon_dev, lat_dev), f32)
    message = ((rows, lat_dev), f32)
    long_message = ((rows + EXTRA, lat_dev), f32)
    table = ((levels * lon_dev, lat_dev), f32)
    dma = pltpu.SemaphoreType.DMA
    merged = pltpu.VMEM((groups, SUB, LANE), f32)
    x = in_vmem(ocean_state.reshape(rows * lon_dev, lat_dev))

    east, west, parts, count, rate = call(
        bind(column_kernel, levels, lon_total),
        [long_message, long_message, ((lon_total, SUB, lat_dev), f32), ((lon_dev, lat_dev), i32), table],
        (ocean_state.reshape(rows, lon_dev, lat_dev), level_count, atmos_flux[0], remap_weight[0],
         remap_target, remap_slot, mix_rate.reshape(levels * lon_dev, lat_dev)),
        scratch=[
            pltpu.VMEM((2, rows, lat_dev), f32),
            pltpu.VMEM(atmos_flux.shape[1:], atmos_flux.dtype),
            pltpu.VMEM(remap_weight.shape[1:], remap_weight.dtype),
            pltpu.SMEM(remap_target.shape, i32),
            pltpu.SMEM(remap_slot.shape, i32),
            dma((8,)),
        ],
        hbm_in=range(7),
    )
    from_west = ring_shift(east, "lon", 1)
    from_east = ring_shift(west, "lon", -1)
    edge, gain, down, up, reply, edge_gain, edge_down, edge_up = call(
        bind(prepare_kernel, levels),
        [(((groups + 1) * SUB, lat_dev), f32)] + [table] * 7,
        (x, count, rate),
    )
    swap_a, swap_b = lat_exchange(edge)
    others = [ring_shift(parts[s], "lon", s) for s in range(2, lon_total - 1)]
    inner, packed, depths = call(
        bind(first_kernel, levels),
        [state_shape, table, ((4 * SUB, LANE), i32)],
        (x, count, gain, down, up, swap_a, swap_b),
        scratch=[merged],
    )
    east_next, west_next, full, change, force, halo_depth = call(
        bind(first_edge_kernel, levels, lon_total),
        [message, message, table, table, ((2 * FIELDS * SUB, LANE), f32), ((SUB, LANE), i32)],
        (from_west, from_east, east, west, packed, edge_gain, edge_down, edge_up, parts, *others),
    )
    from_west = ring_shift(east_next, "lon", 1)
    from_east = ring_shift(west_next, "lon", -1)
    state, edge = call(
        bind(merge_kernel, levels),
        [state_shape, ((groups * SUB, lat_dev), f32)],
        (inner, reply, change, force),
    )
    swap_a, swap_b = lat_exchange(edge)
    inner, packed = call(
        bind(second_kernel, levels),
        [state_shape, table],
        (state, depths, gain, down, up, swap_a, swap_b, force),
        scratch=[merged],
    )
    (result,) = call(
        bind(second_edge_kernel, levels),
        [state_shape],
        (from_west, from_east, full, packed, edge_gain, edge_down, edge_up, halo_depth, inner),
        scratch=[pltpu.VMEM(*state_shape), pltpu.VMEM(*table), dma((groups, FIELDS))],
        hbm_out=(0,),
    )
    return result.reshape(ocean_state.shape)


def solution(mesh):
    placed = (
        P(None, None, "lon", LAT_AXES),
        P("lon", LAT_AXES),
        P(None, "lon", LAT_AXES),
        P(LAT_AXES, "lon", None, None),
        P(LAT_AXES, "lon", None, None),
        P(LAT_AXES, "lon"),
        P(LAT_AXES, "lon"),
    )

    return jax.shard_map(
        local,
        mesh=mesh,
        in_specs=placed,
        out_specs=P(None, None, "lon", LAT_AXES),
        check_vma=False,
    )
```

```python
import jax
import jax.numpy as jnp
from jax import lax
from jax.experimental import pallas as pl
from jax.experimental.pallas import tpu as pltpu
from jax.sharding import PartitionSpec as P


DIFFUSE = 0.2
ADVECTION = 0.5
THERMAL = 0.2
HALINE = 0.15
GRAVITY = 0.05
CORIOLIS = 0.3
SURFACE_GAIN = (0.5, 0.4, 0.6, 0.6)

FIELDS = 4
SUB = 8
LANE = 128
PAIRS = LANE // 2
GROUP = PAIRS // FIELDS
EXTRA = 8
SLOT_ROW = 4
COUNT_ROW = 5
LAT_AXES = ("lat", "comp")
QUARTER = 0.5 * ADVECTION
WARMTH = THERMAL / HALINE
PUSH = 0.5 * GRAVITY * HALINE

VMEM_SPEC = pl.BlockSpec(memory_space=pltpu.VMEM)
HBM_SPEC = pl.BlockSpec(memory_space=pltpu.HBM)
VMEM_BYTES = 16 << 20


def sublane_ids():
    return lax.broadcasted_iota(jnp.int32, (SUB, LANE), 0)


def lane_ids():
    return lax.broadcasted_iota(jnp.int32, (SUB, LANE), 1)


def zeros():
    return jnp.zeros((SUB, LANE), jnp.float32)


def spread(row):
    return jnp.broadcast_to(row, (SUB, LANE))


def tile_at(ref, index):
    return ref[pl.ds(pl.multiple_of(index * SUB, SUB), SUB), :]


def put_tile(ref, index, value):
    ref[pl.ds(pl.multiple_of(index * SUB, SUB), SUB), :] = value


def lat_place():
    return lax.axis_index("lat") * lax.axis_size("comp") + lax.axis_index("comp")


def lat_sides(swap_a, swap_b, index):
    place = lat_place()
    total = lax.axis_size("lat") * lax.axis_size("comp")
    tile_a, tile_b = tile_at(swap_a, index), tile_at(swap_b, index)
    evenly = place % 2 == 0
    north = jnp.where(jnp.logical_and(place < total - 1, evenly), tile_a, 0.0)
    north = jnp.where(jnp.logical_and(place < total - 1, jnp.logical_not(evenly)), tile_b, north)
    south = jnp.where(jnp.logical_and(place > 0, evenly), tile_b, 0.0)
    south = jnp.where(jnp.logical_and(place > 0, jnp.logical_not(evenly)), tile_a, south)
    return south, north


def column_tiles(levels, level, east_ref, west_ref, even):
    half = levels // 2
    if level < half:
        return jnp.where(even, tile_at(east_ref, level), pltpu.roll(tile_at(west_ref, level), 1, 0))
    at = level - half
    return jnp.where(even, pltpu.roll(tile_at(east_ref, at), SUB - 1, 0), tile_at(west_ref, at))


def column_kernel(levels, lon_total, x_ref, count_hbm, flux_hbm, weight_hbm, target_hbm, slot_hbm,
                  rate_hbm, east_ref, west_ref, parts_ref, count_ref, rate_ref,
                  columns, flux_ref, weight_ref, target_ref, slot_ref, sems):
    me = lax.axis_index("lon")
    half = levels // 2
    sub = sublane_ids()
    copies = [
        pltpu.make_async_copy(count_hbm, count_ref, sems.at[2]),
        pltpu.make_async_copy(flux_hbm, flux_ref, sems.at[3]),
        pltpu.make_async_copy(weight_hbm, weight_ref, sems.at[4]),
        pltpu.make_async_copy(target_hbm, target_ref, sems.at[5]),
        pltpu.make_async_copy(slot_hbm, slot_ref, sems.at[6]),
    ]
    sides = [
        pltpu.make_async_copy(x_ref.at[:, SUB - 1, :], columns.at[0], sems.at[0]),
        pltpu.make_async_copy(x_ref.at[:, 0, :], columns.at[1], sems.at[1]),
    ]
    later = pltpu.make_async_copy(rate_hbm, rate_ref, sems.at[7])
    for copy in sides + copies + [later]:
        copy.start()
    for copy in copies:
        copy.wait()

    blocks = flux_ref.shape[0]
    for block in range(blocks):
        partial = jnp.dot(flux_ref[block], weight_ref[block], preferred_element_type=jnp.float32)
        slot = slot_ref[0, block].astype(jnp.float32)
        tile = jnp.concatenate([partial, jnp.full((SUB - FIELDS, LANE), slot, jnp.float32)], axis=0)
        shift = lax.rem(target_ref[0, block] - me + lon_total, lon_total)
        parts_ref[shift] = tile

    count = count_ref[...]
    count_f = count.astype(jnp.float32)
    for side, (out_ref, column, shift) in enumerate(
        ((east_ref, SUB - 1, 1), (west_ref, 0, lon_total - 1))
    ):
        sides[side].wait()
        depth = spread(count[column:column + 1, :])
        for field in range(FIELDS):
            for start in range(0, levels, SUB):
                value = columns[side, pl.ds(field * levels + start, SUB), :]
                value = jnp.where(start + sub < depth, value, 0.0)
                upper = start // half
                row = (start - upper * half) * SUB + 2 * field + upper
                out_ref[pl.ds(row, SUB, stride=SUB), :] = value
        out_ref[pl.ds(half * SUB, EXTRA), :] = jnp.where(
            sub == COUNT_ROW, spread(count_f[column:column + 1, :]), parts_ref[shift]
        )
    later.wait()


def prepare_kernel(levels, x_ref, count_ref, rate_ref, edge_ref, gain_ref, down_ref, up_ref, reply_ref,
                   edge_gain_ref, edge_down_ref, edge_up_ref):
    pair = ((lane_ids() + 1) % LANE) // 2
    count = count_ref[...]

    def group_body(group, carry):
        packed = zeros()
        lower, prev, reply = carry
        for inner in range(GROUP):
            level = group * GROUP + inner
            wet = level < count
            for field in range(FIELDS):
                j = inner * FIELDS + field
                value = jnp.where(wet, tile_at(x_ref, field * levels + level), 0.0)
                packed = jnp.where(pair == j, pltpu.roll(value, 2 * j, 1) if j else value, packed)
            upper = jnp.where(level + 1 < count, tile_at(rate_ref, level), 0.0)
            upper = jnp.where(level < levels - 1, upper, 0.0)
            inverse = 1.0 / (1.0 + upper + lower - lower * prev)
            prev = upper * inverse
            gain = jnp.where(wet, inverse, 0.0)
            down = lower * inverse
            reply = jnp.where(level == 0, gain, down * reply)
            put_tile(gain_ref, level, gain)
            put_tile(down_ref, level, down)
            put_tile(up_ref, level, prev)
            put_tile(reply_ref, level, reply)
            lower = upper
        put_tile(edge_ref, group, packed)
        return lower, prev, reply

    lax.fori_loop(0, levels // GROUP, group_body, (zeros(), zeros(), zeros()))
    put_tile(edge_ref, levels // GROUP, count.astype(jnp.float32))

    def back_body(step, following):
        level = levels - 1 - step
        value = tile_at(reply_ref, level) + tile_at(up_ref, level) * following
        put_tile(reply_ref, level, value)
        return value

    lax.fori_loop(0, levels, back_body, zeros(), unroll=16)
    for source_ref, out_ref in ((gain_ref, edge_gain_ref), (down_ref, edge_down_ref), (up_ref, edge_up_ref)):
        pack_edges(levels, 1, source_ref, out_ref)


def pack_edges(levels, fields, source_ref, out_ref):
    for side, column in ((0, SUB - 1), (1, 0)):
        for start in range(0, levels, SUB):
            for field in range(FIELDS):
                if field < fields:
                    row = (field * levels + start) * SUB + column
                    value = source_ref[pl.ds(row, SUB, stride=SUB), :]
                out_ref[pl.ds(start * SUB + 2 * field + side, SUB, stride=SUB), :] = value


def inner_step(levels, first, x_ref, depth, depths, gain_ref, down_ref, up_ref, swap_a, swap_b,
               out_ref, merged_ref, force_ref=None):
    sub = sublane_ids()
    lane = lane_ids()
    even = lane % 2 == 0
    groups = levels // GROUP
    lat_total = LANE * lax.axis_size("lat") * lax.axis_size("comp")
    row_ids = (lat_place() * LANE + lane).astype(jnp.float32)
    rotation = CORIOLIS * (2.0 * (row_ids + 0.5) / lat_total - 1.0)
    depth_e, depth_w, depth_n, depth_s = depths
    for group in range(groups):
        south, north = lat_sides(swap_a, swap_b, group)
        merged_ref[group] = jnp.where(even, north, pltpu.roll(south, 2, 1))

    def forward_level(level, inner, halo, carry):
        sum_e, sum_w, sum_n, sum_s, *prev = carry
        here, east, west, north, south = [], [], [], [], []
        for field in range(FIELDS):
            value = tile_at(x_ref, field * levels + level)
            if first:
                value = jnp.where(level < depth, value, 0.0)
            j = inner * FIELDS + field
            side = pltpu.roll(halo, (LANE - 1 - 2 * j) % LANE, 1)
            here.append(value)
            east.append(jnp.where(sub == SUB - 1, 0.0, pltpu.roll(value, SUB - 1, 0)))
            west.append(jnp.where(sub == 0, 0.0, pltpu.roll(value, 1, 0)))
            north.append(jnp.where(lane == LANE - 1, side, pltpu.roll(value, LANE - 1, 1)))
            south.append(jnp.where(lane == 0, side, pltpu.roll(value, 1, 1)))
        wet_e, wet_w, wet_n, wet_s = level < depth_e, level < depth_w, level < depth_n, level < depth_s
        keep = 1.0 - (
            (jnp.where(wet_e, DIFFUSE, 0.0) + jnp.where(wet_w, DIFFUSE, 0.0))
            + (jnp.where(wet_n, DIFFUSE, 0.0) + jnp.where(wet_s, DIFFUSE, 0.0))
        )
        sum_e = sum_e + (east[1] - WARMTH * east[0])
        sum_w = sum_w + (west[1] - WARMTH * west[0])
        sum_n = sum_n + (north[1] - WARMTH * north[0])
        sum_s = sum_s + (south[1] - WARMTH * south[0])
        force_x = PUSH * (jnp.where(wet_e, sum_e, 0.0) - jnp.where(wet_w, sum_w, 0.0))
        force_y = PUSH * (jnp.where(wet_n, sum_n, 0.0) - jnp.where(wet_s, sum_s, 0.0))
        u, v = here[2], here[3]
        u_part = QUARTER * u
        v_part = QUARTER * v
        gain = tile_at(gain_ref, level)
        down = tile_at(down_ref, level)
        done = []
        for field in range(FIELDS):
            around = (east[field] + west[field]) + (north[field] + south[field])
            value = keep * here[field] + DIFFUSE * around
            if field < 2:
                value = value - (
                    u_part * (east[field] - west[field]) + v_part * (north[field] - south[field])
                )
            elif field == 2:
                value = value + (rotation * v - force_x)
            else:
                value = value - (rotation * u + force_y)
            if inner == 0 and force_ref is not None:
                value = value + jnp.where(level == 0, tile_at(force_ref, FIELDS + field), 0.0)
            value = value * gain + down * prev[field]
            put_tile(out_ref, field * levels + level, value)
            done.append(value)
        return (sum_e, sum_w, sum_n, sum_s, *done)

    def forward_group(group, carry):
        halo = merged_ref[group]
        for inner in range(GROUP):
            carry = forward_level(group * GROUP + inner, inner, halo, carry)
        return carry

    lax.fori_loop(0, groups, forward_group, (zeros(),) * 8)

    def backward_group(step, following):
        group = groups - 1 - step
        for inner in range(GROUP - 1, -1, -1):
            level = group * GROUP + inner
            ratio = tile_at(up_ref, level)
            now = []
            for field in range(FIELDS):
                value = tile_at(out_ref, field * levels + level) + ratio * following[field]
                put_tile(out_ref, field * levels + level, value)
                now.append(value)
            following = tuple(now)
        return following

    lax.fori_loop(0, groups, backward_group, (zeros(),) * FIELDS)


def first_kernel(levels, x_ref, count_ref, gain_ref, down_ref, up_ref, swap_a, swap_b,
                 out_ref, packed_ref, depth_ref, merged_ref):
    sub = sublane_ids()
    lane = lane_ids()
    depth = count_ref[...]
    count_f = depth.astype(jnp.float32)
    side_s, side_n = lat_sides(swap_a, swap_b, levels // GROUP)
    depths = []
    for at, value in enumerate((
        jnp.where(sub == SUB - 1, 0.0, pltpu.roll(count_f, SUB - 1, 0)),
        jnp.where(sub == 0, 0.0, pltpu.roll(count_f, 1, 0)),
        jnp.where(lane == LANE - 1, pltpu.roll(side_n, LANE - 1, 1), pltpu.roll(count_f, LANE - 1, 1)),
        jnp.where(lane == 0, pltpu.roll(side_s, 1, 1), pltpu.roll(count_f, 1, 1)),
    )):
        value = value.astype(jnp.int32)
        put_tile(depth_ref, at, value)
        depths.append(value)
    inner_step(levels, True, x_ref, depth, depths, gain_ref, down_ref, up_ref, swap_a, swap_b,
               out_ref, merged_ref)
    pack_edges(levels, FIELDS, out_ref, packed_ref)


def second_kernel(levels, x_ref, depth_ref, gain_ref, down_ref, up_ref, swap_a, swap_b, force_ref,
                  out_ref, packed_ref, merged_ref):
    depths = [tile_at(depth_ref, at) for at in range(4)]
    inner_step(levels, False, x_ref, None, depths, gain_ref, down_ref, up_ref, swap_a, swap_b,
               out_ref, merged_ref, force_ref)
    pack_edges(levels, FIELDS, out_ref, packed_ref)


def edge_change(levels, halo_at, own_at, halo_depth, gain_ref, down_ref, up_ref, surface, change_ref, finish):
    sub = sublane_ids()
    even = sub % 2 == 0
    field = sub // 2
    sign = jnp.where(even, 1.0, -1.0)
    carry_by = jnp.where(field < 2, -QUARTER * sign, 0.0)
    push_by = jnp.where(field == 2, -PUSH * sign, 0.0)
    total = zeros()
    value = zeros()
    for level in range(levels):
        halo = halo_at(level)
        own = own_at(level)
        wet = level < halo_depth
        speed = jnp.where(field == 0, pltpu.roll(own, 4, 0), pltpu.roll(own, 6, 0))
        total = total + (pltpu.roll(halo, 2, 0) - WARMTH * pltpu.roll(halo, 4, 0))
        change = DIFFUSE * (halo - jnp.where(wet, own, 0.0)) + (carry_by * speed) * halo
        change = change + push_by * jnp.where(wet, total, 0.0)
        if level == 0 and surface is not None:
            change = change + surface
        value = change * tile_at(gain_ref, level) + tile_at(down_ref, level) * value
        put_tile(change_ref, level, value)
    following = zeros()
    for level in range(levels - 1, -1, -1):
        following = tile_at(change_ref, level) + tile_at(up_ref, level) * following
        put_tile(change_ref, level, following)
        finish(level, following)


def first_edge_kernel(levels, lon_total, west_in, east_in, east_own, west_own, packed_ref,
                      gain_ref, down_ref, up_ref, parts_ref, *rest):
    others = rest[:lon_total - 3]
    east_ref, west_ref, full_ref, change_ref, force_ref, depth_ref = rest[lon_total - 3:]
    sub = sublane_ids()
    even = sub % 2 == 0
    half = levels // 2
    extra_w = west_in[pl.ds(half * SUB, EXTRA), :]
    extra_e = east_in[pl.ds(half * SUB, EXTRA), :]
    depth_f = jnp.where(even, spread(extra_e[COUNT_ROW:COUNT_ROW + 1]), spread(extra_w[COUNT_ROW:COUNT_ROW + 1]))
    halo_depth = depth_f.astype(jnp.int32)
    depth_ref[...] = halo_depth
    forcing = [zeros()] * FIELDS
    for tile in [parts_ref[0], extra_w, extra_e] + [other[...] for other in others]:
        mine = sub == spread(tile[SLOT_ROW:SLOT_ROW + 1]).astype(jnp.int32)
        for field in range(FIELDS):
            forcing[field] = forcing[field] + jnp.where(mine, spread(tile[field:field + 1]), 0.0)
    surface = zeros()
    rim = jnp.logical_or(sub == 0, sub == SUB - 1)
    for field in range(FIELDS):
        value = SURFACE_GAIN[field] * forcing[field]
        surface = jnp.where(sub == 2 * field, spread(value[SUB - 1:SUB]), surface)
        surface = jnp.where(sub == 2 * field + 1, spread(value[0:1]), surface)
        put_tile(force_ref, field, jnp.where(rim, 0.0, value))
        put_tile(force_ref, FIELDS + field, value)

    def finish(level, change):
        full = tile_at(packed_ref, level) + change
        put_tile(full_ref, level, full)
        if level < half:
            later = tile_at(full_ref, level + half)
            put_tile(east_ref, level, jnp.where(even, full, pltpu.roll(later, 1, 0)))
            put_tile(west_ref, level, jnp.where(even, pltpu.roll(full, SUB - 1, 0), later))

    edge_change(
        levels,
        lambda level: column_tiles(levels, level, east_in, west_in, even),
        lambda level: column_tiles(levels, level, east_own, west_own, even),
        halo_depth, gain_ref, down_ref, up_ref, surface, change_ref, finish,
    )


def merge_kernel(levels, inner_ref, reply_ref, change_ref, force_ref, out_ref, edge_ref):
    sub = sublane_ids()
    pair = ((lane_ids() + 1) % LANE) // 2
    forces = [tile_at(force_ref, field) for field in range(FIELDS)]

    def group_body(group, carry):
        packed = zeros()
        for inner in range(GROUP):
            level = group * GROUP + inner
            reply = tile_at(reply_ref, level)
            change = tile_at(change_ref, level)
            for field in range(FIELDS):
                j = inner * FIELDS + field
                side = pltpu.roll(change, SUB - 1 - 2 * field, 0)
                rim = jnp.logical_or(sub == 0, sub == SUB - 1)
                value = tile_at(inner_ref, field * levels + level) + jnp.where(rim, side, forces[field] * reply)
                put_tile(out_ref, field * levels + level, value)
                packed = jnp.where(pair == j, pltpu.roll(value, 2 * j, 1) if j else value, packed)
        put_tile(edge_ref, group, packed)
        return carry

    lax.fori_loop(0, levels // GROUP, group_body, 0)


def second_edge_kernel(levels, west_in, east_in, full_ref, packed_ref, gain_ref, down_ref, up_ref, depth_ref,
                       inner_ref, result_ref, state_ref, change_ref, sems):
    even = sublane_ids() % 2 == 0
    sub = sublane_ids()
    copies = []

    def finish(level, change):
        edge = tile_at(packed_ref, level) + change
        for field in range(FIELDS):
            side = pltpu.roll(edge, SUB - 1 - 2 * field, 0)
            rim = jnp.logical_or(sub == 0, sub == SUB - 1)
            row = field * levels + level
            put_tile(state_ref, row, jnp.where(rim, side, tile_at(inner_ref, row)))
        if level % GROUP == 0:
            for field in range(FIELDS):
                piece = pl.ds((field * levels + level) * SUB, GROUP * SUB)
                copy = pltpu.make_async_copy(
                    state_ref.at[piece, :], result_ref.at[piece, :], sems.at[level // GROUP, field]
                )
                copy.start()
                copies.append(copy)

    edge_change(
        levels,
        lambda level: column_tiles(levels, level, east_in, west_in, even),
        lambda level: tile_at(full_ref, level),
        depth_ref[...], gain_ref, down_ref, up_ref, None, change_ref, finish,
    )
    for copy in copies:
        copy.wait()


def in_vmem(value):
    return pltpu.with_memory_space_constraint(value, pltpu.VMEM)


def in_hbm(value):
    return pltpu.with_memory_space_constraint(value, pltpu.HBM)


def call(kernel, outs, args, scratch=(), hbm_in=(), hbm_out=(), aliases=None):
    return pl.pallas_call(
        kernel,
        out_shape=[
            (pltpu.HBM if at in hbm_out else pltpu.VMEM)(shape, dtype)
            for at, (shape, dtype) in enumerate(outs)
        ],
        in_specs=[HBM_SPEC if at in hbm_in else VMEM_SPEC for at in range(len(args))],
        out_specs=[HBM_SPEC if at in hbm_out else VMEM_SPEC for at in range(len(outs))],
        scratch_shapes=list(scratch),
        input_output_aliases=aliases or {},
        compiler_params=pltpu.CompilerParams(vmem_limit_bytes=VMEM_BYTES),
    )(*[in_hbm(arg) if at in hbm_in else in_vmem(arg) for at, arg in enumerate(args)])


def ring_shift(value, axis, amount):
    count = lax.axis_size(axis)
    return lax.ppermute(value, axis, [(i, (i + amount) % count) for i in range(count)])


def pair_swap(value, axis, first):
    count = lax.axis_size(axis)
    pairs = []
    for low in range(first, count, 2):
        high = (low + 1) % count
        pairs += [(low, high), (high, low)]
    return lax.ppermute(value, axis, pairs)


def lat_exchange(edge):
    swap_a = pair_swap(edge, LAT_AXES, 0)
    swap_b = pair_swap(edge, LAT_AXES, 1)
    return swap_a, swap_b


def bind(kernel, *head):
    def bound(*refs):
        return kernel(*head, *refs)

    bound.__name__ = kernel.__name__
    return bound


def local(ocean_state, level_count, mix_rate, atmos_flux, remap_weight, remap_target, remap_slot):
    field_total, levels, lon_dev, lat_dev = ocean_state.shape
    lon_total = lax.axis_size("lon")
    rows = field_total * levels
    groups = levels // GROUP
    f32, i32 = jnp.float32, jnp.int32
    state_shape = ((rows * lon_dev, lat_dev), f32)
    message = ((rows, lat_dev), f32)
    long_message = ((rows + EXTRA, lat_dev), f32)
    table = ((levels * lon_dev, lat_dev), f32)
    dma = pltpu.SemaphoreType.DMA
    merged = pltpu.VMEM((groups, SUB, LANE), f32)
    x = in_vmem(ocean_state.reshape(rows * lon_dev, lat_dev))

    east, west, parts, count, rate = call(
        bind(column_kernel, levels, lon_total),
        [long_message, long_message, ((lon_total, SUB, lat_dev), f32), ((lon_dev, lat_dev), i32), table],
        (ocean_state.reshape(rows, lon_dev, lat_dev), level_count, atmos_flux[0], remap_weight[0],
         remap_target, remap_slot, mix_rate.reshape(levels * lon_dev, lat_dev)),
        scratch=[
            pltpu.VMEM((2, rows, lat_dev), f32),
            pltpu.VMEM(atmos_flux.shape[1:], atmos_flux.dtype),
            pltpu.VMEM(remap_weight.shape[1:], remap_weight.dtype),
            pltpu.SMEM(remap_target.shape, i32),
            pltpu.SMEM(remap_slot.shape, i32),
            dma((8,)),
        ],
        hbm_in=range(7),
    )
    from_west = ring_shift(east, "lon", 1)
    from_east = ring_shift(west, "lon", -1)
    edge, gain, down, up, reply, edge_gain, edge_down, edge_up = call(
        bind(prepare_kernel, levels),
        [(((groups + 1) * SUB, lat_dev), f32)] + [table] * 7,
        (x, count, rate),
    )
    swap_a, swap_b = lat_exchange(edge)
    others = [ring_shift(parts[s], "lon", s) for s in range(2, lon_total - 1)]
    inner, packed, depths = call(
        bind(first_kernel, levels),
        [state_shape, table, ((4 * SUB, LANE), i32)],
        (x, count, gain, down, up, swap_a, swap_b),
        scratch=[merged],
    )
    east_next, west_next, full, change, force, halo_depth = call(
        bind(first_edge_kernel, levels, lon_total),
        [message, message, table, table, ((2 * FIELDS * SUB, LANE), f32), ((SUB, LANE), i32)],
        (from_west, from_east, east, west, packed, edge_gain, edge_down, edge_up, parts, *others),
    )
    from_west = ring_shift(east_next, "lon", 1)
    from_east = ring_shift(west_next, "lon", -1)
    state, edge = call(
        bind(merge_kernel, levels),
        [state_shape, ((groups * SUB, lat_dev), f32)],
        (inner, reply, change, force),
    )
    swap_a, swap_b = lat_exchange(edge)
    inner, packed = call(
        bind(second_kernel, levels),
        [state_shape, table],
        (state, depths, gain, down, up, swap_a, swap_b, force),
        scratch=[merged],
    )
    (result,) = call(
        bind(second_edge_kernel, levels),
        [state_shape],
        (from_west, from_east, full, packed, edge_gain, edge_down, edge_up, halo_depth, inner),
        scratch=[pltpu.VMEM(*state_shape), pltpu.VMEM(*table), dma((groups, FIELDS))],
        hbm_out=(0,),
    )
    return result.reshape(ocean_state.shape)


def solution(mesh):
    placed = (
        P(None, None, "lon", LAT_AXES),
        P("lon", LAT_AXES),
        P(None, "lon", LAT_AXES),
        P(LAT_AXES, "lon", None, None),
        P(LAT_AXES, "lon", None, None),
        P(LAT_AXES, "lon"),
        P(LAT_AXES, "lon"),
    )

    return jax.shard_map(
        local,
        mesh=mesh,
        in_specs=placed,
        out_specs=P(None, None, "lon", LAT_AXES),
        check_vma=False,
    )
```

```python
import jax
import jax.numpy as jnp
from jax import lax
from jax.experimental import pallas as pl
from jax.experimental.pallas import tpu as pltpu
from jax.sharding import PartitionSpec as P


DIFFUSE = 0.2
ADVECTION = 0.5
THERMAL = 0.2
HALINE = 0.15
GRAVITY = 0.05
CORIOLIS = 0.3
SURFACE_GAIN = (0.5, 0.4, 0.6, 0.6)

FIELDS = 4
SUB = 8
LANE = 128
PAIRS = LANE // 2
GROUP = PAIRS // FIELDS
EXTRA = 8
SLOT_ROW = 4
COUNT_ROW = 5
LAT_AXES = ("lat", "comp")
QUARTER = 0.5 * ADVECTION
WARMTH = THERMAL / HALINE
PUSH = 0.5 * GRAVITY * HALINE

VMEM_SPEC = pl.BlockSpec(memory_space=pltpu.VMEM)
HBM_SPEC = pl.BlockSpec(memory_space=pltpu.HBM)
VMEM_BYTES = 16 << 20


def sublane_ids():
    return lax.broadcasted_iota(jnp.int32, (SUB, LANE), 0)


def lane_ids():
    return lax.broadcasted_iota(jnp.int32, (SUB, LANE), 1)


def zeros():
    return jnp.zeros((SUB, LANE), jnp.float32)


def spread(row):
    return jnp.broadcast_to(row, (SUB, LANE))


def tile_at(ref, index):
    return ref[pl.ds(pl.multiple_of(index * SUB, SUB), SUB), :]


def put_tile(ref, index, value):
    ref[pl.ds(pl.multiple_of(index * SUB, SUB), SUB), :] = value


def lat_place():
    return lax.axis_index("lat") * lax.axis_size("comp") + lax.axis_index("comp")


def lat_sides(swap_a, swap_b, index):
    place = lat_place()
    total = lax.axis_size("lat") * lax.axis_size("comp")
    tile_a, tile_b = tile_at(swap_a, index), tile_at(swap_b, index)
    evenly = place % 2 == 0
    north = jnp.where(jnp.logical_and(place < total - 1, evenly), tile_a, 0.0)
    north = jnp.where(jnp.logical_and(place < total - 1, jnp.logical_not(evenly)), tile_b, north)
    south = jnp.where(jnp.logical_and(place > 0, evenly), tile_b, 0.0)
    south = jnp.where(jnp.logical_and(place > 0, jnp.logical_not(evenly)), tile_a, south)
    return south, north


def column_tiles(levels, level, east_ref, west_ref, even):
    half = levels // 2
    if level < half:
        return jnp.where(even, tile_at(east_ref, level), pltpu.roll(tile_at(west_ref, level), 1, 0))
    at = level - half
    return jnp.where(even, pltpu.roll(tile_at(east_ref, at), SUB - 1, 0), tile_at(west_ref, at))


def column_kernel(levels, lon_total, x_ref, count_hbm, flux_hbm, weight_hbm, target_hbm, slot_hbm,
                  rate_hbm, east_ref, west_ref, parts_ref, count_ref, rate_ref,
                  columns, flux_ref, weight_ref, target_ref, slot_ref, sems):
    me = lax.axis_index("lon")
    half = levels // 2
    sub = sublane_ids()
    copies = [
        pltpu.make_async_copy(count_hbm, count_ref, sems.at[2]),
        pltpu.make_async_copy(flux_hbm, flux_ref, sems.at[3]),
        pltpu.make_async_copy(weight_hbm, weight_ref, sems.at[4]),
        pltpu.make_async_copy(target_hbm, target_ref, sems.at[5]),
        pltpu.make_async_copy(slot_hbm, slot_ref, sems.at[6]),
    ]
    sides = [
        pltpu.make_async_copy(x_ref.at[:, SUB - 1, :], columns.at[0], sems.at[0]),
        pltpu.make_async_copy(x_ref.at[:, 0, :], columns.at[1], sems.at[1]),
    ]
    later = pltpu.make_async_copy(rate_hbm, rate_ref, sems.at[7])
    for copy in sides + copies + [later]:
        copy.start()
    for copy in copies:
        copy.wait()

    blocks = flux_ref.shape[0]
    for block in range(blocks):
        partial = jnp.dot(flux_ref[block], weight_ref[block], preferred_element_type=jnp.float32)
        slot = slot_ref[0, block].astype(jnp.float32)
        tile = jnp.concatenate([partial, jnp.full((SUB - FIELDS, LANE), slot, jnp.float32)], axis=0)
        shift = lax.rem(target_ref[0, block] - me + lon_total, lon_total)
        parts_ref[shift] = tile

    count = count_ref[...]
    count_f = count.astype(jnp.float32)
    for side, (out_ref, column, shift) in enumerate(
        ((east_ref, SUB - 1, 1), (west_ref, 0, lon_total - 1))
    ):
        sides[side].wait()
        depth = spread(count[column:column + 1, :])
        for field in range(FIELDS):
            for start in range(0, levels, SUB):
                value = columns[side, pl.ds(field * levels + start, SUB), :]
                value = jnp.where(start + sub < depth, value, 0.0)
                upper = start // half
                row = (start - upper * half) * SUB + 2 * field + upper
                out_ref[pl.ds(row, SUB, stride=SUB), :] = value
        out_ref[pl.ds(half * SUB, EXTRA), :] = jnp.where(
            sub == COUNT_ROW, spread(count_f[column:column + 1, :]), parts_ref[shift]
        )
    later.wait()


def prepare_kernel(levels, x_ref, count_ref, rate_ref, edge_ref, gain_ref, down_ref, up_ref, reply_ref,
                   edge_gain_ref, edge_down_ref, edge_up_ref):
    pair = ((lane_ids() + 1) % LANE) // 2
    count = count_ref[...]

    def group_body(group, carry):
        packed = zeros()
        lower, prev, reply = carry
        for inner in range(GROUP):
            level = group * GROUP + inner
            wet = level < count
            for field in range(FIELDS):
                j = inner * FIELDS + field
                value = jnp.where(wet, tile_at(x_ref, field * levels + level), 0.0)
                packed = jnp.where(pair == j, pltpu.roll(value, 2 * j, 1) if j else value, packed)
            upper = jnp.where(level + 1 < count, tile_at(rate_ref, level), 0.0)
            upper = jnp.where(level < levels - 1, upper, 0.0)
            inverse = 1.0 / (1.0 + upper + lower - lower * prev)
            prev = upper * inverse
            gain = jnp.where(wet, inverse, 0.0)
            down = lower * inverse
            reply = jnp.where(level == 0, gain, down * reply)
            put_tile(gain_ref, level, gain)
            put_tile(down_ref, level, down)
            put_tile(up_ref, level, prev)
            put_tile(reply_ref, level, reply)
            lower = upper
        put_tile(edge_ref, group, packed)
        return lower, prev, reply

    lax.fori_loop(0, levels // GROUP, group_body, (zeros(), zeros(), zeros()))
    put_tile(edge_ref, levels // GROUP, count.astype(jnp.float32))

    def back_body(step, following):
        level = levels - 1 - step
        value = tile_at(reply_ref, level) + tile_at(up_ref, level) * following
        put_tile(reply_ref, level, value)
        return value

    lax.fori_loop(0, levels, back_body, zeros(), unroll=16)
    for source_ref, out_ref in ((gain_ref, edge_gain_ref), (down_ref, edge_down_ref), (up_ref, edge_up_ref)):
        pack_edges(levels, 1, source_ref, out_ref)


def pack_edges(levels, fields, source_ref, out_ref):
    for side, column in ((0, SUB - 1), (1, 0)):
        for start in range(0, levels, SUB):
            for field in range(FIELDS):
                if field < fields:
                    row = (field * levels + start) * SUB + column
                    value = source_ref[pl.ds(row, SUB, stride=SUB), :]
                out_ref[pl.ds(start * SUB + 2 * field + side, SUB, stride=SUB), :] = value


def inner_step(levels, first, x_ref, depth, depths, gain_ref, down_ref, up_ref, swap_a, swap_b,
               out_ref, merged_ref, force_ref=None):
    sub = sublane_ids()
    lane = lane_ids()
    even = lane % 2 == 0
    groups = levels // GROUP
    lat_total = LANE * lax.axis_size("lat") * lax.axis_size("comp")
    row_ids = (lat_place() * LANE + lane).astype(jnp.float32)
    rotation = CORIOLIS * (2.0 * (row_ids + 0.5) / lat_total - 1.0)
    depth_e, depth_w, depth_n, depth_s = depths
    for group in range(groups):
        south, north = lat_sides(swap_a, swap_b, group)
        merged_ref[group] = jnp.where(even, north, pltpu.roll(south, 2, 1))

    def forward_level(level, inner, halo, carry):
        sum_e, sum_w, sum_n, sum_s, *prev = carry
        here, east, west, north, south = [], [], [], [], []
        for field in range(FIELDS):
            value = tile_at(x_ref, field * levels + level)
            if first:
                value = jnp.where(level < depth, value, 0.0)
            j = inner * FIELDS + field
            side = pltpu.roll(halo, (LANE - 1 - 2 * j) % LANE, 1)
            here.append(value)
            east.append(jnp.where(sub == SUB - 1, 0.0, pltpu.roll(value, SUB - 1, 0)))
            west.append(jnp.where(sub == 0, 0.0, pltpu.roll(value, 1, 0)))
            north.append(jnp.where(lane == LANE - 1, side, pltpu.roll(value, LANE - 1, 1)))
            south.append(jnp.where(lane == 0, side, pltpu.roll(value, 1, 1)))
        wet_e, wet_w, wet_n, wet_s = level < depth_e, level < depth_w, level < depth_n, level < depth_s
        keep = 1.0 - (
            (jnp.where(wet_e, DIFFUSE, 0.0) + jnp.where(wet_w, DIFFUSE, 0.0))
            + (jnp.where(wet_n, DIFFUSE, 0.0) + jnp.where(wet_s, DIFFUSE, 0.0))
        )
        sum_e = sum_e + (east[1] - WARMTH * east[0])
        sum_w = sum_w + (west[1] - WARMTH * west[0])
        sum_n = sum_n + (north[1] - WARMTH * north[0])
        sum_s = sum_s + (south[1] - WARMTH * south[0])
        force_x = PUSH * (jnp.where(wet_e, sum_e, 0.0) - jnp.where(wet_w, sum_w, 0.0))
        force_y = PUSH * (jnp.where(wet_n, sum_n, 0.0) - jnp.where(wet_s, sum_s, 0.0))
        u, v = here[2], here[3]
        u_part = QUARTER * u
        v_part = QUARTER * v
        gain = tile_at(gain_ref, level)
        down = tile_at(down_ref, level)
        done = []
        for field in range(FIELDS):
            around = (east[field] + west[field]) + (north[field] + south[field])
            value = keep * here[field] + DIFFUSE * around
            if field < 2:
                value = value - (
                    u_part * (east[field] - west[field]) + v_part * (north[field] - south[field])
                )
            elif field == 2:
                value = value + (rotation * v - force_x)
            else:
                value = value - (rotation * u + force_y)
            if inner == 0 and force_ref is not None:
                value = value + jnp.where(level == 0, tile_at(force_ref, FIELDS + field), 0.0)
            value = value * gain + down * prev[field]
            put_tile(out_ref, field * levels + level, value)
            done.append(value)
        return (sum_e, sum_w, sum_n, sum_s, *done)

    def forward_group(group, carry):
        halo = merged_ref[group]
        for inner in range(GROUP):
            carry = forward_level(group * GROUP + inner, inner, halo, carry)
        return carry

    lax.fori_loop(0, groups, forward_group, (zeros(),) * 8)

    def backward_group(step, following):
        group = groups - 1 - step
        for inner in range(GROUP - 1, -1, -1):
            level = group * GROUP + inner
            ratio = tile_at(up_ref, level)
            now = []
            for field in range(FIELDS):
                value = tile_at(out_ref, field * levels + level) + ratio * following[field]
                put_tile(out_ref, field * levels + level, value)
                now.append(value)
            following = tuple(now)
        return following

    lax.fori_loop(0, groups, backward_group, (zeros(),) * FIELDS)


def first_kernel(levels, x_ref, count_ref, gain_ref, down_ref, up_ref, swap_a, swap_b,
                 out_ref, packed_ref, depth_ref, merged_ref):
    sub = sublane_ids()
    lane = lane_ids()
    depth = count_ref[...]
    count_f = depth.astype(jnp.float32)
    side_s, side_n = lat_sides(swap_a, swap_b, levels // GROUP)
    depths = []
    for at, value in enumerate((
        jnp.where(sub == SUB - 1, 0.0, pltpu.roll(count_f, SUB - 1, 0)),
        jnp.where(sub == 0, 0.0, pltpu.roll(count_f, 1, 0)),
        jnp.where(lane == LANE - 1, pltpu.roll(side_n, LANE - 1, 1), pltpu.roll(count_f, LANE - 1, 1)),
        jnp.where(lane == 0, pltpu.roll(side_s, 1, 1), pltpu.roll(count_f, 1, 1)),
    )):
        value = value.astype(jnp.int32)
        put_tile(depth_ref, at, value)
        depths.append(value)
    inner_step(levels, True, x_ref, depth, depths, gain_ref, down_ref, up_ref, swap_a, swap_b,
               out_ref, merged_ref)
    pack_edges(levels, FIELDS, out_ref, packed_ref)


def second_kernel(levels, x_ref, depth_ref, gain_ref, down_ref, up_ref, swap_a, swap_b, force_ref,
                  out_ref, packed_ref, merged_ref):
    depths = [tile_at(depth_ref, at) for at in range(4)]
    inner_step(levels, False, x_ref, None, depths, gain_ref, down_ref, up_ref, swap_a, swap_b,
               out_ref, merged_ref, force_ref)
    pack_edges(levels, FIELDS, out_ref, packed_ref)


def edge_change(levels, halo_at, own_at, halo_depth, gain_ref, down_ref, up_ref, surface, change_ref, finish):
    sub = sublane_ids()
    even = sub % 2 == 0
    field = sub // 2
    sign = jnp.where(even, 1.0, -1.0)
    carry_by = jnp.where(field < 2, -QUARTER * sign, 0.0)
    push_by = jnp.where(field == 2, -PUSH * sign, 0.0)
    total = zeros()
    value = zeros()
    for level in range(levels):
        halo = halo_at(level)
        own = own_at(level)
        wet = level < halo_depth
        speed = jnp.where(field == 0, pltpu.roll(own, 4, 0), pltpu.roll(own, 6, 0))
        total = total + (pltpu.roll(halo, 2, 0) - WARMTH * pltpu.roll(halo, 4, 0))
        change = DIFFUSE * (halo - jnp.where(wet, own, 0.0)) + (carry_by * speed) * halo
        change = change + push_by * jnp.where(wet, total, 0.0)
        if level == 0 and surface is not None:
            change = change + surface
        value = change * tile_at(gain_ref, level) + tile_at(down_ref, level) * value
        put_tile(change_ref, level, value)
    following = zeros()
    for level in range(levels - 1, -1, -1):
        following = tile_at(change_ref, level) + tile_at(up_ref, level) * following
        put_tile(change_ref, level, following)
        finish(level, following)


def first_edge_kernel(levels, lon_total, west_in, east_in, east_own, west_own, packed_ref,
                      gain_ref, down_ref, up_ref, parts_ref, *rest):
    others = rest[:lon_total - 3]
    east_ref, west_ref, full_ref, change_ref, force_ref, depth_ref = rest[lon_total - 3:]
    sub = sublane_ids()
    even = sub % 2 == 0
    half = levels // 2
    extra_w = west_in[pl.ds(half * SUB, EXTRA), :]
    extra_e = east_in[pl.ds(half * SUB, EXTRA), :]
    depth_f = jnp.where(even, spread(extra_e[COUNT_ROW:COUNT_ROW + 1]), spread(extra_w[COUNT_ROW:COUNT_ROW + 1]))
    halo_depth = depth_f.astype(jnp.int32)
    depth_ref[...] = halo_depth
    forcing = [zeros()] * FIELDS
    for tile in [parts_ref[0], extra_w, extra_e] + [other[...] for other in others]:
        mine = sub == spread(tile[SLOT_ROW:SLOT_ROW + 1]).astype(jnp.int32)
        for field in range(FIELDS):
            forcing[field] = forcing[field] + jnp.where(mine, spread(tile[field:field + 1]), 0.0)
    surface = zeros()
    rim = jnp.logical_or(sub == 0, sub == SUB - 1)
    for field in range(FIELDS):
        value = SURFACE_GAIN[field] * forcing[field]
        surface = jnp.where(sub == 2 * field, spread(value[SUB - 1:SUB]), surface)
        surface = jnp.where(sub == 2 * field + 1, spread(value[0:1]), surface)
        put_tile(force_ref, field, jnp.where(rim, 0.0, value))
        put_tile(force_ref, FIELDS + field, value)

    def finish(level, change):
        full = tile_at(packed_ref, level) + change
        put_tile(full_ref, level, full)
        if level < half:
            later = tile_at(full_ref, level + half)
            put_tile(east_ref, level, jnp.where(even, full, pltpu.roll(later, 1, 0)))
            put_tile(west_ref, level, jnp.where(even, pltpu.roll(full, SUB - 1, 0), later))

    edge_change(
        levels,
        lambda level: column_tiles(levels, level, east_in, west_in, even),
        lambda level: column_tiles(levels, level, east_own, west_own, even),
        halo_depth, gain_ref, down_ref, up_ref, surface, change_ref, finish,
    )


def merge_kernel(levels, inner_ref, reply_ref, change_ref, force_ref, out_ref, edge_ref):
    sub = sublane_ids()
    pair = ((lane_ids() + 1) % LANE) // 2
    forces = [tile_at(force_ref, field) for field in range(FIELDS)]

    def group_body(group, carry):
        packed = zeros()
        for inner in range(GROUP):
            level = group * GROUP + inner
            reply = tile_at(reply_ref, level)
            change = tile_at(change_ref, level)
            for field in range(FIELDS):
                j = inner * FIELDS + field
                side = pltpu.roll(change, SUB - 1 - 2 * field, 0)
                rim = jnp.logical_or(sub == 0, sub == SUB - 1)
                value = tile_at(inner_ref, field * levels + level) + jnp.where(rim, side, forces[field] * reply)
                put_tile(out_ref, field * levels + level, value)
                packed = jnp.where(pair == j, pltpu.roll(value, 2 * j, 1) if j else value, packed)
        put_tile(edge_ref, group, packed)
        return carry

    lax.fori_loop(0, levels // GROUP, group_body, 0)


def second_edge_kernel(levels, west_in, east_in, full_ref, packed_ref, gain_ref, down_ref, up_ref, depth_ref,
                       inner_ref, result_ref, state_ref, change_ref, sems):
    even = sublane_ids() % 2 == 0
    sub = sublane_ids()
    copies = []

    def finish(level, change):
        edge = tile_at(packed_ref, level) + change
        for field in range(FIELDS):
            side = pltpu.roll(edge, SUB - 1 - 2 * field, 0)
            rim = jnp.logical_or(sub == 0, sub == SUB - 1)
            row = field * levels + level
            put_tile(state_ref, row, jnp.where(rim, side, tile_at(inner_ref, row)))
        if level % GROUP == 0:
            for field in range(FIELDS):
                piece = pl.ds((field * levels + level) * SUB, GROUP * SUB)
                copy = pltpu.make_async_copy(
                    state_ref.at[piece, :], result_ref.at[piece, :], sems.at[level // GROUP, field]
                )
                copy.start()
                copies.append(copy)

    edge_change(
        levels,
        lambda level: column_tiles(levels, level, east_in, west_in, even),
        lambda level: tile_at(full_ref, level),
        depth_ref[...], gain_ref, down_ref, up_ref, None, change_ref, finish,
    )
    for copy in copies:
        copy.wait()


def in_vmem(value):
    return pltpu.with_memory_space_constraint(value, pltpu.VMEM)


def in_hbm(value):
    return pltpu.with_memory_space_constraint(value, pltpu.HBM)


def call(kernel, outs, args, scratch=(), hbm_in=(), hbm_out=(), aliases=None):
    return pl.pallas_call(
        kernel,
        out_shape=[
            (pltpu.HBM if at in hbm_out else pltpu.VMEM)(shape, dtype)
            for at, (shape, dtype) in enumerate(outs)
        ],
        in_specs=[HBM_SPEC if at in hbm_in else VMEM_SPEC for at in range(len(args))],
        out_specs=[HBM_SPEC if at in hbm_out else VMEM_SPEC for at in range(len(outs))],
        scratch_shapes=list(scratch),
        input_output_aliases=aliases or {},
        compiler_params=pltpu.CompilerParams(vmem_limit_bytes=VMEM_BYTES),
    )(*[in_hbm(arg) if at in hbm_in else in_vmem(arg) for at, arg in enumerate(args)])


def ring_shift(value, axis, amount):
    count = lax.axis_size(axis)
    return lax.ppermute(value, axis, [(i, (i + amount) % count) for i in range(count)])


def lat_exchange(edge):
    lon_total = lax.axis_size("lon")
    lat_total = lax.axis_size("lat") * lax.axis_size("comp")
    inside, between = [], []
    for lon in range(lon_total):
        first = lon * lat_total
        for low in range(0, lat_total, 2):
            inside += [(first + low, first + low + 1), (first + low + 1, first + low)]
        for low in range(1, lat_total - 1, 2):
            between += [(first + low, first + low + 1), (first + low + 1, first + low)]
        across = (lon + lon_total // 2) % lon_total * lat_total
        for end in (0, lat_total - 1):
            between.append((first + end, across + end))
    swap_a = lax.ppermute(edge, ("lon",) + LAT_AXES, inside)
    swap_b = lax.ppermute(edge, ("lon",) + LAT_AXES, between)
    return swap_a, swap_b


def bind(kernel, *head):
    def bound(*refs):
        return kernel(*head, *refs)

    bound.__name__ = kernel.__name__
    return bound


def local(ocean_state, level_count, mix_rate, atmos_flux, remap_weight, remap_target, remap_slot):
    field_total, levels, lon_dev, lat_dev = ocean_state.shape
    lon_total = lax.axis_size("lon")
    rows = field_total * levels
    groups = levels // GROUP
    f32, i32 = jnp.float32, jnp.int32
    state_shape = ((rows * lon_dev, lat_dev), f32)
    message = ((rows, lat_dev), f32)
    long_message = ((rows + EXTRA, lat_dev), f32)
    table = ((levels * lon_dev, lat_dev), f32)
    dma = pltpu.SemaphoreType.DMA
    merged = pltpu.VMEM((groups, SUB, LANE), f32)
    x = in_vmem(ocean_state.reshape(rows * lon_dev, lat_dev))

    east, west, parts, count, rate = call(
        bind(column_kernel, levels, lon_total),
        [long_message, long_message, ((lon_total, SUB, lat_dev), f32), ((lon_dev, lat_dev), i32), table],
        (ocean_state.reshape(rows, lon_dev, lat_dev), level_count, atmos_flux[0], remap_weight[0],
         remap_target, remap_slot, mix_rate.reshape(levels * lon_dev, lat_dev)),
        scratch=[
            pltpu.VMEM((2, rows, lat_dev), f32),
            pltpu.VMEM(atmos_flux.shape[1:], atmos_flux.dtype),
            pltpu.VMEM(remap_weight.shape[1:], remap_weight.dtype),
            pltpu.SMEM(remap_target.shape, i32),
            pltpu.SMEM(remap_slot.shape, i32),
            dma((8,)),
        ],
        hbm_in=range(7),
    )
    from_west = ring_shift(east, "lon", 1)
    from_east = ring_shift(west, "lon", -1)
    edge, gain, down, up, reply, edge_gain, edge_down, edge_up = call(
        bind(prepare_kernel, levels),
        [(((groups + 1) * SUB, lat_dev), f32)] + [table] * 7,
        (x, count, rate),
    )
    swap_a, swap_b = lat_exchange(edge)
    others = [ring_shift(parts[s], "lon", s) for s in range(2, lon_total - 1)]
    inner, packed, depths = call(
        bind(first_kernel, levels),
        [state_shape, table, ((4 * SUB, LANE), i32)],
        (x, count, gain, down, up, swap_a, swap_b),
        scratch=[merged],
    )
    east_next, west_next, full, change, force, halo_depth = call(
        bind(first_edge_kernel, levels, lon_total),
        [message, message, table, table, ((2 * FIELDS * SUB, LANE), f32), ((SUB, LANE), i32)],
        (from_west, from_east, east, west, packed, edge_gain, edge_down, edge_up, parts, *others),
    )
    from_west = ring_shift(east_next, "lon", 1)
    from_east = ring_shift(west_next, "lon", -1)
    state, edge = call(
        bind(merge_kernel, levels),
        [state_shape, ((groups * SUB, lat_dev), f32)],
        (inner, reply, change, force),
    )
    swap_a, swap_b = lat_exchange(edge)
    inner, packed = call(
        bind(second_kernel, levels),
        [state_shape, table],
        (state, depths, gain, down, up, swap_a, swap_b, force),
        scratch=[merged],
    )
    (result,) = call(
        bind(second_edge_kernel, levels),
        [state_shape],
        (from_west, from_east, full, packed, edge_gain, edge_down, edge_up, halo_depth, inner),
        scratch=[pltpu.VMEM(*state_shape), pltpu.VMEM(*table), dma((groups, FIELDS))],
        hbm_out=(0,),
    )
    return result.reshape(ocean_state.shape)


def solution(mesh):
    placed = (
        P(None, None, "lon", LAT_AXES),
        P("lon", LAT_AXES),
        P(None, "lon", LAT_AXES),
        P(LAT_AXES, "lon", None, None),
        P(LAT_AXES, "lon", None, None),
        P(LAT_AXES, "lon"),
        P(LAT_AXES, "lon"),
    )

    return jax.shard_map(
        local,
        mesh=mesh,
        in_specs=placed,
        out_specs=P(None, None, "lon", LAT_AXES),
        check_vma=False,
    )
```

```python
import jax
import jax.numpy as jnp
from jax import lax
from jax.experimental import pallas as pl
from jax.experimental.pallas import tpu as pltpu
from jax.sharding import PartitionSpec as P


DIFFUSE = 0.2
ADVECTION = 0.5
THERMAL = 0.2
HALINE = 0.15
GRAVITY = 0.05
CORIOLIS = 0.3
SURFACE_GAIN = (0.5, 0.4, 0.6, 0.6)

FIELDS = 4
SUB = 8
LANE = 128
PAIRS = LANE // 2
GROUP = PAIRS // FIELDS
EXTRA = 8
SLOT_ROW = 4
COUNT_ROW = 5
LAT_AXES = ("lat", "comp")
QUARTER = 0.5 * ADVECTION
WARMTH = THERMAL / HALINE
PUSH = 0.5 * GRAVITY * HALINE

VMEM_SPEC = pl.BlockSpec(memory_space=pltpu.VMEM)
HBM_SPEC = pl.BlockSpec(memory_space=pltpu.HBM)
VMEM_BYTES = 16 << 20


def sublane_ids():
    return lax.broadcasted_iota(jnp.int32, (SUB, LANE), 0)


def lane_ids():
    return lax.broadcasted_iota(jnp.int32, (SUB, LANE), 1)


def zeros():
    return jnp.zeros((SUB, LANE), jnp.float32)


def spread(row):
    return jnp.broadcast_to(row, (SUB, LANE))


def tile_at(ref, index):
    return ref[pl.ds(pl.multiple_of(index * SUB, SUB), SUB), :]


def put_tile(ref, index, value):
    ref[pl.ds(pl.multiple_of(index * SUB, SUB), SUB), :] = value


def lat_place():
    return lax.axis_index("lat") * lax.axis_size("comp") + lax.axis_index("comp")


def lat_sides(swap_a, swap_b, index):
    place = lat_place()
    total = lax.axis_size("lat") * lax.axis_size("comp")
    tile_a, tile_b = tile_at(swap_a, index), tile_at(swap_b, index)
    evenly = place % 2 == 0
    north = jnp.where(jnp.logical_and(place < total - 1, evenly), tile_a, 0.0)
    north = jnp.where(jnp.logical_and(place < total - 1, jnp.logical_not(evenly)), tile_b, north)
    south = jnp.where(jnp.logical_and(place > 0, evenly), tile_b, 0.0)
    south = jnp.where(jnp.logical_and(place > 0, jnp.logical_not(evenly)), tile_a, south)
    return south, north


def column_tiles(levels, level, east_ref, west_ref, even):
    half = levels // 2
    if level < half:
        return jnp.where(even, tile_at(east_ref, level), pltpu.roll(tile_at(west_ref, level), 1, 0))
    at = level - half
    return jnp.where(even, pltpu.roll(tile_at(east_ref, at), SUB - 1, 0), tile_at(west_ref, at))


def column_kernel(levels, lon_total, x_ref, count_hbm, flux_hbm, weight_hbm, target_hbm, slot_hbm,
                  rate_hbm, east_ref, west_ref, parts_ref, count_ref, rate_ref,
                  columns, flux_ref, weight_ref, target_ref, slot_ref, sems):
    me = lax.axis_index("lon")
    half = levels // 2
    sub = sublane_ids()
    copies = [
        pltpu.make_async_copy(count_hbm, count_ref, sems.at[2]),
        pltpu.make_async_copy(flux_hbm, flux_ref, sems.at[3]),
        pltpu.make_async_copy(weight_hbm, weight_ref, sems.at[4]),
        pltpu.make_async_copy(target_hbm, target_ref, sems.at[5]),
        pltpu.make_async_copy(slot_hbm, slot_ref, sems.at[6]),
    ]
    sides = [
        pltpu.make_async_copy(x_ref.at[:, SUB - 1, :], columns.at[0], sems.at[0]),
        pltpu.make_async_copy(x_ref.at[:, 0, :], columns.at[1], sems.at[1]),
    ]
    later = pltpu.make_async_copy(rate_hbm, rate_ref, sems.at[7])
    for copy in sides + copies + [later]:
        copy.start()
    for copy in copies:
        copy.wait()

    blocks = flux_ref.shape[0]
    for block in range(blocks):
        partial = jnp.dot(flux_ref[block], weight_ref[block], preferred_element_type=jnp.float32)
        slot = slot_ref[0, block].astype(jnp.float32)
        tile = jnp.concatenate([partial, jnp.full((SUB - FIELDS, LANE), slot, jnp.float32)], axis=0)
        shift = lax.rem(target_ref[0, block] - me + lon_total, lon_total)
        parts_ref[shift] = tile

    count = count_ref[...]
    count_f = count.astype(jnp.float32)
    for side, (out_ref, column, shift) in enumerate(
        ((east_ref, SUB - 1, 1), (west_ref, 0, lon_total - 1))
    ):
        sides[side].wait()
        depth = spread(count[column:column + 1, :])
        for field in range(FIELDS):
            for start in range(0, levels, SUB):
                value = columns[side, pl.ds(field * levels + start, SUB), :]
                value = jnp.where(start + sub < depth, value, 0.0)
                upper = start // half
                row = (start - upper * half) * SUB + 2 * field + upper
                out_ref[pl.ds(row, SUB, stride=SUB), :] = value
        out_ref[pl.ds(half * SUB, EXTRA), :] = jnp.where(
            sub == COUNT_ROW, spread(count_f[column:column + 1, :]), parts_ref[shift]
        )
    later.wait()


def prepare_kernel(levels, x_ref, count_ref, rate_ref, edge_ref, gain_ref, down_ref, up_ref, reply_ref,
                   edge_gain_ref, edge_down_ref, edge_up_ref):
    pair = ((lane_ids() + 1) % LANE) // 2
    count = count_ref[...]

    def group_body(group, carry):
        packed = zeros()
        lower, prev, reply = carry
        for inner in range(GROUP):
            level = group * GROUP + inner
            wet = level < count
            for field in range(FIELDS):
                j = inner * FIELDS + field
                value = jnp.where(wet, tile_at(x_ref, field * levels + level), 0.0)
                packed = jnp.where(pair == j, pltpu.roll(value, 2 * j, 1) if j else value, packed)
            upper = jnp.where(level + 1 < count, tile_at(rate_ref, level), 0.0)
            upper = jnp.where(level < levels - 1, upper, 0.0)
            inverse = 1.0 / (1.0 + upper + lower - lower * prev)
            prev = upper * inverse
            gain = jnp.where(wet, inverse, 0.0)
            down = lower * inverse
            reply = jnp.where(level == 0, gain, down * reply)
            put_tile(gain_ref, level, gain)
            put_tile(down_ref, level, down)
            put_tile(up_ref, level, prev)
            put_tile(reply_ref, level, reply)
            lower = upper
        put_tile(edge_ref, group, packed)
        return lower, prev, reply

    lax.fori_loop(0, levels // GROUP, group_body, (zeros(), zeros(), zeros()))
    put_tile(edge_ref, levels // GROUP, count.astype(jnp.float32))

    def back_body(step, following):
        level = levels - 1 - step
        value = tile_at(reply_ref, level) + tile_at(up_ref, level) * following
        put_tile(reply_ref, level, value)
        return value

    lax.fori_loop(0, levels, back_body, zeros(), unroll=16)
    for source_ref, out_ref in ((gain_ref, edge_gain_ref), (down_ref, edge_down_ref), (up_ref, edge_up_ref)):
        pack_edges(levels, 1, source_ref, out_ref)


def pack_edges(levels, fields, source_ref, out_ref):
    for side, column in ((0, SUB - 1), (1, 0)):
        for start in range(0, levels, SUB):
            for field in range(FIELDS):
                if field < fields:
                    row = (field * levels + start) * SUB + column
                    value = source_ref[pl.ds(row, SUB, stride=SUB), :]
                out_ref[pl.ds(start * SUB + 2 * field + side, SUB, stride=SUB), :] = value


def explicit_kernel(levels, later, x_ref, count_ref, *rest):
    force_ref, out_ref = rest if later else (None, rest[0])
    sub = sublane_ids()
    lane = lane_ids()
    lat_total = LANE * lax.axis_size("lat") * lax.axis_size("comp")
    row_ids = (lat_place() * LANE + lane).astype(jnp.float32)
    rotation = CORIOLIS * (2.0 * (row_ids + 0.5) / lat_total - 1.0)
    depth = count_ref[...]

    def neighbours(value):
        return (
            jnp.where(sub == SUB - 1, 0, pltpu.roll(value, SUB - 1, 0)),
            jnp.where(sub == 0, 0, pltpu.roll(value, 1, 0)),
            jnp.where(lane == LANE - 1, 0, pltpu.roll(value, LANE - 1, 1)),
            jnp.where(lane == 0, 0, pltpu.roll(value, 1, 1)),
        )

    depth_e, depth_w, depth_n, depth_s = neighbours(depth)

    def level_body(level, inner, carry):
        sum_e, sum_w, sum_n, sum_s = carry
        here, east, west, north, south = [], [], [], [], []
        for field in range(FIELDS):
            value = tile_at(x_ref, field * levels + level)
            if not later:
                value = jnp.where(level < depth, value, 0.0)
            here.append(value)
            for into, side in zip((east, west, north, south), neighbours(value)):
                into.append(side)
        wet_e, wet_w, wet_n, wet_s = level < depth_e, level < depth_w, level < depth_n, level < depth_s
        keep = 1.0 - (
            (jnp.where(wet_e, DIFFUSE, 0.0) + jnp.where(wet_w, DIFFUSE, 0.0))
            + (jnp.where(wet_n, DIFFUSE, 0.0) + jnp.where(wet_s, DIFFUSE, 0.0))
        )
        sum_e = sum_e + (east[1] - WARMTH * east[0])
        sum_w = sum_w + (west[1] - WARMTH * west[0])
        sum_n = sum_n + (north[1] - WARMTH * north[0])
        sum_s = sum_s + (south[1] - WARMTH * south[0])
        force_x = PUSH * (jnp.where(wet_e, sum_e, 0.0) - jnp.where(wet_w, sum_w, 0.0))
        force_y = PUSH * (jnp.where(wet_n, sum_n, 0.0) - jnp.where(wet_s, sum_s, 0.0))
        u, v = here[2], here[3]
        u_part = QUARTER * u
        v_part = QUARTER * v
        for field in range(FIELDS):
            around = (east[field] + west[field]) + (north[field] + south[field])
            value = keep * here[field] + DIFFUSE * around
            if field < 2:
                value = value - (
                    u_part * (east[field] - west[field]) + v_part * (north[field] - south[field])
                )
            elif field == 2:
                value = value + (rotation * v - force_x)
            else:
                value = value - (rotation * u + force_y)
            if inner == 0 and later:
                value = value + jnp.where(level == 0, tile_at(force_ref, FIELDS + field), 0.0)
            put_tile(out_ref, field * levels + level, value)
        return sum_e, sum_w, sum_n, sum_s

    def group_body(group, carry):
        for inner in range(GROUP):
            carry = level_body(group * GROUP + inner, inner, carry)
        return carry

    lax.fori_loop(0, levels // GROUP, group_body, (zeros(),) * 4)


def solve_kernel(levels, later, x_ref, explicit_ref, gain_ref, down_ref, up_ref, swap_a, swap_b, *rest):
    if later:
        depth_ref, out_ref, packed_ref, merged_ref = rest
    else:
        out_ref, packed_ref, depth_ref, merged_ref = rest
    lane = lane_ids()
    even = lane % 2 == 0
    groups = levels // GROUP
    north_lane, south_lane = lane == LANE - 1, lane == 0
    rim = jnp.logical_or(north_lane, south_lane)
    sign = jnp.where(north_lane, -1.0, jnp.where(south_lane, 1.0, 0.0))
    if later:
        halo_depth = depth_ref[...]
    else:
        south, north = lat_sides(swap_a, swap_b, groups)
        halo_depth = jnp.where(
            north_lane, pltpu.roll(north, LANE - 1, 1), jnp.where(south_lane, pltpu.roll(south, 1, 1), 0.0)
        ).astype(jnp.int32)
        depth_ref[...] = halo_depth
    for group in range(groups):
        south, north = lat_sides(swap_a, swap_b, group)
        merged_ref[group] = jnp.where(even, north, pltpu.roll(south, 2, 1))

    def level_body(level, inner, halo, carry):
        total, *prev = carry
        sides = []
        for field in range(FIELDS):
            j = inner * FIELDS + field
            sides.append(jnp.where(rim, pltpu.roll(halo, (LANE - 1 - 2 * j) % LANE, 1), 0.0))
        total = total + (sides[1] - WARMTH * sides[0])
        wet = level < halo_depth
        v_part = (QUARTER * sign) * tile_at(x_ref, 3 * levels + level)
        gain = tile_at(gain_ref, level)
        down = tile_at(down_ref, level)
        done = []
        for field in range(FIELDS):
            row = field * levels + level
            value = tile_at(explicit_ref, row)
            value = value + DIFFUSE * (sides[field] - jnp.where(wet, tile_at(x_ref, row), 0.0))
            if field < 2:
                value = value + v_part * sides[field]
            elif field == 3:
                value = value + (PUSH * sign) * jnp.where(wet, total, 0.0)
            value = value * gain + down * prev[field]
            put_tile(out_ref, row, value)
            done.append(value)
        return (total, *done)

    def forward_group(group, carry):
        halo = merged_ref[group]
        for inner in range(GROUP):
            carry = level_body(group * GROUP + inner, inner, halo, carry)
        return carry

    lax.fori_loop(0, groups, forward_group, (zeros(),) * (1 + FIELDS))

    def backward_group(step, following):
        group = groups - 1 - step
        for inner in range(GROUP - 1, -1, -1):
            level = group * GROUP + inner
            ratio = tile_at(up_ref, level)
            now = []
            for field in range(FIELDS):
                value = tile_at(out_ref, field * levels + level) + ratio * following[field]
                put_tile(out_ref, field * levels + level, value)
                now.append(value)
            following = tuple(now)
        return following

    lax.fori_loop(0, groups, backward_group, (zeros(),) * FIELDS)
    pack_edges(levels, FIELDS, out_ref, packed_ref)


def edge_change(levels, halo_at, own_at, halo_depth, gain_ref, down_ref, up_ref, surface, change_ref, finish):
    sub = sublane_ids()
    even = sub % 2 == 0
    field = sub // 2
    sign = jnp.where(even, 1.0, -1.0)
    carry_by = jnp.where(field < 2, -QUARTER * sign, 0.0)
    push_by = jnp.where(field == 2, -PUSH * sign, 0.0)
    total = zeros()
    value = zeros()
    for level in range(levels):
        halo = halo_at(level)
        own = own_at(level)
        wet = level < halo_depth
        speed = jnp.where(field == 0, pltpu.roll(own, 4, 0), pltpu.roll(own, 6, 0))
        total = total + (pltpu.roll(halo, 2, 0) - WARMTH * pltpu.roll(halo, 4, 0))
        change = DIFFUSE * (halo - jnp.where(wet, own, 0.0)) + (carry_by * speed) * halo
        change = change + push_by * jnp.where(wet, total, 0.0)
        if level == 0 and surface is not None:
            change = change + surface
        value = change * tile_at(gain_ref, level) + tile_at(down_ref, level) * value
        put_tile(change_ref, level, value)
    following = zeros()
    for level in range(levels - 1, -1, -1):
        following = tile_at(change_ref, level) + tile_at(up_ref, level) * following
        put_tile(change_ref, level, following)
        finish(level, following)


def first_edge_kernel(levels, lon_total, west_in, east_in, east_own, west_own, packed_ref,
                      gain_ref, down_ref, up_ref, parts_ref, *rest):
    others = rest[:lon_total - 3]
    east_ref, west_ref, full_ref, change_ref, force_ref, depth_ref = rest[lon_total - 3:]
    sub = sublane_ids()
    even = sub % 2 == 0
    half = levels // 2
    extra_w = west_in[pl.ds(half * SUB, EXTRA), :]
    extra_e = east_in[pl.ds(half * SUB, EXTRA), :]
    depth_f = jnp.where(even, spread(extra_e[COUNT_ROW:COUNT_ROW + 1]), spread(extra_w[COUNT_ROW:COUNT_ROW + 1]))
    halo_depth = depth_f.astype(jnp.int32)
    depth_ref[...] = halo_depth
    forcing = [zeros()] * FIELDS
    for tile in [parts_ref[0], extra_w, extra_e] + [other[...] for other in others]:
        mine = sub == spread(tile[SLOT_ROW:SLOT_ROW + 1]).astype(jnp.int32)
        for field in range(FIELDS):
            forcing[field] = forcing[field] + jnp.where(mine, spread(tile[field:field + 1]), 0.0)
    surface = zeros()
    rim = jnp.logical_or(sub == 0, sub == SUB - 1)
    for field in range(FIELDS):
        value = SURFACE_GAIN[field] * forcing[field]
        surface = jnp.where(sub == 2 * field, spread(value[SUB - 1:SUB]), surface)
        surface = jnp.where(sub == 2 * field + 1, spread(value[0:1]), surface)
        put_tile(force_ref, field, jnp.where(rim, 0.0, value))
        put_tile(force_ref, FIELDS + field, value)

    def finish(level, change):
        full = tile_at(packed_ref, level) + change
        put_tile(full_ref, level, full)
        if level < half:
            later = tile_at(full_ref, level + half)
            put_tile(east_ref, level, jnp.where(even, full, pltpu.roll(later, 1, 0)))
            put_tile(west_ref, level, jnp.where(even, pltpu.roll(full, SUB - 1, 0), later))

    edge_change(
        levels,
        lambda level: column_tiles(levels, level, east_in, west_in, even),
        lambda level: column_tiles(levels, level, east_own, west_own, even),
        halo_depth, gain_ref, down_ref, up_ref, surface, change_ref, finish,
    )


def merge_kernel(levels, inner_ref, reply_ref, change_ref, force_ref, out_ref, edge_ref):
    sub = sublane_ids()
    pair = ((lane_ids() + 1) % LANE) // 2
    forces = [tile_at(force_ref, field) for field in range(FIELDS)]

    def group_body(group, carry):
        packed = zeros()
        for inner in range(GROUP):
            level = group * GROUP + inner
            reply = tile_at(reply_ref, level)
            change = tile_at(change_ref, level)
            for field in range(FIELDS):
                j = inner * FIELDS + field
                side = pltpu.roll(change, SUB - 1 - 2 * field, 0)
                rim = jnp.logical_or(sub == 0, sub == SUB - 1)
                value = tile_at(inner_ref, field * levels + level) + jnp.where(rim, side, forces[field] * reply)
                put_tile(out_ref, field * levels + level, value)
                packed = jnp.where(pair == j, pltpu.roll(value, 2 * j, 1) if j else value, packed)
        put_tile(edge_ref, group, packed)
        return carry

    lax.fori_loop(0, levels // GROUP, group_body, 0)


def second_edge_kernel(levels, west_in, east_in, full_ref, packed_ref, gain_ref, down_ref, up_ref, depth_ref,
                       inner_ref, result_ref, change_ref, columns, bulk_sems, sems):
    even = sublane_ids() % 2 == 0
    copies = []

    def bulk(group):
        for field in range(FIELDS):
            piece = pl.ds(field * levels + group * GROUP, GROUP)
            yield pltpu.make_async_copy(inner_ref.at[piece], result_ref.at[piece], bulk_sems.at[group, field])

    for group in range(levels // GROUP - 1, -1, -1):
        for copy in bulk(group):
            copy.start()

    def finish(level, change):
        columns[level] = tile_at(packed_ref, level) + change
        if level % GROUP == 0:
            for copy in bulk(level // GROUP):
                copy.wait()
            for field in range(FIELDS):
                for side, column in ((0, SUB - 1), (1, 0)):
                    copy = pltpu.make_async_copy(
                        columns.at[pl.ds(level, GROUP), 2 * field + side, :],
                        result_ref.at[pl.ds(field * levels + level, GROUP), column, :],
                        sems.at[level // GROUP, 2 * field + side],
                    )
                    copy.start()
                    copies.append(copy)

    edge_change(
        levels,
        lambda level: column_tiles(levels, level, east_in, west_in, even),
        lambda level: tile_at(full_ref, level),
        depth_ref[...], gain_ref, down_ref, up_ref, None, change_ref, finish,
    )
    for copy in copies:
        copy.wait()


def in_vmem(value):
    return pltpu.with_memory_space_constraint(value, pltpu.VMEM)


def in_hbm(value):
    return pltpu.with_memory_space_constraint(value, pltpu.HBM)


def call(kernel, outs, args, scratch=(), hbm_in=(), hbm_out=(), aliases=None):
    return pl.pallas_call(
        kernel,
        out_shape=[
            (pltpu.HBM if at in hbm_out else pltpu.VMEM)(shape, dtype)
            for at, (shape, dtype) in enumerate(outs)
        ],
        in_specs=[HBM_SPEC if at in hbm_in else VMEM_SPEC for at in range(len(args))],
        out_specs=[HBM_SPEC if at in hbm_out else VMEM_SPEC for at in range(len(outs))],
        scratch_shapes=list(scratch),
        input_output_aliases=aliases or {},
        compiler_params=pltpu.CompilerParams(vmem_limit_bytes=VMEM_BYTES),
    )(*[in_hbm(arg) if at in hbm_in else in_vmem(arg) for at, arg in enumerate(args)])


def ring_shift(value, axis, amount):
    count = lax.axis_size(axis)
    return lax.ppermute(value, axis, [(i, (i + amount) % count) for i in range(count)])


def lat_exchange(edge):
    lon_total = lax.axis_size("lon")
    lat_total = lax.axis_size("lat") * lax.axis_size("comp")
    inside, between = [], []
    for lon in range(lon_total):
        first = lon * lat_total
        for low in range(0, lat_total, 2):
            inside += [(first + low, first + low + 1), (first + low + 1, first + low)]
        for low in range(1, lat_total - 1, 2):
            between += [(first + low, first + low + 1), (first + low + 1, first + low)]
        across = (lon + lon_total // 2) % lon_total * lat_total
        for end in (0, lat_total - 1):
            between.append((first + end, across + end))
    swap_a = lax.ppermute(edge, ("lon",) + LAT_AXES, inside)
    swap_b = lax.ppermute(edge, ("lon",) + LAT_AXES, between)
    return swap_a, swap_b


def bind(kernel, *head):
    def bound(*refs):
        return kernel(*head, *refs)

    bound.__name__ = kernel.__name__
    return bound


def local(ocean_state, level_count, mix_rate, atmos_flux, remap_weight, remap_target, remap_slot):
    field_total, levels, lon_dev, lat_dev = ocean_state.shape
    lon_total = lax.axis_size("lon")
    rows = field_total * levels
    groups = levels // GROUP
    f32, i32 = jnp.float32, jnp.int32
    state_shape = ((rows * lon_dev, lat_dev), f32)
    message = ((rows, lat_dev), f32)
    long_message = ((rows + EXTRA, lat_dev), f32)
    table = ((levels * lon_dev, lat_dev), f32)
    dma = pltpu.SemaphoreType.DMA
    merged = pltpu.VMEM((groups, SUB, LANE), f32)
    x = in_vmem(ocean_state.reshape(rows * lon_dev, lat_dev))

    east, west, parts, count, rate = call(
        bind(column_kernel, levels, lon_total),
        [long_message, long_message, ((lon_total, SUB, lat_dev), f32), ((lon_dev, lat_dev), i32), table],
        (ocean_state.reshape(rows, lon_dev, lat_dev), level_count, atmos_flux[0], remap_weight[0],
         remap_target, remap_slot, mix_rate.reshape(levels * lon_dev, lat_dev)),
        scratch=[
            pltpu.VMEM((2, rows, lat_dev), f32),
            pltpu.VMEM(atmos_flux.shape[1:], atmos_flux.dtype),
            pltpu.VMEM(remap_weight.shape[1:], remap_weight.dtype),
            pltpu.SMEM(remap_target.shape, i32),
            pltpu.SMEM(remap_slot.shape, i32),
            dma((8,)),
        ],
        hbm_in=range(7),
    )
    from_west = ring_shift(east, "lon", 1)
    from_east = ring_shift(west, "lon", -1)
    edge, gain, down, up, reply, edge_gain, edge_down, edge_up = call(
        bind(prepare_kernel, levels),
        [(((groups + 1) * SUB, lat_dev), f32)] + [table] * 7,
        (x, count, rate),
    )
    swap_a, swap_b = lat_exchange(edge)
    others = []
    for s in range(2, lon_total - 1):
        others.append(ring_shift(parts[s], "lon", s))
    (explicit,) = call(bind(explicit_kernel, levels, False), [state_shape], (x, count))
    inner, packed, lat_depth = call(
        bind(solve_kernel, levels, False),
        [state_shape, table, ((SUB, LANE), i32)],
        (x, explicit, gain, down, up, swap_a, swap_b),
        scratch=[merged],
    )
    east_next, west_next, full, change, force, halo_depth = call(
        bind(first_edge_kernel, levels, lon_total),
        [message, message, table, table, ((2 * FIELDS * SUB, LANE), f32), ((SUB, LANE), i32)],
        (from_west, from_east, east, west, packed, edge_gain, edge_down, edge_up, parts, *others),
    )
    from_west = ring_shift(east_next, "lon", 1)
    from_east = ring_shift(west_next, "lon", -1)
    state, edge = call(
        bind(merge_kernel, levels),
        [state_shape, ((groups * SUB, lat_dev), f32)],
        (inner, reply, change, force),
    )
    swap_a, swap_b = lat_exchange(edge)
    (explicit,) = call(bind(explicit_kernel, levels, True), [state_shape], (state, count, force))
    inner, packed = call(
        bind(solve_kernel, levels, True),
        [state_shape, table],
        (state, explicit, gain, down, up, swap_a, swap_b, lat_depth),
        scratch=[merged],
    )
    (result,) = call(
        bind(second_edge_kernel, levels),
        [((rows, lon_dev, lat_dev), f32)],
        (from_west, from_east, full, packed, edge_gain, edge_down, edge_up, halo_depth,
         inner.reshape(rows, lon_dev, lat_dev)),
        scratch=[pltpu.VMEM(*table), pltpu.VMEM((levels, SUB, LANE), f32), dma((groups, FIELDS)),
                 dma((groups, 2 * FIELDS))],
        hbm_out=(0,),
    )
    return result.reshape(ocean_state.shape)


def solution(mesh):
    placed = (
        P(None, None, "lon", LAT_AXES),
        P("lon", LAT_AXES),
        P(None, "lon", LAT_AXES),
        P(LAT_AXES, "lon", None, None),
        P(LAT_AXES, "lon", None, None),
        P(LAT_AXES, "lon"),
        P(LAT_AXES, "lon"),
    )

    return jax.shard_map(
        local,
        mesh=mesh,
        in_specs=placed,
        out_specs=P(None, None, "lon", LAT_AXES),
        check_vma=False,
    )
```

```python
import jax
import jax.numpy as jnp
from jax import lax
from jax.experimental import pallas as pl
from jax.experimental.pallas import tpu as pltpu
from jax.sharding import PartitionSpec as P


DIFFUSE = 0.2
ADVECTION = 0.5
THERMAL = 0.2
HALINE = 0.15
GRAVITY = 0.05
CORIOLIS = 0.3
SURFACE_GAIN = (0.5, 0.4, 0.6, 0.6)

FIELDS = 4
SUB = 8
LANE = 128
PAIRS = LANE // 2
GROUP = PAIRS // FIELDS
EXTRA = 8
SLOT_ROW = 4
COUNT_ROW = 5
LAT_AXES = ("lat", "comp")
QUARTER = 0.5 * ADVECTION
WARMTH = THERMAL / HALINE
PUSH = 0.5 * GRAVITY * HALINE

VMEM_SPEC = pl.BlockSpec(memory_space=pltpu.VMEM)
HBM_SPEC = pl.BlockSpec(memory_space=pltpu.HBM)
VMEM_BYTES = 16 << 20


def sublane_ids():
    return lax.broadcasted_iota(jnp.int32, (SUB, LANE), 0)


def lane_ids():
    return lax.broadcasted_iota(jnp.int32, (SUB, LANE), 1)


def zeros():
    return jnp.zeros((SUB, LANE), jnp.float32)


def spread(row):
    return jnp.broadcast_to(row, (SUB, LANE))


def tile_at(ref, index):
    return ref[pl.ds(pl.multiple_of(index * SUB, SUB), SUB), :]


def put_tile(ref, index, value):
    ref[pl.ds(pl.multiple_of(index * SUB, SUB), SUB), :] = value


def lat_place():
    return lax.axis_index("lat") * lax.axis_size("comp") + lax.axis_index("comp")


def lat_sides(swap_a, swap_b, index):
    place = lat_place()
    total = lax.axis_size("lat") * lax.axis_size("comp")
    tile_a, tile_b = tile_at(swap_a, index), tile_at(swap_b, index)
    evenly = place % 2 == 0
    north = jnp.where(jnp.logical_and(place < total - 1, evenly), tile_a, 0.0)
    north = jnp.where(jnp.logical_and(place < total - 1, jnp.logical_not(evenly)), tile_b, north)
    south = jnp.where(jnp.logical_and(place > 0, evenly), tile_b, 0.0)
    south = jnp.where(jnp.logical_and(place > 0, jnp.logical_not(evenly)), tile_a, south)
    return south, north


def column_tiles(levels, level, east_ref, west_ref, even):
    half = levels // 2
    if level < half:
        return jnp.where(even, tile_at(east_ref, level), pltpu.roll(tile_at(west_ref, level), 1, 0))
    at = level - half
    return jnp.where(even, pltpu.roll(tile_at(east_ref, at), SUB - 1, 0), tile_at(west_ref, at))


def column_kernel(levels, lon_total, x_ref, count_hbm, flux_hbm, weight_hbm, target_hbm, slot_hbm,
                  rate_hbm, east_ref, west_ref, parts_ref, count_ref, rate_ref,
                  columns, flux_ref, weight_ref, target_ref, slot_ref, sems):
    me = lax.axis_index("lon")
    half = levels // 2
    sub = sublane_ids()
    copies = [
        pltpu.make_async_copy(count_hbm, count_ref, sems.at[2]),
        pltpu.make_async_copy(flux_hbm, flux_ref, sems.at[3]),
        pltpu.make_async_copy(weight_hbm, weight_ref, sems.at[4]),
        pltpu.make_async_copy(target_hbm, target_ref, sems.at[5]),
        pltpu.make_async_copy(slot_hbm, slot_ref, sems.at[6]),
    ]
    sides = [
        pltpu.make_async_copy(x_ref.at[:, SUB - 1, :], columns.at[0], sems.at[0]),
        pltpu.make_async_copy(x_ref.at[:, 0, :], columns.at[1], sems.at[1]),
    ]
    later = pltpu.make_async_copy(rate_hbm, rate_ref, sems.at[7])
    for copy in sides + copies + [later]:
        copy.start()
    for copy in copies:
        copy.wait()

    blocks = flux_ref.shape[0]
    for block in range(blocks):
        partial = jnp.dot(flux_ref[block], weight_ref[block], preferred_element_type=jnp.float32)
        slot = slot_ref[0, block].astype(jnp.float32)
        tile = jnp.concatenate([partial, jnp.full((SUB - FIELDS, LANE), slot, jnp.float32)], axis=0)
        shift = lax.rem(target_ref[0, block] - me + lon_total, lon_total)
        parts_ref[shift] = tile

    count = count_ref[...]
    count_f = count.astype(jnp.float32)
    for side, (out_ref, column, shift) in enumerate(
        ((east_ref, SUB - 1, 1), (west_ref, 0, lon_total - 1))
    ):
        sides[side].wait()
        depth = spread(count[column:column + 1, :])
        for field in range(FIELDS):
            for start in range(0, levels, SUB):
                value = columns[side, pl.ds(field * levels + start, SUB), :]
                value = jnp.where(start + sub < depth, value, 0.0)
                upper = start // half
                row = (start - upper * half) * SUB + 2 * field + upper
                out_ref[pl.ds(row, SUB, stride=SUB), :] = value
        out_ref[pl.ds(half * SUB, EXTRA), :] = jnp.where(
            sub == COUNT_ROW, spread(count_f[column:column + 1, :]), parts_ref[shift]
        )
    later.wait()


def prepare_kernel(levels, x_ref, count_ref, rate_ref, edge_ref, gain_ref, down_ref, up_ref, reply_ref,
                   edge_gain_ref, edge_down_ref, edge_up_ref):
    pair = ((lane_ids() + 1) % LANE) // 2
    count = count_ref[...]

    def group_body(group, carry):
        packed = zeros()
        lower, prev, reply = carry
        for inner in range(GROUP):
            level = group * GROUP + inner
            wet = level < count
            for field in range(FIELDS):
                j = inner * FIELDS + field
                value = jnp.where(wet, tile_at(x_ref, field * levels + level), 0.0)
                packed = jnp.where(pair == j, pltpu.roll(value, 2 * j, 1) if j else value, packed)
            upper = jnp.where(level + 1 < count, tile_at(rate_ref, level), 0.0)
            upper = jnp.where(level < levels - 1, upper, 0.0)
            inverse = 1.0 / (1.0 + upper + lower - lower * prev)
            prev = upper * inverse
            gain = jnp.where(wet, inverse, 0.0)
            down = lower * inverse
            reply = jnp.where(level == 0, gain, down * reply)
            put_tile(gain_ref, level, gain)
            put_tile(down_ref, level, down)
            put_tile(up_ref, level, prev)
            put_tile(reply_ref, level, reply)
            lower = upper
        put_tile(edge_ref, group, packed)
        return lower, prev, reply

    lax.fori_loop(0, levels // GROUP, group_body, (zeros(), zeros(), zeros()))
    put_tile(edge_ref, levels // GROUP, count.astype(jnp.float32))

    def back_body(step, following):
        level = levels - 1 - step
        value = tile_at(reply_ref, level) + tile_at(up_ref, level) * following
        put_tile(reply_ref, level, value)
        return value

    lax.fori_loop(0, levels, back_body, zeros(), unroll=16)
    for source_ref, out_ref in ((gain_ref, edge_gain_ref), (down_ref, edge_down_ref), (up_ref, edge_up_ref)):
        pack_edges(levels, 1, source_ref, out_ref)


def pack_edges(levels, fields, source_ref, out_ref):
    for side, column in ((0, SUB - 1), (1, 0)):
        for start in range(0, levels, SUB):
            for field in range(FIELDS):
                if field < fields:
                    row = (field * levels + start) * SUB + column
                    value = source_ref[pl.ds(row, SUB, stride=SUB), :]
                out_ref[pl.ds(start * SUB + 2 * field + side, SUB, stride=SUB), :] = value


def explicit_kernel(levels, later, x_ref, count_ref, *rest):
    force_ref, out_ref = rest if later else (None, rest[0])
    sub = sublane_ids()
    lane = lane_ids()
    lat_total = LANE * lax.axis_size("lat") * lax.axis_size("comp")
    row_ids = (lat_place() * LANE + lane).astype(jnp.float32)
    rotation = CORIOLIS * (2.0 * (row_ids + 0.5) / lat_total - 1.0)
    depth = count_ref[...]

    def neighbours(value):
        return (
            jnp.where(sub == SUB - 1, 0, pltpu.roll(value, SUB - 1, 0)),
            jnp.where(sub == 0, 0, pltpu.roll(value, 1, 0)),
            jnp.where(lane == LANE - 1, 0, pltpu.roll(value, LANE - 1, 1)),
            jnp.where(lane == 0, 0, pltpu.roll(value, 1, 1)),
        )

    depth_e, depth_w, depth_n, depth_s = neighbours(depth)

    def level_body(level, inner, carry):
        sum_e, sum_w, sum_n, sum_s = carry
        here, east, west, north, south = [], [], [], [], []
        for field in range(FIELDS):
            value = tile_at(x_ref, field * levels + level)
            if not later:
                value = jnp.where(level < depth, value, 0.0)
            here.append(value)
            for into, side in zip((east, west, north, south), neighbours(value)):
                into.append(side)
        wet_e, wet_w, wet_n, wet_s = level < depth_e, level < depth_w, level < depth_n, level < depth_s
        keep = 1.0 - (
            (jnp.where(wet_e, DIFFUSE, 0.0) + jnp.where(wet_w, DIFFUSE, 0.0))
            + (jnp.where(wet_n, DIFFUSE, 0.0) + jnp.where(wet_s, DIFFUSE, 0.0))
        )
        sum_e = sum_e + (east[1] - WARMTH * east[0])
        sum_w = sum_w + (west[1] - WARMTH * west[0])
        sum_n = sum_n + (north[1] - WARMTH * north[0])
        sum_s = sum_s + (south[1] - WARMTH * south[0])
        force_x = PUSH * (jnp.where(wet_e, sum_e, 0.0) - jnp.where(wet_w, sum_w, 0.0))
        force_y = PUSH * (jnp.where(wet_n, sum_n, 0.0) - jnp.where(wet_s, sum_s, 0.0))
        u, v = here[2], here[3]
        u_part = QUARTER * u
        v_part = QUARTER * v
        for field in range(FIELDS):
            around = (east[field] + west[field]) + (north[field] + south[field])
            value = keep * here[field] + DIFFUSE * around
            if field < 2:
                value = value - (
                    u_part * (east[field] - west[field]) + v_part * (north[field] - south[field])
                )
            elif field == 2:
                value = value + (rotation * v - force_x)
            else:
                value = value - (rotation * u + force_y)
            if inner == 0 and later:
                value = value + jnp.where(level == 0, tile_at(force_ref, FIELDS + field), 0.0)
            put_tile(out_ref, field * levels + level, value)
        return sum_e, sum_w, sum_n, sum_s

    def group_body(group, carry):
        for inner in range(GROUP):
            carry = level_body(group * GROUP + inner, inner, carry)
        return carry

    lax.fori_loop(0, levels // GROUP, group_body, (zeros(),) * 4)


def solve_kernel(levels, later, x_ref, explicit_ref, gain_ref, down_ref, up_ref, swap_a, swap_b, *rest):
    if later:
        depth_ref, out_ref, packed_ref, merged_ref = rest
    else:
        out_ref, packed_ref, depth_ref, merged_ref = rest
    lane = lane_ids()
    even = lane % 2 == 0
    groups = levels // GROUP
    north_lane, south_lane = lane == LANE - 1, lane == 0
    rim = jnp.logical_or(north_lane, south_lane)
    sign = jnp.where(north_lane, -1.0, jnp.where(south_lane, 1.0, 0.0))
    if later:
        halo_depth = depth_ref[...]
    else:
        south, north = lat_sides(swap_a, swap_b, groups)
        halo_depth = jnp.where(
            north_lane, pltpu.roll(north, LANE - 1, 1), jnp.where(south_lane, pltpu.roll(south, 1, 1), 0.0)
        ).astype(jnp.int32)
        depth_ref[...] = halo_depth
    for group in range(groups):
        south, north = lat_sides(swap_a, swap_b, group)
        merged_ref[group] = jnp.where(even, north, pltpu.roll(south, 2, 1))

    def level_body(level, inner, halo, carry):
        total, *prev = carry
        sides = []
        for field in range(FIELDS):
            j = inner * FIELDS + field
            sides.append(jnp.where(rim, pltpu.roll(halo, (LANE - 1 - 2 * j) % LANE, 1), 0.0))
        total = total + (sides[1] - WARMTH * sides[0])
        wet = level < halo_depth
        v_part = (QUARTER * sign) * tile_at(x_ref, 3 * levels + level)
        gain = tile_at(gain_ref, level)
        down = tile_at(down_ref, level)
        done = []
        for field in range(FIELDS):
            row = field * levels + level
            value = tile_at(explicit_ref, row)
            value = value + DIFFUSE * (sides[field] - jnp.where(wet, tile_at(x_ref, row), 0.0))
            if field < 2:
                value = value + v_part * sides[field]
            elif field == 3:
                value = value + (PUSH * sign) * jnp.where(wet, total, 0.0)
            value = value * gain + down * prev[field]
            put_tile(out_ref, row, value)
            done.append(value)
        return (total, *done)

    def forward_group(group, carry):
        halo = merged_ref[group]
        for inner in range(GROUP):
            carry = level_body(group * GROUP + inner, inner, halo, carry)
        return carry

    lax.fori_loop(0, groups, forward_group, (zeros(),) * (1 + FIELDS))

    def backward_group(step, following):
        group = groups - 1 - step
        for inner in range(GROUP - 1, -1, -1):
            level = group * GROUP + inner
            ratio = tile_at(up_ref, level)
            now = []
            for field in range(FIELDS):
                value = tile_at(out_ref, field * levels + level) + ratio * following[field]
                put_tile(out_ref, field * levels + level, value)
                now.append(value)
            following = tuple(now)
        return following

    lax.fori_loop(0, groups, backward_group, (zeros(),) * FIELDS)
    pack_edges(levels, FIELDS, out_ref, packed_ref)


def edge_change(levels, halo_at, own_at, halo_depth, gain_ref, down_ref, up_ref, surface, change_ref, finish):
    sub = sublane_ids()
    even = sub % 2 == 0
    field = sub // 2
    sign = jnp.where(even, 1.0, -1.0)
    carry_by = jnp.where(field < 2, -QUARTER * sign, 0.0)
    push_by = jnp.where(field == 2, -PUSH * sign, 0.0)
    total = zeros()
    value = zeros()
    for level in range(levels):
        halo = halo_at(level)
        own = own_at(level)
        wet = level < halo_depth
        speed = jnp.where(field == 0, pltpu.roll(own, 4, 0), pltpu.roll(own, 6, 0))
        total = total + (pltpu.roll(halo, 2, 0) - WARMTH * pltpu.roll(halo, 4, 0))
        change = DIFFUSE * (halo - jnp.where(wet, own, 0.0)) + (carry_by * speed) * halo
        change = change + push_by * jnp.where(wet, total, 0.0)
        if level == 0 and surface is not None:
            change = change + surface
        value = change * tile_at(gain_ref, level) + tile_at(down_ref, level) * value
        put_tile(change_ref, level, value)
    following = zeros()
    for level in range(levels - 1, -1, -1):
        following = tile_at(change_ref, level) + tile_at(up_ref, level) * following
        put_tile(change_ref, level, following)
        finish(level, following)


def first_edge_kernel(levels, lon_total, west_in, east_in, east_own, west_own, packed_ref,
                      gain_ref, down_ref, up_ref, parts_ref, *rest):
    others = rest[:lon_total - 3]
    east_ref, west_ref, full_ref, change_ref, force_ref, depth_ref = rest[lon_total - 3:]
    sub = sublane_ids()
    even = sub % 2 == 0
    half = levels // 2
    extra_w = west_in[pl.ds(half * SUB, EXTRA), :]
    extra_e = east_in[pl.ds(half * SUB, EXTRA), :]
    depth_f = jnp.where(even, spread(extra_e[COUNT_ROW:COUNT_ROW + 1]), spread(extra_w[COUNT_ROW:COUNT_ROW + 1]))
    halo_depth = depth_f.astype(jnp.int32)
    depth_ref[...] = halo_depth
    forcing = [zeros()] * FIELDS
    for tile in [parts_ref[0], extra_w, extra_e] + [other[...] for other in others]:
        mine = sub == spread(tile[SLOT_ROW:SLOT_ROW + 1]).astype(jnp.int32)
        for field in range(FIELDS):
            forcing[field] = forcing[field] + jnp.where(mine, spread(tile[field:field + 1]), 0.0)
    surface = zeros()
    rim = jnp.logical_or(sub == 0, sub == SUB - 1)
    for field in range(FIELDS):
        value = SURFACE_GAIN[field] * forcing[field]
        surface = jnp.where(sub == 2 * field, spread(value[SUB - 1:SUB]), surface)
        surface = jnp.where(sub == 2 * field + 1, spread(value[0:1]), surface)
        put_tile(force_ref, field, jnp.where(rim, 0.0, value))
        put_tile(force_ref, FIELDS + field, value)

    def finish(level, change):
        full = tile_at(packed_ref, level) + change
        put_tile(full_ref, level, full)
        if level < half:
            later = tile_at(full_ref, level + half)
            put_tile(east_ref, level, jnp.where(even, full, pltpu.roll(later, 1, 0)))
            put_tile(west_ref, level, jnp.where(even, pltpu.roll(full, SUB - 1, 0), later))

    edge_change(
        levels,
        lambda level: column_tiles(levels, level, east_in, west_in, even),
        lambda level: column_tiles(levels, level, east_own, west_own, even),
        halo_depth, gain_ref, down_ref, up_ref, surface, change_ref, finish,
    )


def merge_kernel(levels, inner_ref, reply_ref, change_ref, force_ref, out_ref, edge_ref):
    sub = sublane_ids()
    pair = ((lane_ids() + 1) % LANE) // 2
    forces = [tile_at(force_ref, field) for field in range(FIELDS)]

    def group_body(group, carry):
        packed = zeros()
        for inner in range(GROUP):
            level = group * GROUP + inner
            reply = tile_at(reply_ref, level)
            change = tile_at(change_ref, level)
            for field in range(FIELDS):
                j = inner * FIELDS + field
                side = pltpu.roll(change, SUB - 1 - 2 * field, 0)
                rim = jnp.logical_or(sub == 0, sub == SUB - 1)
                value = tile_at(inner_ref, field * levels + level) + jnp.where(rim, side, forces[field] * reply)
                put_tile(out_ref, field * levels + level, value)
                packed = jnp.where(pair == j, pltpu.roll(value, 2 * j, 1) if j else value, packed)
        put_tile(edge_ref, group, packed)
        return carry

    lax.fori_loop(0, levels // GROUP, group_body, 0)


def second_edge_kernel(levels, west_in, east_in, full_ref, packed_ref, gain_ref, down_ref, up_ref, depth_ref,
                       inner_ref, result_ref, state_ref, change_ref, sems):
    even = sublane_ids() % 2 == 0
    sub = sublane_ids()
    copies = []

    def finish(level, change):
        edge = tile_at(packed_ref, level) + change
        for field in range(FIELDS):
            side = pltpu.roll(edge, SUB - 1 - 2 * field, 0)
            rim = jnp.logical_or(sub == 0, sub == SUB - 1)
            row = field * levels + level
            put_tile(state_ref, row, jnp.where(rim, side, tile_at(inner_ref, row)))
        if level % GROUP == 0:
            for field in range(FIELDS):
                piece = pl.ds((field * levels + level) * SUB, GROUP * SUB)
                copy = pltpu.make_async_copy(
                    state_ref.at[piece, :], result_ref.at[piece, :], sems.at[level // GROUP, field]
                )
                copy.start()
                copies.append(copy)

    edge_change(
        levels,
        lambda level: column_tiles(levels, level, east_in, west_in, even),
        lambda level: tile_at(full_ref, level),
        depth_ref[...], gain_ref, down_ref, up_ref, None, change_ref, finish,
    )
    for copy in copies:
        copy.wait()


def in_vmem(value):
    return pltpu.with_memory_space_constraint(value, pltpu.VMEM)


def in_hbm(value):
    return pltpu.with_memory_space_constraint(value, pltpu.HBM)


def call(kernel, outs, args, scratch=(), hbm_in=(), hbm_out=(), aliases=None):
    return pl.pallas_call(
        kernel,
        out_shape=[
            (pltpu.HBM if at in hbm_out else pltpu.VMEM)(shape, dtype)
            for at, (shape, dtype) in enumerate(outs)
        ],
        in_specs=[HBM_SPEC if at in hbm_in else VMEM_SPEC for at in range(len(args))],
        out_specs=[HBM_SPEC if at in hbm_out else VMEM_SPEC for at in range(len(outs))],
        scratch_shapes=list(scratch),
        input_output_aliases=aliases or {},
        compiler_params=pltpu.CompilerParams(vmem_limit_bytes=VMEM_BYTES),
    )(*[in_hbm(arg) if at in hbm_in else in_vmem(arg) for at, arg in enumerate(args)])


def ring_shift(value, axis, amount):
    count = lax.axis_size(axis)
    return lax.ppermute(value, axis, [(i, (i + amount) % count) for i in range(count)])


def lat_exchange(edge):
    lon_total = lax.axis_size("lon")
    lat_total = lax.axis_size("lat") * lax.axis_size("comp")
    inside, between = [], []
    for lon in range(lon_total):
        first = lon * lat_total
        for low in range(0, lat_total, 2):
            inside += [(first + low, first + low + 1), (first + low + 1, first + low)]
        for low in range(1, lat_total - 1, 2):
            between += [(first + low, first + low + 1), (first + low + 1, first + low)]
        across = (lon + lon_total // 2) % lon_total * lat_total
        for end in (0, lat_total - 1):
            between.append((first + end, across + end))
    swap_a = lax.ppermute(edge, ("lon",) + LAT_AXES, inside)
    swap_b = lax.ppermute(edge, ("lon",) + LAT_AXES, between)
    return swap_a, swap_b


def bind(kernel, *head):
    def bound(*refs):
        return kernel(*head, *refs)

    bound.__name__ = kernel.__name__
    return bound


def local(ocean_state, level_count, mix_rate, atmos_flux, remap_weight, remap_target, remap_slot):
    field_total, levels, lon_dev, lat_dev = ocean_state.shape
    lon_total = lax.axis_size("lon")
    rows = field_total * levels
    groups = levels // GROUP
    f32, i32 = jnp.float32, jnp.int32
    state_shape = ((rows * lon_dev, lat_dev), f32)
    message = ((rows, lat_dev), f32)
    long_message = ((rows + EXTRA, lat_dev), f32)
    table = ((levels * lon_dev, lat_dev), f32)
    dma = pltpu.SemaphoreType.DMA
    merged = pltpu.VMEM((groups, SUB, LANE), f32)

    east, west, parts, count, rate = call(
        bind(column_kernel, levels, lon_total),
        [long_message, long_message, ((lon_total, SUB, lat_dev), f32), ((lon_dev, lat_dev), i32), table],
        (ocean_state.reshape(rows, lon_dev, lat_dev), level_count, atmos_flux[0], remap_weight[0],
         remap_target, remap_slot, mix_rate.reshape(levels * lon_dev, lat_dev)),
        scratch=[
            pltpu.VMEM((2, rows, lat_dev), f32),
            pltpu.VMEM(atmos_flux.shape[1:], atmos_flux.dtype),
            pltpu.VMEM(remap_weight.shape[1:], remap_weight.dtype),
            pltpu.SMEM(remap_target.shape, i32),
            pltpu.SMEM(remap_slot.shape, i32),
            dma((8,)),
        ],
        hbm_in=range(7),
    )
    x = in_vmem(ocean_state.reshape(rows * lon_dev, lat_dev))
    from_west = ring_shift(east, "lon", 1)
    from_east = ring_shift(west, "lon", -1)
    edge, gain, down, up, reply, edge_gain, edge_down, edge_up = call(
        bind(prepare_kernel, levels),
        [(((groups + 1) * SUB, lat_dev), f32)] + [table] * 7,
        (x, count, rate),
    )
    swap_a, swap_b = lat_exchange(edge)
    others = []
    for s in range(2, lon_total - 1):
        others.append(ring_shift(parts[s], "lon", s))
    (explicit,) = call(bind(explicit_kernel, levels, False), [state_shape], (x, count))
    inner, packed, lat_depth = call(
        bind(solve_kernel, levels, False),
        [state_shape, table, ((SUB, LANE), i32)],
        (x, explicit, gain, down, up, swap_a, swap_b),
        scratch=[merged],
    )
    east_next, west_next, full, change, force, halo_depth = call(
        bind(first_edge_kernel, levels, lon_total),
        [message, message, table, table, ((2 * FIELDS * SUB, LANE), f32), ((SUB, LANE), i32)],
        (from_west, from_east, east, west, packed, edge_gain, edge_down, edge_up, parts, *others),
    )
    from_west = ring_shift(east_next, "lon", 1)
    from_east = ring_shift(west_next, "lon", -1)
    state, edge = call(
        bind(merge_kernel, levels),
        [state_shape, ((groups * SUB, lat_dev), f32)],
        (inner, reply, change, force),
    )
    swap_a, swap_b = lat_exchange(edge)
    (explicit,) = call(bind(explicit_kernel, levels, True), [state_shape], (state, count, force))
    inner, packed = call(
        bind(solve_kernel, levels, True),
        [state_shape, table],
        (state, explicit, gain, down, up, swap_a, swap_b, lat_depth),
        scratch=[merged],
    )
    (result,) = call(
        bind(second_edge_kernel, levels),
        [state_shape],
        (from_west, from_east, full, packed, edge_gain, edge_down, edge_up, halo_depth, inner),
        scratch=[pltpu.VMEM(*state_shape), pltpu.VMEM(*table), dma((groups, FIELDS))],
        hbm_out=(0,),
    )
    return result.reshape(ocean_state.shape)


def solution(mesh):
    placed = (
        P(None, None, "lon", LAT_AXES),
        P("lon", LAT_AXES),
        P(None, "lon", LAT_AXES),
        P(LAT_AXES, "lon", None, None),
        P(LAT_AXES, "lon", None, None),
        P(LAT_AXES, "lon"),
        P(LAT_AXES, "lon"),
    )

    return jax.shard_map(
        local,
        mesh=mesh,
        in_specs=placed,
        out_specs=P(None, None, "lon", LAT_AXES),
        check_vma=False,
    )
```

```python
import jax
import jax.numpy as jnp
from jax import lax
from jax.experimental import pallas as pl
from jax.experimental.pallas import tpu as pltpu
from jax.sharding import PartitionSpec as P


DIFFUSE = 0.2
ADVECTION = 0.5
THERMAL = 0.2
HALINE = 0.15
GRAVITY = 0.05
CORIOLIS = 0.3
SURFACE_GAIN = (0.5, 0.4, 0.6, 0.6)

FIELDS = 4
SUB = 8
LANE = 128
PAIRS = LANE // 2
GROUP = PAIRS // FIELDS
EXTRA = 8
SLOT_ROW = 4
COUNT_ROW = 5
LAT_AXES = ("lat", "comp")
QUARTER = 0.5 * ADVECTION
WARMTH = THERMAL / HALINE
PUSH = 0.5 * GRAVITY * HALINE

VMEM_SPEC = pl.BlockSpec(memory_space=pltpu.VMEM)
HBM_SPEC = pl.BlockSpec(memory_space=pltpu.HBM)
VMEM_BYTES = 16 << 20


def sublane_ids():
    return lax.broadcasted_iota(jnp.int32, (SUB, LANE), 0)


def lane_ids():
    return lax.broadcasted_iota(jnp.int32, (SUB, LANE), 1)


def zeros():
    return jnp.zeros((SUB, LANE), jnp.float32)


def spread(row):
    return jnp.broadcast_to(row, (SUB, LANE))


def tile_at(ref, index):
    return ref[pl.ds(pl.multiple_of(index * SUB, SUB), SUB), :]


def put_tile(ref, index, value):
    ref[pl.ds(pl.multiple_of(index * SUB, SUB), SUB), :] = value


def lat_place():
    return lax.axis_index("lat") * lax.axis_size("comp") + lax.axis_index("comp")


def lat_sides(swap_a, swap_b, index):
    place = lat_place()
    total = lax.axis_size("lat") * lax.axis_size("comp")
    tile_a, tile_b = tile_at(swap_a, index), tile_at(swap_b, index)
    evenly = place % 2 == 0
    north = jnp.where(jnp.logical_and(place < total - 1, evenly), tile_a, 0.0)
    north = jnp.where(jnp.logical_and(place < total - 1, jnp.logical_not(evenly)), tile_b, north)
    south = jnp.where(jnp.logical_and(place > 0, evenly), tile_b, 0.0)
    south = jnp.where(jnp.logical_and(place > 0, jnp.logical_not(evenly)), tile_a, south)
    return south, north


def column_tiles(levels, level, east_ref, west_ref, even):
    half = levels // 2
    if level < half:
        return jnp.where(even, tile_at(east_ref, level), pltpu.roll(tile_at(west_ref, level), 1, 0))
    at = level - half
    return jnp.where(even, pltpu.roll(tile_at(east_ref, at), SUB - 1, 0), tile_at(west_ref, at))


def column_kernel(levels, lon_total, x_ref, count_hbm, flux_hbm, weight_hbm, target_hbm, slot_hbm,
                  rate_hbm, east_ref, west_ref, parts_ref, count_ref, rate_ref,
                  columns, flux_ref, weight_ref, target_ref, slot_ref, sems):
    me = lax.axis_index("lon")
    half = levels // 2
    sub = sublane_ids()
    copies = [
        pltpu.make_async_copy(count_hbm, count_ref, sems.at[2]),
        pltpu.make_async_copy(flux_hbm, flux_ref, sems.at[3]),
        pltpu.make_async_copy(weight_hbm, weight_ref, sems.at[4]),
        pltpu.make_async_copy(target_hbm, target_ref, sems.at[5]),
        pltpu.make_async_copy(slot_hbm, slot_ref, sems.at[6]),
    ]
    sides = [
        pltpu.make_async_copy(x_ref.at[:, SUB - 1, :], columns.at[0], sems.at[0]),
        pltpu.make_async_copy(x_ref.at[:, 0, :], columns.at[1], sems.at[1]),
    ]
    later = pltpu.make_async_copy(rate_hbm, rate_ref, sems.at[7])
    for copy in sides + copies + [later]:
        copy.start()
    for copy in copies:
        copy.wait()

    blocks = flux_ref.shape[0]
    for block in range(blocks):
        partial = jnp.dot(flux_ref[block], weight_ref[block], preferred_element_type=jnp.float32)
        slot = slot_ref[0, block].astype(jnp.float32)
        tile = jnp.concatenate([partial, jnp.full((SUB - FIELDS, LANE), slot, jnp.float32)], axis=0)
        shift = lax.rem(target_ref[0, block] - me + lon_total, lon_total)
        parts_ref[shift] = tile

    count = count_ref[...]
    count_f = count.astype(jnp.float32)
    for side, (out_ref, column, shift) in enumerate(
        ((east_ref, SUB - 1, 1), (west_ref, 0, lon_total - 1))
    ):
        sides[side].wait()
        depth = spread(count[column:column + 1, :])
        for field in range(FIELDS):
            for start in range(0, levels, SUB):
                value = columns[side, pl.ds(field * levels + start, SUB), :]
                value = jnp.where(start + sub < depth, value, 0.0)
                upper = start // half
                row = (start - upper * half) * SUB + 2 * field + upper
                out_ref[pl.ds(row, SUB, stride=SUB), :] = value
        out_ref[pl.ds(half * SUB, EXTRA), :] = jnp.where(
            sub == COUNT_ROW, spread(count_f[column:column + 1, :]), parts_ref[shift]
        )
    later.wait()


def prepare_kernel(levels, x_ref, count_ref, rate_ref, edge_ref, gain_ref, down_ref, up_ref, reply_ref):
    pair = ((lane_ids() + 1) % LANE) // 2
    count = count_ref[...]

    def group_body(group, carry):
        packed = zeros()
        lower, prev, reply = carry
        for inner in range(GROUP):
            level = group * GROUP + inner
            wet = level < count
            for field in range(FIELDS):
                j = inner * FIELDS + field
                value = jnp.where(wet, tile_at(x_ref, field * levels + level), 0.0)
                packed = jnp.where(pair == j, pltpu.roll(value, 2 * j, 1) if j else value, packed)
            upper = jnp.where(level + 1 < count, tile_at(rate_ref, level), 0.0)
            upper = jnp.where(level < levels - 1, upper, 0.0)
            inverse = 1.0 / (1.0 + upper + lower - lower * prev)
            prev = upper * inverse
            gain = jnp.where(wet, inverse, 0.0)
            down = lower * inverse
            reply = jnp.where(level == 0, gain, down * reply)
            put_tile(gain_ref, level, gain)
            put_tile(down_ref, level, down)
            put_tile(up_ref, level, prev)
            put_tile(reply_ref, level, reply)
            lower = upper
        put_tile(edge_ref, group, packed)
        return lower, prev, reply

    lax.fori_loop(0, levels // GROUP, group_body, (zeros(), zeros(), zeros()))
    put_tile(edge_ref, levels // GROUP, count.astype(jnp.float32))


def pack_edges(levels, fields, source_ref, out_ref):
    for side, column in ((0, SUB - 1), (1, 0)):
        for start in range(0, levels, SUB):
            for field in range(FIELDS):
                if field < fields:
                    row = (field * levels + start) * SUB + column
                    value = source_ref[pl.ds(row, SUB, stride=SUB), :]
                out_ref[pl.ds(start * SUB + 2 * field + side, SUB, stride=SUB), :] = value


def finish_tables(levels, gain_ref, down_ref, up_ref, start_ref, reply_ref, edge_gain_ref, edge_down_ref, edge_up_ref):
    def back_body(step, following):
        level = levels - 1 - step
        value = tile_at(start_ref, level) + tile_at(up_ref, level) * following
        put_tile(reply_ref, level, value)
        return value

    lax.fori_loop(0, levels, back_body, zeros(), unroll=16)
    for source_ref, out_ref in ((gain_ref, edge_gain_ref), (down_ref, edge_down_ref), (up_ref, edge_up_ref)):
        pack_edges(levels, 1, source_ref, out_ref)


def explicit_kernel(levels, later, x_ref, count_ref, *rest):
    if later:
        force_ref, out_ref = rest
    else:
        tables, (out_ref, *finished) = rest[:4], rest[4:]
    sub = sublane_ids()
    lane = lane_ids()
    lat_total = LANE * lax.axis_size("lat") * lax.axis_size("comp")
    row_ids = (lat_place() * LANE + lane).astype(jnp.float32)
    rotation = CORIOLIS * (2.0 * (row_ids + 0.5) / lat_total - 1.0)
    depth = count_ref[...]

    def neighbours(value):
        return (
            jnp.where(sub == SUB - 1, 0, pltpu.roll(value, SUB - 1, 0)),
            jnp.where(sub == 0, 0, pltpu.roll(value, 1, 0)),
            jnp.where(lane == LANE - 1, 0, pltpu.roll(value, LANE - 1, 1)),
            jnp.where(lane == 0, 0, pltpu.roll(value, 1, 1)),
        )

    depth_e, depth_w, depth_n, depth_s = neighbours(depth)

    def level_body(level, inner, carry):
        sum_e, sum_w, sum_n, sum_s = carry
        here, east, west, north, south = [], [], [], [], []
        for field in range(FIELDS):
            value = tile_at(x_ref, field * levels + level)
            if not later:
                value = jnp.where(level < depth, value, 0.0)
            here.append(value)
            for into, side in zip((east, west, north, south), neighbours(value)):
                into.append(side)
        wet_e, wet_w, wet_n, wet_s = level < depth_e, level < depth_w, level < depth_n, level < depth_s
        keep = 1.0 - (
            (jnp.where(wet_e, DIFFUSE, 0.0) + jnp.where(wet_w, DIFFUSE, 0.0))
            + (jnp.where(wet_n, DIFFUSE, 0.0) + jnp.where(wet_s, DIFFUSE, 0.0))
        )
        sum_e = sum_e + (east[1] - WARMTH * east[0])
        sum_w = sum_w + (west[1] - WARMTH * west[0])
        sum_n = sum_n + (north[1] - WARMTH * north[0])
        sum_s = sum_s + (south[1] - WARMTH * south[0])
        force_x = PUSH * (jnp.where(wet_e, sum_e, 0.0) - jnp.where(wet_w, sum_w, 0.0))
        force_y = PUSH * (jnp.where(wet_n, sum_n, 0.0) - jnp.where(wet_s, sum_s, 0.0))
        u, v = here[2], here[3]
        u_part = QUARTER * u
        v_part = QUARTER * v
        for field in range(FIELDS):
            around = (east[field] + west[field]) + (north[field] + south[field])
            value = keep * here[field] + DIFFUSE * around
            if field < 2:
                value = value - (
                    u_part * (east[field] - west[field]) + v_part * (north[field] - south[field])
                )
            elif field == 2:
                value = value + (rotation * v - force_x)
            else:
                value = value - (rotation * u + force_y)
            if inner == 0 and later:
                value = value + jnp.where(level == 0, tile_at(force_ref, FIELDS + field), 0.0)
            put_tile(out_ref, field * levels + level, value)
        return sum_e, sum_w, sum_n, sum_s

    def group_body(group, carry):
        for inner in range(GROUP):
            carry = level_body(group * GROUP + inner, inner, carry)
        return carry

    lax.fori_loop(0, levels // GROUP, group_body, (zeros(),) * 4)
    if not later:
        finish_tables(levels, *tables, *finished)


def solve_kernel(levels, later, x_ref, explicit_ref, gain_ref, down_ref, up_ref, swap_a, swap_b, *rest):
    if later:
        depth_ref, out_ref, packed_ref, merged_ref = rest
    else:
        out_ref, packed_ref, depth_ref, merged_ref = rest
    lane = lane_ids()
    even = lane % 2 == 0
    groups = levels // GROUP
    north_lane, south_lane = lane == LANE - 1, lane == 0
    rim = jnp.logical_or(north_lane, south_lane)
    sign = jnp.where(north_lane, -1.0, jnp.where(south_lane, 1.0, 0.0))
    if later:
        halo_depth = depth_ref[...]
    else:
        south, north = lat_sides(swap_a, swap_b, groups)
        halo_depth = jnp.where(
            north_lane, pltpu.roll(north, LANE - 1, 1), jnp.where(south_lane, pltpu.roll(south, 1, 1), 0.0)
        ).astype(jnp.int32)
        depth_ref[...] = halo_depth
    for group in range(groups):
        south, north = lat_sides(swap_a, swap_b, group)
        merged_ref[group] = jnp.where(even, north, pltpu.roll(south, 2, 1))

    def level_body(level, inner, halo, carry):
        total, *prev = carry
        sides = []
        for field in range(FIELDS):
            j = inner * FIELDS + field
            sides.append(jnp.where(rim, pltpu.roll(halo, (LANE - 1 - 2 * j) % LANE, 1), 0.0))
        total = total + (sides[1] - WARMTH * sides[0])
        wet = level < halo_depth
        v_part = (QUARTER * sign) * tile_at(x_ref, 3 * levels + level)
        gain = tile_at(gain_ref, level)
        down = tile_at(down_ref, level)
        done = []
        for field in range(FIELDS):
            row = field * levels + level
            value = tile_at(explicit_ref, row)
            value = value + DIFFUSE * (sides[field] - jnp.where(wet, tile_at(x_ref, row), 0.0))
            if field < 2:
                value = value + v_part * sides[field]
            elif field == 3:
                value = value + (PUSH * sign) * jnp.where(wet, total, 0.0)
            value = value * gain + down * prev[field]
            put_tile(out_ref, row, value)
            done.append(value)
        return (total, *done)

    def forward_group(group, carry):
        halo = merged_ref[group]
        for inner in range(GROUP):
            carry = level_body(group * GROUP + inner, inner, halo, carry)
        return carry

    lax.fori_loop(0, groups, forward_group, (zeros(),) * (1 + FIELDS))

    def backward_group(step, following):
        group = groups - 1 - step
        for inner in range(GROUP - 1, -1, -1):
            level = group * GROUP + inner
            ratio = tile_at(up_ref, level)
            now = []
            for field in range(FIELDS):
                value = tile_at(out_ref, field * levels + level) + ratio * following[field]
                put_tile(out_ref, field * levels + level, value)
                now.append(value)
            following = tuple(now)
        return following

    lax.fori_loop(0, groups, backward_group, (zeros(),) * FIELDS)
    pack_edges(levels, FIELDS, out_ref, packed_ref)


def edge_change(levels, halo_at, own_at, halo_depth, gain_ref, down_ref, up_ref, surface, change_ref, finish):
    sub = sublane_ids()
    even = sub % 2 == 0
    field = sub // 2
    sign = jnp.where(even, 1.0, -1.0)
    carry_by = jnp.where(field < 2, -QUARTER * sign, 0.0)
    push_by = jnp.where(field == 2, -PUSH * sign, 0.0)
    total = zeros()
    value = zeros()
    for level in range(levels):
        halo = halo_at(level)
        own = own_at(level)
        wet = level < halo_depth
        speed = jnp.where(field == 0, pltpu.roll(own, 4, 0), pltpu.roll(own, 6, 0))
        total = total + (pltpu.roll(halo, 2, 0) - WARMTH * pltpu.roll(halo, 4, 0))
        change = DIFFUSE * (halo - jnp.where(wet, own, 0.0)) + (carry_by * speed) * halo
        change = change + push_by * jnp.where(wet, total, 0.0)
        if level == 0 and surface is not None:
            change = change + surface
        value = change * tile_at(gain_ref, level) + tile_at(down_ref, level) * value
        put_tile(change_ref, level, value)
    following = zeros()
    for level in range(levels - 1, -1, -1):
        following = tile_at(change_ref, level) + tile_at(up_ref, level) * following
        put_tile(change_ref, level, following)
        finish(level, following)


def first_edge_kernel(levels, lon_total, west_in, east_in, east_own, west_own, packed_ref,
                      gain_ref, down_ref, up_ref, parts_ref, *rest):
    others = rest[:lon_total - 3]
    east_ref, west_ref, full_ref, change_ref, force_ref, depth_ref = rest[lon_total - 3:]
    sub = sublane_ids()
    even = sub % 2 == 0
    half = levels // 2
    extra_w = west_in[pl.ds(half * SUB, EXTRA), :]
    extra_e = east_in[pl.ds(half * SUB, EXTRA), :]
    depth_f = jnp.where(even, spread(extra_e[COUNT_ROW:COUNT_ROW + 1]), spread(extra_w[COUNT_ROW:COUNT_ROW + 1]))
    halo_depth = depth_f.astype(jnp.int32)
    depth_ref[...] = halo_depth
    forcing = [zeros()] * FIELDS
    for tile in [parts_ref[0], extra_w, extra_e] + [other[...] for other in others]:
        mine = sub == spread(tile[SLOT_ROW:SLOT_ROW + 1]).astype(jnp.int32)
        for field in range(FIELDS):
            forcing[field] = forcing[field] + jnp.where(mine, spread(tile[field:field + 1]), 0.0)
    surface = zeros()
    rim = jnp.logical_or(sub == 0, sub == SUB - 1)
    for field in range(FIELDS):
        value = SURFACE_GAIN[field] * forcing[field]
        surface = jnp.where(sub == 2 * field, spread(value[SUB - 1:SUB]), surface)
        surface = jnp.where(sub == 2 * field + 1, spread(value[0:1]), surface)
        put_tile(force_ref, field, jnp.where(rim, 0.0, value))
        put_tile(force_ref, FIELDS + field, value)

    def finish(level, change):
        full = tile_at(packed_ref, level) + change
        put_tile(full_ref, level, full)
        if level < half:
            later = tile_at(full_ref, level + half)
            put_tile(east_ref, level, jnp.where(even, full, pltpu.roll(later, 1, 0)))
            put_tile(west_ref, level, jnp.where(even, pltpu.roll(full, SUB - 1, 0), later))

    edge_change(
        levels,
        lambda level: column_tiles(levels, level, east_in, west_in, even),
        lambda level: column_tiles(levels, level, east_own, west_own, even),
        halo_depth, gain_ref, down_ref, up_ref, surface, change_ref, finish,
    )


def merge_kernel(levels, inner_ref, reply_ref, change_ref, force_ref, out_ref, edge_ref):
    sub = sublane_ids()
    pair = ((lane_ids() + 1) % LANE) // 2
    forces = [tile_at(force_ref, field) for field in range(FIELDS)]

    def group_body(group, carry):
        packed = zeros()
        for inner in range(GROUP):
            level = group * GROUP + inner
            reply = tile_at(reply_ref, level)
            change = tile_at(change_ref, level)
            for field in range(FIELDS):
                j = inner * FIELDS + field
                side = pltpu.roll(change, SUB - 1 - 2 * field, 0)
                rim = jnp.logical_or(sub == 0, sub == SUB - 1)
                value = tile_at(inner_ref, field * levels + level) + jnp.where(rim, side, forces[field] * reply)
                put_tile(out_ref, field * levels + level, value)
                packed = jnp.where(pair == j, pltpu.roll(value, 2 * j, 1) if j else value, packed)
        put_tile(edge_ref, group, packed)
        return carry

    lax.fori_loop(0, levels // GROUP, group_body, 0)


def second_edge_kernel(levels, west_in, east_in, full_ref, packed_ref, gain_ref, down_ref, up_ref, depth_ref,
                       inner_ref, result_ref, state_ref, change_ref, sems):
    even = sublane_ids() % 2 == 0
    sub = sublane_ids()
    copies = []

    def finish(level, change):
        edge = tile_at(packed_ref, level) + change
        for field in range(FIELDS):
            side = pltpu.roll(edge, SUB - 1 - 2 * field, 0)
            rim = jnp.logical_or(sub == 0, sub == SUB - 1)
            row = field * levels + level
            put_tile(state_ref, row, jnp.where(rim, side, tile_at(inner_ref, row)))
        if level % GROUP == 0:
            for field in range(FIELDS):
                piece = pl.ds((field * levels + level) * SUB, GROUP * SUB)
                copy = pltpu.make_async_copy(
                    state_ref.at[piece, :], result_ref.at[piece, :], sems.at[level // GROUP, field]
                )
                copy.start()
                copies.append(copy)

    edge_change(
        levels,
        lambda level: column_tiles(levels, level, east_in, west_in, even),
        lambda level: tile_at(full_ref, level),
        depth_ref[...], gain_ref, down_ref, up_ref, None, change_ref, finish,
    )
    for copy in copies:
        copy.wait()


def in_vmem(value):
    return pltpu.with_memory_space_constraint(value, pltpu.VMEM)


def in_hbm(value):
    return pltpu.with_memory_space_constraint(value, pltpu.HBM)


def call(kernel, outs, args, scratch=(), hbm_in=(), hbm_out=(), aliases=None):
    return pl.pallas_call(
        kernel,
        out_shape=[
            (pltpu.HBM if at in hbm_out else pltpu.VMEM)(shape, dtype)
            for at, (shape, dtype) in enumerate(outs)
        ],
        in_specs=[HBM_SPEC if at in hbm_in else VMEM_SPEC for at in range(len(args))],
        out_specs=[HBM_SPEC if at in hbm_out else VMEM_SPEC for at in range(len(outs))],
        scratch_shapes=list(scratch),
        input_output_aliases=aliases or {},
        compiler_params=pltpu.CompilerParams(vmem_limit_bytes=VMEM_BYTES),
    )(*[in_hbm(arg) if at in hbm_in else in_vmem(arg) for at, arg in enumerate(args)])


def ring_shift(value, axis, amount):
    count = lax.axis_size(axis)
    return lax.ppermute(value, axis, [(i, (i + amount) % count) for i in range(count)])


def lat_exchange(edge):
    lon_total = lax.axis_size("lon")
    lat_total = lax.axis_size("lat") * lax.axis_size("comp")
    inside, between = [], []
    for lon in range(lon_total):
        first = lon * lat_total
        for low in range(0, lat_total, 2):
            inside += [(first + low, first + low + 1), (first + low + 1, first + low)]
        for low in range(1, lat_total - 1, 2):
            between += [(first + low, first + low + 1), (first + low + 1, first + low)]
        across = (lon + lon_total // 2) % lon_total * lat_total
        for end in (0, lat_total - 1):
            between.append((first + end, across + end))
    swap_a = lax.ppermute(edge, ("lon",) + LAT_AXES, inside)
    swap_b = lax.ppermute(edge, ("lon",) + LAT_AXES, between)
    return swap_a, swap_b


def bind(kernel, *head):
    def bound(*refs):
        return kernel(*head, *refs)

    bound.__name__ = kernel.__name__
    return bound


def local(ocean_state, level_count, mix_rate, atmos_flux, remap_weight, remap_target, remap_slot):
    field_total, levels, lon_dev, lat_dev = ocean_state.shape
    lon_total = lax.axis_size("lon")
    rows = field_total * levels
    groups = levels // GROUP
    f32, i32 = jnp.float32, jnp.int32
    state_shape = ((rows * lon_dev, lat_dev), f32)
    message = ((rows, lat_dev), f32)
    long_message = ((rows + EXTRA, lat_dev), f32)
    table = ((levels * lon_dev, lat_dev), f32)
    dma = pltpu.SemaphoreType.DMA
    merged = pltpu.VMEM((groups, SUB, LANE), f32)

    east, west, parts, count, rate = call(
        bind(column_kernel, levels, lon_total),
        [long_message, long_message, ((lon_total, SUB, lat_dev), f32), ((lon_dev, lat_dev), i32), table],
        (ocean_state.reshape(rows, lon_dev, lat_dev), level_count, atmos_flux[0], remap_weight[0],
         remap_target, remap_slot, mix_rate.reshape(levels * lon_dev, lat_dev)),
        scratch=[
            pltpu.VMEM((2, rows, lat_dev), f32),
            pltpu.VMEM(atmos_flux.shape[1:], atmos_flux.dtype),
            pltpu.VMEM(remap_weight.shape[1:], remap_weight.dtype),
            pltpu.SMEM(remap_target.shape, i32),
            pltpu.SMEM(remap_slot.shape, i32),
            dma((8,)),
        ],
        hbm_in=range(7),
    )
    x = in_vmem(ocean_state.reshape(rows * lon_dev, lat_dev))
    from_west = ring_shift(east, "lon", 1)
    from_east = ring_shift(west, "lon", -1)
    edge, gain, down, up, start = call(
        bind(prepare_kernel, levels),
        [(((groups + 1) * SUB, lat_dev), f32)] + [table] * 4,
        (x, count, rate),
    )
    swap_a, swap_b = lat_exchange(edge)
    others = []
    for s in range(2, lon_total - 1):
        others.append(ring_shift(parts[s], "lon", s))
    explicit, reply, edge_gain, edge_down, edge_up = call(
        bind(explicit_kernel, levels, False), [state_shape] + [table] * 4, (x, count, gain, down, up, start)
    )
    inner, packed, lat_depth = call(
        bind(solve_kernel, levels, False),
        [state_shape, table, ((SUB, LANE), i32)],
        (x, explicit, gain, down, up, swap_a, swap_b),
        scratch=[merged],
    )
    east_next, west_next, full, change, force, halo_depth = call(
        bind(first_edge_kernel, levels, lon_total),
        [message, message, table, table, ((2 * FIELDS * SUB, LANE), f32), ((SUB, LANE), i32)],
        (from_west, from_east, east, west, packed, edge_gain, edge_down, edge_up, parts, *others),
    )
    from_west = ring_shift(east_next, "lon", 1)
    from_east = ring_shift(west_next, "lon", -1)
    state, edge = call(
        bind(merge_kernel, levels),
        [state_shape, ((groups * SUB, lat_dev), f32)],
        (inner, reply, change, force),
    )
    swap_a, swap_b = lat_exchange(edge)
    (explicit,) = call(bind(explicit_kernel, levels, True), [state_shape], (state, count, force))
    inner, packed = call(
        bind(solve_kernel, levels, True),
        [state_shape, table],
        (state, explicit, gain, down, up, swap_a, swap_b, lat_depth),
        scratch=[merged],
    )
    (result,) = call(
        bind(second_edge_kernel, levels),
        [state_shape],
        (from_west, from_east, full, packed, edge_gain, edge_down, edge_up, halo_depth, inner),
        scratch=[pltpu.VMEM(*state_shape), pltpu.VMEM(*table), dma((groups, FIELDS))],
        hbm_out=(0,),
    )
    return result.reshape(ocean_state.shape)


def solution(mesh):
    placed = (
        P(None, None, "lon", LAT_AXES),
        P("lon", LAT_AXES),
        P(None, "lon", LAT_AXES),
        P(LAT_AXES, "lon", None, None),
        P(LAT_AXES, "lon", None, None),
        P(LAT_AXES, "lon"),
        P(LAT_AXES, "lon"),
    )

    return jax.shard_map(
        local,
        mesh=mesh,
        in_specs=placed,
        out_specs=P(None, None, "lon", LAT_AXES),
        check_vma=False,
    )
```

```python
import jax
import jax.numpy as jnp
from jax import lax
from jax.experimental import pallas as pl
from jax.experimental.pallas import tpu as pltpu
from jax.sharding import PartitionSpec as P


DIFFUSE = 0.2
ADVECTION = 0.5
THERMAL = 0.2
HALINE = 0.15
GRAVITY = 0.05
CORIOLIS = 0.3
SURFACE_GAIN = (0.5, 0.4, 0.6, 0.6)

FIELDS = 4
SUB = 8
LANE = 128
PAIRS = LANE // 2
GROUP = PAIRS // FIELDS
EXTRA = 8
SLOT_ROW = 4
COUNT_ROW = 5
LAT_AXES = ("lat", "comp")
QUARTER = 0.5 * ADVECTION
WARMTH = THERMAL / HALINE
PUSH = 0.5 * GRAVITY * HALINE

VMEM_SPEC = pl.BlockSpec(memory_space=pltpu.VMEM)
HBM_SPEC = pl.BlockSpec(memory_space=pltpu.HBM)
VMEM_BYTES = 16 << 20


def sublane_ids():
    return lax.broadcasted_iota(jnp.int32, (SUB, LANE), 0)


def lane_ids():
    return lax.broadcasted_iota(jnp.int32, (SUB, LANE), 1)


def zeros():
    return jnp.zeros((SUB, LANE), jnp.float32)


def spread(row):
    return jnp.broadcast_to(row, (SUB, LANE))


def tile_at(ref, index):
    return ref[pl.ds(pl.multiple_of(index * SUB, SUB), SUB), :]


def put_tile(ref, index, value):
    ref[pl.ds(pl.multiple_of(index * SUB, SUB), SUB), :] = value


def lat_place():
    return lax.axis_index("lat") * lax.axis_size("comp") + lax.axis_index("comp")


def lat_sides(swap_a, swap_b, index):
    place = lat_place()
    total = lax.axis_size("lat") * lax.axis_size("comp")
    tile_a, tile_b = tile_at(swap_a, index), tile_at(swap_b, index)
    evenly = place % 2 == 0
    north = jnp.where(jnp.logical_and(place < total - 1, evenly), tile_a, 0.0)
    north = jnp.where(jnp.logical_and(place < total - 1, jnp.logical_not(evenly)), tile_b, north)
    south = jnp.where(jnp.logical_and(place > 0, evenly), tile_b, 0.0)
    south = jnp.where(jnp.logical_and(place > 0, jnp.logical_not(evenly)), tile_a, south)
    return south, north


def column_tiles(levels, level, east_ref, west_ref, even):
    half = levels // 2
    if level < half:
        return jnp.where(even, tile_at(east_ref, level), pltpu.roll(tile_at(west_ref, level), 1, 0))
    at = level - half
    return jnp.where(even, pltpu.roll(tile_at(east_ref, at), SUB - 1, 0), tile_at(west_ref, at))


def column_kernel(levels, lon_total, x_ref, count_hbm, flux_hbm, weight_hbm, target_hbm, slot_hbm,
                  rate_hbm, east_ref, west_ref, parts_ref, count_ref, rate_ref,
                  columns, flux_ref, weight_ref, target_ref, slot_ref, sems):
    me = lax.axis_index("lon")
    half = levels // 2
    sub = sublane_ids()
    copies = [
        pltpu.make_async_copy(count_hbm, count_ref, sems.at[2]),
        pltpu.make_async_copy(flux_hbm, flux_ref, sems.at[3]),
        pltpu.make_async_copy(weight_hbm, weight_ref, sems.at[4]),
        pltpu.make_async_copy(target_hbm, target_ref, sems.at[5]),
        pltpu.make_async_copy(slot_hbm, slot_ref, sems.at[6]),
    ]
    sides = [
        pltpu.make_async_copy(x_ref.at[:, SUB - 1, :], columns.at[0], sems.at[0]),
        pltpu.make_async_copy(x_ref.at[:, 0, :], columns.at[1], sems.at[1]),
    ]
    later = pltpu.make_async_copy(rate_hbm, rate_ref, sems.at[7])
    for copy in copies[:1] + sides + copies[1:] + [later]:
        copy.start()
    copies[0].wait()
    count = count_ref[...]
    for side, (out_ref, column) in enumerate(((east_ref, SUB - 1), (west_ref, 0))):
        sides[side].wait()
        depth = spread(count[column:column + 1, :])
        for field in range(FIELDS):
            for start in range(0, levels, SUB):
                value = columns[side, pl.ds(field * levels + start, SUB), :]
                value = jnp.where(start + sub < depth, value, 0.0)
                upper = start // half
                row = (start - upper * half) * SUB + 2 * field + upper
                out_ref[pl.ds(row, SUB, stride=SUB), :] = value
    for copy in copies[1:]:
        copy.wait()

    blocks = flux_ref.shape[0]
    for block in range(blocks):
        partial = jnp.dot(flux_ref[block], weight_ref[block], preferred_element_type=jnp.float32)
        slot = slot_ref[0, block].astype(jnp.float32)
        tile = jnp.concatenate([partial, jnp.full((SUB - FIELDS, LANE), slot, jnp.float32)], axis=0)
        shift = lax.rem(target_ref[0, block] - me + lon_total, lon_total)
        parts_ref[shift] = tile

    count_f = count.astype(jnp.float32)
    for out_ref, column, shift in ((east_ref, SUB - 1, 1), (west_ref, 0, lon_total - 1)):
        out_ref[pl.ds(half * SUB, EXTRA), :] = jnp.where(
            sub == COUNT_ROW, spread(count_f[column:column + 1, :]), parts_ref[shift]
        )
    later.wait()


def prepare_kernel(levels, x_ref, count_ref, rate_ref, edge_ref, gain_ref, down_ref, up_ref, reply_ref):
    pair = ((lane_ids() + 1) % LANE) // 2
    count = count_ref[...]

    def group_body(group, carry):
        packed = zeros()
        lower, prev, reply = carry
        for inner in range(GROUP):
            level = group * GROUP + inner
            wet = level < count
            for field in range(FIELDS):
                j = inner * FIELDS + field
                value = jnp.where(wet, tile_at(x_ref, field * levels + level), 0.0)
                packed = jnp.where(pair == j, pltpu.roll(value, 2 * j, 1) if j else value, packed)
            upper = jnp.where(level + 1 < count, tile_at(rate_ref, level), 0.0)
            upper = jnp.where(level < levels - 1, upper, 0.0)
            inverse = 1.0 / (1.0 + upper + lower - lower * prev)
            prev = upper * inverse
            gain = jnp.where(wet, inverse, 0.0)
            down = lower * inverse
            reply = jnp.where(level == 0, gain, down * reply)
            put_tile(gain_ref, level, gain)
            put_tile(down_ref, level, down)
            put_tile(up_ref, level, prev)
            put_tile(reply_ref, level, reply)
            lower = upper
        put_tile(edge_ref, group, packed)
        return lower, prev, reply

    lax.fori_loop(0, levels // GROUP, group_body, (zeros(), zeros(), zeros()))
    put_tile(edge_ref, levels // GROUP, count.astype(jnp.float32))


def pack_edges(levels, fields, source_ref, out_ref):
    for side, column in ((0, SUB - 1), (1, 0)):
        for start in range(0, levels, SUB):
            for field in range(FIELDS):
                if field < fields:
                    row = (field * levels + start) * SUB + column
                    value = source_ref[pl.ds(row, SUB, stride=SUB), :]
                out_ref[pl.ds(start * SUB + 2 * field + side, SUB, stride=SUB), :] = value


def finish_tables(levels, gain_ref, down_ref, up_ref, start_ref, reply_ref, edge_gain_ref, edge_down_ref, edge_up_ref):
    def back_body(step, following):
        level = levels - 1 - step
        value = tile_at(start_ref, level) + tile_at(up_ref, level) * following
        put_tile(reply_ref, level, value)
        return value

    lax.fori_loop(0, levels, back_body, zeros(), unroll=16)
    for source_ref, out_ref in ((gain_ref, edge_gain_ref), (down_ref, edge_down_ref), (up_ref, edge_up_ref)):
        pack_edges(levels, 1, source_ref, out_ref)


def explicit_kernel(levels, later, x_ref, count_ref, *rest):
    if later:
        force_ref, out_ref = rest
    else:
        tables, (out_ref, *finished) = rest[:4], rest[4:]
    sub = sublane_ids()
    lane = lane_ids()
    lat_total = LANE * lax.axis_size("lat") * lax.axis_size("comp")
    row_ids = (lat_place() * LANE + lane).astype(jnp.float32)
    rotation = CORIOLIS * (2.0 * (row_ids + 0.5) / lat_total - 1.0)
    depth = count_ref[...]

    def neighbours(value):
        return (
            jnp.where(sub == SUB - 1, 0, pltpu.roll(value, SUB - 1, 0)),
            jnp.where(sub == 0, 0, pltpu.roll(value, 1, 0)),
            jnp.where(lane == LANE - 1, 0, pltpu.roll(value, LANE - 1, 1)),
            jnp.where(lane == 0, 0, pltpu.roll(value, 1, 1)),
        )

    depth_e, depth_w, depth_n, depth_s = neighbours(depth)

    def level_body(level, inner, carry):
        sum_e, sum_w, sum_n, sum_s = carry
        here, east, west, north, south = [], [], [], [], []
        for field in range(FIELDS):
            value = tile_at(x_ref, field * levels + level)
            if not later:
                value = jnp.where(level < depth, value, 0.0)
            here.append(value)
            for into, side in zip((east, west, north, south), neighbours(value)):
                into.append(side)
        wet_e, wet_w, wet_n, wet_s = level < depth_e, level < depth_w, level < depth_n, level < depth_s
        keep = 1.0 - (
            (jnp.where(wet_e, DIFFUSE, 0.0) + jnp.where(wet_w, DIFFUSE, 0.0))
            + (jnp.where(wet_n, DIFFUSE, 0.0) + jnp.where(wet_s, DIFFUSE, 0.0))
        )
        sum_e = sum_e + (east[1] - WARMTH * east[0])
        sum_w = sum_w + (west[1] - WARMTH * west[0])
        sum_n = sum_n + (north[1] - WARMTH * north[0])
        sum_s = sum_s + (south[1] - WARMTH * south[0])
        force_x = PUSH * (jnp.where(wet_e, sum_e, 0.0) - jnp.where(wet_w, sum_w, 0.0))
        force_y = PUSH * (jnp.where(wet_n, sum_n, 0.0) - jnp.where(wet_s, sum_s, 0.0))
        u, v = here[2], here[3]
        u_part = QUARTER * u
        v_part = QUARTER * v
        for field in range(FIELDS):
            around = (east[field] + west[field]) + (north[field] + south[field])
            value = keep * here[field] + DIFFUSE * around
            if field < 2:
                value = value - (
                    u_part * (east[field] - west[field]) + v_part * (north[field] - south[field])
                )
            elif field == 2:
                value = value + (rotation * v - force_x)
            else:
                value = value - (rotation * u + force_y)
            if inner == 0 and later:
                value = value + jnp.where(level == 0, tile_at(force_ref, FIELDS + field), 0.0)
            put_tile(out_ref, field * levels + level, value)
        return sum_e, sum_w, sum_n, sum_s

    def group_body(group, carry):
        for inner in range(GROUP):
            carry = level_body(group * GROUP + inner, inner, carry)
        return carry

    lax.fori_loop(0, levels // GROUP, group_body, (zeros(),) * 4)
    if not later:
        finish_tables(levels, *tables, *finished)


def solve_kernel(levels, later, x_ref, explicit_ref, gain_ref, down_ref, up_ref, swap_a, swap_b, *rest):
    if later:
        depth_ref, out_ref, packed_ref, merged_ref = rest
    else:
        out_ref, packed_ref, depth_ref, merged_ref = rest
    lane = lane_ids()
    even = lane % 2 == 0
    groups = levels // GROUP
    north_lane, south_lane = lane == LANE - 1, lane == 0
    rim = jnp.logical_or(north_lane, south_lane)
    sign = jnp.where(north_lane, -1.0, jnp.where(south_lane, 1.0, 0.0))
    if later:
        halo_depth = depth_ref[...]
    else:
        south, north = lat_sides(swap_a, swap_b, groups)
        halo_depth = jnp.where(
            north_lane, pltpu.roll(north, LANE - 1, 1), jnp.where(south_lane, pltpu.roll(south, 1, 1), 0.0)
        ).astype(jnp.int32)
        depth_ref[...] = halo_depth
    for group in range(groups):
        south, north = lat_sides(swap_a, swap_b, group)
        merged_ref[group] = jnp.where(even, north, pltpu.roll(south, 2, 1))

    def level_body(level, inner, halo, carry):
        total, *prev = carry
        sides = []
        for field in range(FIELDS):
            j = inner * FIELDS + field
            sides.append(jnp.where(rim, pltpu.roll(halo, (LANE - 1 - 2 * j) % LANE, 1), 0.0))
        total = total + (sides[1] - WARMTH * sides[0])
        wet = level < halo_depth
        v_part = (QUARTER * sign) * tile_at(x_ref, 3 * levels + level)
        gain = tile_at(gain_ref, level)
        down = tile_at(down_ref, level)
        done = []
        for field in range(FIELDS):
            row = field * levels + level
            value = tile_at(explicit_ref, row)
            value = value + DIFFUSE * (sides[field] - jnp.where(wet, tile_at(x_ref, row), 0.0))
            if field < 2:
                value = value + v_part * sides[field]
            elif field == 3:
                value = value + (PUSH * sign) * jnp.where(wet, total, 0.0)
            value = value * gain + down * prev[field]
            put_tile(out_ref, row, value)
            done.append(value)
        return (total, *done)

    def forward_group(group, carry):
        halo = merged_ref[group]
        for inner in range(GROUP):
            carry = level_body(group * GROUP + inner, inner, halo, carry)
        return carry

    lax.fori_loop(0, groups, forward_group, (zeros(),) * (1 + FIELDS))

    def backward_group(step, following):
        group = groups - 1 - step
        for inner in range(GROUP - 1, -1, -1):
            level = group * GROUP + inner
            ratio = tile_at(up_ref, level)
            now = []
            for field in range(FIELDS):
                value = tile_at(out_ref, field * levels + level) + ratio * following[field]
                put_tile(out_ref, field * levels + level, value)
                now.append(value)
            following = tuple(now)
        return following

    lax.fori_loop(0, groups, backward_group, (zeros(),) * FIELDS)
    pack_edges(levels, FIELDS, out_ref, packed_ref)


def edge_change(levels, halo_at, own_at, halo_depth, gain_ref, down_ref, up_ref, surface, change_ref, finish):
    sub = sublane_ids()
    even = sub % 2 == 0
    field = sub // 2
    sign = jnp.where(even, 1.0, -1.0)
    carry_by = jnp.where(field < 2, -QUARTER * sign, 0.0)
    push_by = jnp.where(field == 2, -PUSH * sign, 0.0)
    total = zeros()
    value = zeros()
    for level in range(levels):
        halo = halo_at(level)
        own = own_at(level)
        wet = level < halo_depth
        speed = jnp.where(field == 0, pltpu.roll(own, 4, 0), pltpu.roll(own, 6, 0))
        total = total + (pltpu.roll(halo, 2, 0) - WARMTH * pltpu.roll(halo, 4, 0))
        change = DIFFUSE * (halo - jnp.where(wet, own, 0.0)) + (carry_by * speed) * halo
        change = change + push_by * jnp.where(wet, total, 0.0)
        if level == 0 and surface is not None:
            change = change + surface
        value = change * tile_at(gain_ref, level) + tile_at(down_ref, level) * value
        put_tile(change_ref, level, value)
    following = zeros()
    for level in range(levels - 1, -1, -1):
        following = tile_at(change_ref, level) + tile_at(up_ref, level) * following
        put_tile(change_ref, level, following)
        finish(level, following)


def first_edge_kernel(levels, lon_total, west_in, east_in, east_own, west_own, packed_ref,
                      gain_ref, down_ref, up_ref, parts_ref, *rest):
    others = rest[:lon_total - 3]
    east_ref, west_ref, full_ref, change_ref, force_ref, depth_ref = rest[lon_total - 3:]
    sub = sublane_ids()
    even = sub % 2 == 0
    half = levels // 2
    extra_w = west_in[pl.ds(half * SUB, EXTRA), :]
    extra_e = east_in[pl.ds(half * SUB, EXTRA), :]
    depth_f = jnp.where(even, spread(extra_e[COUNT_ROW:COUNT_ROW + 1]), spread(extra_w[COUNT_ROW:COUNT_ROW + 1]))
    halo_depth = depth_f.astype(jnp.int32)
    depth_ref[...] = halo_depth
    forcing = [zeros()] * FIELDS
    for tile in [parts_ref[0], extra_w, extra_e] + [other[...] for other in others]:
        mine = sub == spread(tile[SLOT_ROW:SLOT_ROW + 1]).astype(jnp.int32)
        for field in range(FIELDS):
            forcing[field] = forcing[field] + jnp.where(mine, spread(tile[field:field + 1]), 0.0)
    surface = zeros()
    rim = jnp.logical_or(sub == 0, sub == SUB - 1)
    for field in range(FIELDS):
        value = SURFACE_GAIN[field] * forcing[field]
        surface = jnp.where(sub == 2 * field, spread(value[SUB - 1:SUB]), surface)
        surface = jnp.where(sub == 2 * field + 1, spread(value[0:1]), surface)
        put_tile(force_ref, field, jnp.where(rim, 0.0, value))
        put_tile(force_ref, FIELDS + field, value)

    def finish(level, change):
        full = tile_at(packed_ref, level) + change
        put_tile(full_ref, level, full)
        if level < half:
            later = tile_at(full_ref, level + half)
            put_tile(east_ref, level, jnp.where(even, full, pltpu.roll(later, 1, 0)))
            put_tile(west_ref, level, jnp.where(even, pltpu.roll(full, SUB - 1, 0), later))

    edge_change(
        levels,
        lambda level: column_tiles(levels, level, east_in, west_in, even),
        lambda level: column_tiles(levels, level, east_own, west_own, even),
        halo_depth, gain_ref, down_ref, up_ref, surface, change_ref, finish,
    )


def merge_kernel(levels, inner_ref, reply_ref, change_ref, force_ref, out_ref, edge_ref):
    sub = sublane_ids()
    pair = ((lane_ids() + 1) % LANE) // 2
    forces = [tile_at(force_ref, field) for field in range(FIELDS)]

    def group_body(group, carry):
        packed = zeros()
        for inner in range(GROUP):
            level = group * GROUP + inner
            reply = tile_at(reply_ref, level)
            change = tile_at(change_ref, level)
            for field in range(FIELDS):
                j = inner * FIELDS + field
                side = pltpu.roll(change, SUB - 1 - 2 * field, 0)
                rim = jnp.logical_or(sub == 0, sub == SUB - 1)
                value = tile_at(inner_ref, field * levels + level) + jnp.where(rim, side, forces[field] * reply)
                put_tile(out_ref, field * levels + level, value)
                packed = jnp.where(pair == j, pltpu.roll(value, 2 * j, 1) if j else value, packed)
        put_tile(edge_ref, group, packed)
        return carry

    lax.fori_loop(0, levels // GROUP, group_body, 0)


def second_edge_kernel(levels, west_in, east_in, full_ref, packed_ref, gain_ref, down_ref, up_ref, depth_ref,
                       inner_ref, result_ref, state_ref, change_ref, sems):
    even = sublane_ids() % 2 == 0
    sub = sublane_ids()
    copies = []

    def finish(level, change):
        edge = tile_at(packed_ref, level) + change
        for field in range(FIELDS):
            side = pltpu.roll(edge, SUB - 1 - 2 * field, 0)
            rim = jnp.logical_or(sub == 0, sub == SUB - 1)
            row = field * levels + level
            put_tile(state_ref, row, jnp.where(rim, side, tile_at(inner_ref, row)))
        if level % GROUP == 0:
            for field in range(FIELDS):
                piece = pl.ds((field * levels + level) * SUB, GROUP * SUB)
                copy = pltpu.make_async_copy(
                    state_ref.at[piece, :], result_ref.at[piece, :], sems.at[level // GROUP, field]
                )
                copy.start()
                copies.append(copy)

    edge_change(
        levels,
        lambda level: column_tiles(levels, level, east_in, west_in, even),
        lambda level: tile_at(full_ref, level),
        depth_ref[...], gain_ref, down_ref, up_ref, None, change_ref, finish,
    )
    for copy in copies:
        copy.wait()


def in_vmem(value):
    return pltpu.with_memory_space_constraint(value, pltpu.VMEM)


def in_hbm(value):
    return pltpu.with_memory_space_constraint(value, pltpu.HBM)


def call(kernel, outs, args, scratch=(), hbm_in=(), hbm_out=(), aliases=None):
    return pl.pallas_call(
        kernel,
        out_shape=[
            (pltpu.HBM if at in hbm_out else pltpu.VMEM)(shape, dtype)
            for at, (shape, dtype) in enumerate(outs)
        ],
        in_specs=[HBM_SPEC if at in hbm_in else VMEM_SPEC for at in range(len(args))],
        out_specs=[HBM_SPEC if at in hbm_out else VMEM_SPEC for at in range(len(outs))],
        scratch_shapes=list(scratch),
        input_output_aliases=aliases or {},
        compiler_params=pltpu.CompilerParams(vmem_limit_bytes=VMEM_BYTES),
    )(*[in_hbm(arg) if at in hbm_in else in_vmem(arg) for at, arg in enumerate(args)])


def ring_shift(value, axis, amount):
    count = lax.axis_size(axis)
    return lax.ppermute(value, axis, [(i, (i + amount) % count) for i in range(count)])


def lat_exchange(edge):
    lon_total = lax.axis_size("lon")
    lat_total = lax.axis_size("lat") * lax.axis_size("comp")
    inside, between = [], []
    for lon in range(lon_total):
        first = lon * lat_total
        for low in range(0, lat_total, 2):
            inside += [(first + low, first + low + 1), (first + low + 1, first + low)]
        for low in range(1, lat_total - 1, 2):
            between += [(first + low, first + low + 1), (first + low + 1, first + low)]
        across = (lon + lon_total // 2) % lon_total * lat_total
        for end in (0, lat_total - 1):
            between.append((first + end, across + end))
    swap_a = lax.ppermute(edge, ("lon",) + LAT_AXES, inside)
    swap_b = lax.ppermute(edge, ("lon",) + LAT_AXES, between)
    return swap_a, swap_b


def bind(kernel, *head):
    def bound(*refs):
        return kernel(*head, *refs)

    bound.__name__ = kernel.__name__
    return bound


def local(ocean_state, level_count, mix_rate, atmos_flux, remap_weight, remap_target, remap_slot):
    field_total, levels, lon_dev, lat_dev = ocean_state.shape
    lon_total = lax.axis_size("lon")
    rows = field_total * levels
    groups = levels // GROUP
    f32, i32 = jnp.float32, jnp.int32
    state_shape = ((rows * lon_dev, lat_dev), f32)
    message = ((rows, lat_dev), f32)
    long_message = ((rows + EXTRA, lat_dev), f32)
    table = ((levels * lon_dev, lat_dev), f32)
    dma = pltpu.SemaphoreType.DMA
    merged = pltpu.VMEM((groups, SUB, LANE), f32)

    east, west, parts, count, rate = call(
        bind(column_kernel, levels, lon_total),
        [long_message, long_message, ((lon_total, SUB, lat_dev), f32), ((lon_dev, lat_dev), i32), table],
        (ocean_state.reshape(rows, lon_dev, lat_dev), level_count, atmos_flux[0], remap_weight[0],
         remap_target, remap_slot, mix_rate.reshape(levels * lon_dev, lat_dev)),
        scratch=[
            pltpu.VMEM((2, rows, lat_dev), f32),
            pltpu.VMEM(atmos_flux.shape[1:], atmos_flux.dtype),
            pltpu.VMEM(remap_weight.shape[1:], remap_weight.dtype),
            pltpu.SMEM(remap_target.shape, i32),
            pltpu.SMEM(remap_slot.shape, i32),
            dma((8,)),
        ],
        hbm_in=range(7),
    )
    x = in_vmem(ocean_state.reshape(rows * lon_dev, lat_dev))
    from_west = ring_shift(east, "lon", 1)
    from_east = ring_shift(west, "lon", -1)
    edge, gain, down, up, start = call(
        bind(prepare_kernel, levels),
        [(((groups + 1) * SUB, lat_dev), f32)] + [table] * 4,
        (x, count, rate),
    )
    swap_a, swap_b = lat_exchange(edge)
    others = []
    for s in range(2, lon_total - 1):
        others.append(ring_shift(parts[s], "lon", s))
    explicit, reply, edge_gain, edge_down, edge_up = call(
        bind(explicit_kernel, levels, False), [state_shape] + [table] * 4, (x, count, gain, down, up, start)
    )
    inner, packed, lat_depth = call(
        bind(solve_kernel, levels, False),
        [state_shape, table, ((SUB, LANE), i32)],
        (x, explicit, gain, down, up, swap_a, swap_b),
        scratch=[merged],
    )
    east_next, west_next, full, change, force, halo_depth = call(
        bind(first_edge_kernel, levels, lon_total),
        [message, message, table, table, ((2 * FIELDS * SUB, LANE), f32), ((SUB, LANE), i32)],
        (from_west, from_east, east, west, packed, edge_gain, edge_down, edge_up, parts, *others),
    )
    from_west = ring_shift(east_next, "lon", 1)
    from_east = ring_shift(west_next, "lon", -1)
    state, edge = call(
        bind(merge_kernel, levels),
        [state_shape, ((groups * SUB, lat_dev), f32)],
        (inner, reply, change, force),
    )
    swap_a, swap_b = lat_exchange(edge)
    (explicit,) = call(bind(explicit_kernel, levels, True), [state_shape], (state, count, force))
    inner, packed = call(
        bind(solve_kernel, levels, True),
        [state_shape, table],
        (state, explicit, gain, down, up, swap_a, swap_b, lat_depth),
        scratch=[merged],
    )
    (result,) = call(
        bind(second_edge_kernel, levels),
        [state_shape],
        (from_west, from_east, full, packed, edge_gain, edge_down, edge_up, halo_depth, inner),
        scratch=[pltpu.VMEM(*state_shape), pltpu.VMEM(*table), dma((groups, FIELDS))],
        hbm_out=(0,),
    )
    return result.reshape(ocean_state.shape)


def solution(mesh):
    placed = (
        P(None, None, "lon", LAT_AXES),
        P("lon", LAT_AXES),
        P(None, "lon", LAT_AXES),
        P(LAT_AXES, "lon", None, None),
        P(LAT_AXES, "lon", None, None),
        P(LAT_AXES, "lon"),
        P(LAT_AXES, "lon"),
    )

    return jax.shard_map(
        local,
        mesh=mesh,
        in_specs=placed,
        out_specs=P(None, None, "lon", LAT_AXES),
        check_vma=False,
    )
```
